256 devices in a mesh: lat: 8 (over y, core), lon: 4 (over z_lo), ens: 8 (over x, z_hi).
Axes of the slice: x: 4, y: 4, z: 8 (z_hi: 2, z_lo: 4; z = z_hi * 4 + z_lo), core: 2. Of those that a mesh axis runs over, the one named last changes fastest.
Arguments:
- fields: bfloat16 [8, 96, 64, 640], P('ens', 'lat', 'lon'), may hold values from -6 to 6
- filter_basis: bfloat16 [96, 5, 4, 16], P(('lat', 'lon')), may hold values from -0.625 to 0.625
- lon_offsets: int32 [96, 5, 16], P(('lat', 'lon')), may hold values from -32 to 31, as said below
- conv_weight: bfloat16 [2560, 640], replicated, may hold values from -0.125 to 0.125
- weight_in: bfloat16 [640, 1280], replicated, may hold values from -0.25 to 0.25
- weight_out: bfloat16 [1280, 640], replicated, may hold values from -0.15625 to 0.15625
- cotangent: bfloat16 [8, 96, 64, 640], P('ens', 'lat', 'lon'), may hold values from -6 to 6
Outputs:
- block_out: bfloat16 [8, 96, 64, 640], P('ens', 'lat', 'lon')
- field_grad: bfloat16 [8, 96, 64, 640], P('ens', 'lat', 'lon')
- conv_weight_grad: float32 [2560, 640], P(('lat', 'lon', 'ens'))
- weight_in_grad: float32 [640, 1280], P(None, ('lat', 'lon', 'ens'))
- weight_out_grad: float32 [1280, 640], P(('lat', 'lon', 'ens'))
The draws below stay inside these ranges and needn't reach their ends.
Inputs may be any that keep to these rules, and one draw needn't show every extreme that they name: `lon_offsets`: within one cycle and one cycle offset the 16 longitude offsets are distinct. In the 2 cycles nearest each pole they lie in -32 to 31; in every other cycle they lie in -16 to 15.
All inputs are finite; a program needn't handle non-finite values.
Results may differ from the reference program's by a relative error of at most 0.015.
Values may be sent and summed in bfloat16 or wider, within the bound.
No kernel may reach another device: no remote copies, remote signals or barrier semaphores. Data moves between devices by JAX's collectives and lax.ppermute only.
A program may use at most 128 MiB of HBM per device.

```python
import math
import jax
import jax.numpy as jnp
from jax import lax

EMBED = 640
HIDDEN_SIZE = 1280
BASIS = 4
TAPS = 16
REACH_ROWS = 2
ROW_SPAN = 5
REACH_LON = 16
POLAR_CYCLES = 2
NLON = 64
NLAT = 96
MEMBERS = 8


def draw_lon_offsets(key, part):
    total_rows = NLAT * ROW_SPAN
    positions = jnp.arange(NLON, dtype=jnp.int32)
    scores = jax.random.randint(key, (total_rows, NLON), 0, 4096, dtype=jnp.int32) * NLON + positions[None, :]
    cycles = jnp.arange(total_rows, dtype=jnp.int32) // ROW_SPAN
    polar = (cycles < POLAR_CYCLES) | (cycles >= NLAT - POLAR_CYCLES)
    limits = jnp.where(polar, NLON, 2 * REACH_LON).astype(jnp.int32)
    scores = jnp.where(positions[None, :] < limits[:, None], scores, scores + 2 * 4096 * NLON)
    at_ends = (positions[None, :] == 0) | (positions[None, :] == NLON - 1)
    scores = jnp.where(polar[:, None] & at_ends, positions[None, :] - NLON, scores)
    ranked = jnp.argsort(scores, axis=1, stable=True).astype(jnp.int32)
    chosen = ranked[:, :TAPS] - (limits // 2)[:, None]
    return chosen.reshape(NLAT, ROW_SPAN, TAPS).astype(jnp.int32)


def levels(rng, extent, cuts, low, high):
    loudness = 1.0
    for position, shards_of in cuts:
        steps = jax.random.uniform(jax.random.fold_in(jax.random.fold_in(rng, 6), position), (shards_of,), jnp.float32, low / len(cuts), high / len(cuts))
        loudness = loudness * jnp.repeat(jnp.exp(steps), extent[position] // shards_of).reshape((-1,) + (1,) * (len(extent) - 1 - position))
    return loudness


def normal_values(own_key, dims, deviation, bound, shards=(), kind=jnp.bfloat16):
    level = levels(own_key, dims, shards, -0.22, 0.18) if shards else 1.0
    entries = jax.random.normal(own_key, dims, jnp.float32) * deviation * level
    return jnp.minimum(jnp.maximum(entries, -bound), bound).astype(kind)


def setup_inputs(seed: int = 0) -> dict:
    key_of = jax.random.split(jax.random.key(seed), 8)
    fields = normal_values(key_of[0], (MEMBERS, NLAT, NLON, EMBED), 1.0, 6.0, ((0, 8), (1, 8), (2, 4)))
    filter_basis = normal_values(key_of[1], (NLAT, ROW_SPAN, BASIS, TAPS), (ROW_SPAN * TAPS) ** -0.5, 0.625, ((0, 32),))
    lon_offsets = draw_lon_offsets(jax.random.fold_in(key_of[7], 71), 0)
    conv_weight = normal_values(key_of[3], (BASIS * EMBED, EMBED), (BASIS * EMBED) ** -0.5, 0.125)
    weight_in = normal_values(key_of[4], (EMBED, HIDDEN_SIZE), EMBED ** -0.5, 0.25)
    weight_out = normal_values(key_of[5], (HIDDEN_SIZE, EMBED), HIDDEN_SIZE ** -0.5, 0.15625)
    cotangent = normal_values(key_of[6], (MEMBERS, NLAT, NLON, EMBED), 1.0, 6.0, ((0, 8), (1, 8), (2, 4)))
    return dict(fields=fields, filter_basis=filter_basis, lon_offsets=lon_offsets, conv_weight=conv_weight, weight_in=weight_in, weight_out=weight_out, cotangent=cotangent)


half_root = 0.7071067811865476
gauss_norm = 0.3989422804014327

def feed_forward(blend_rows, tangent_rows, weight_in, weight_out):
    preact = jnp.dot(blend_rows, weight_in, preferred_element_type=jnp.float32)
    normal_cdf = 0.5 * (1.0 + jax.scipy.special.erf(preact * half_root))
    hidden_act = (preact * normal_cdf).astype(jnp.bfloat16)
    output_rows = (blend_rows.astype(jnp.float32) + jnp.dot(hidden_act, weight_out, preferred_element_type=jnp.float32)).astype(jnp.bfloat16)
    hidden_grad = lax.dot_general(tangent_rows, weight_out, (((1,), (1,)), ((), ())), preferred_element_type=jnp.float32)
    slope = normal_cdf + preact * jnp.exp(-0.5 * preact * preact) * gauss_norm
    preact_grad = (hidden_grad * slope).astype(jnp.bfloat16)
    blend_grad = (tangent_rows.astype(jnp.float32) + lax.dot_general(preact_grad, weight_in, (((1,), (1,)), ((), ())), preferred_element_type=jnp.float32)).astype(jnp.bfloat16)
    grad_in = lax.dot_general(blend_rows, preact_grad, (((0,), (0,)), ((), ())), preferred_element_type=jnp.float32)
    grad_out = lax.dot_general(hidden_act, tangent_rows, (((0,), (0,)), ((), ())), preferred_element_type=jnp.float32)
    return (output_rows, blend_grad, grad_in, grad_out)

def convolve(member_field, basis_float, lon_offsets):
    padded = jnp.pad(member_field, ((REACH_ROWS, REACH_ROWS), (0, 0), (0, 0)))
    columns = jnp.arange(NLON, dtype=jnp.int32)
    result = jnp.zeros((NLAT, NLON, BASIS, EMBED), member_field.dtype)
    for offset_row in range(ROW_SPAN):
        source = padded[offset_row:offset_row + NLAT]
        for tap_index in range(TAPS):
            lon_index = (columns[None, :] + lon_offsets[:, offset_row, tap_index][:, None]) % NLON
            shifted = jnp.take_along_axis(source, lon_index[:, :, None], axis=1)
            weights = basis_float[:, offset_row, :, tap_index]
            result = result + weights[:, None, :, None] * shifted[:, :, None, :]
    return result.reshape(NLAT, NLON, BASIS * EMBED)

def reference(fields, filter_basis, lon_offsets, conv_weight, weight_in, weight_out, cotangent):
    basis_float = filter_basis.astype(jnp.float32)

    def member(sums, inputs):
        member_field, tangent = inputs

        def local_conv(values):
            return convolve(values, basis_float, lon_offsets)
        spread_full, pullback = jax.vjp(local_conv, member_field.astype(jnp.float32))
        spread = spread_full.astype(jnp.bfloat16).reshape(NLAT * NLON, BASIS * EMBED)
        field_rows = member_field.reshape(NLAT * NLON, EMBED)
        blended = (field_rows.astype(jnp.float32) + jnp.dot(spread, conv_weight, preferred_element_type=jnp.float32)).astype(jnp.bfloat16)
        tangent_rows = tangent.reshape(NLAT * NLON, EMBED)
        output_rows, blend_grad, grad_in, grad_out = feed_forward(blended, tangent_rows, weight_in, weight_out)
        spread_grad = lax.dot_general(blend_grad, conv_weight, (((1,), (1,)), ((), ())), preferred_element_type=jnp.float32).astype(jnp.bfloat16)
        adjoint, = pullback(spread_grad.astype(jnp.float32).reshape(NLAT, NLON, BASIS * EMBED))
        member_grad = (blend_grad.astype(jnp.float32).reshape(NLAT, NLON, EMBED) + adjoint).astype(jnp.bfloat16)
        grad_conv = lax.dot_general(spread, blend_grad, (((0,), (0,)), ((), ())), preferred_element_type=jnp.float32)
        new_sums = (sums[0] + grad_conv, sums[1] + grad_in, sums[2] + grad_out)
        return (new_sums, (output_rows.reshape(NLAT, NLON, EMBED), member_grad))
    start_sums = (jnp.zeros((BASIS * EMBED, EMBED), jnp.float32), jnp.zeros((EMBED, HIDDEN_SIZE), jnp.float32), jnp.zeros((HIDDEN_SIZE, EMBED), jnp.float32))
    sums, (block_out, field_grad) = lax.scan(member, start_sums, (fields, cotangent))
    factor = 1.0 / math.sqrt(MEMBERS * NLAT * NLON)
    return (block_out, field_grad, sums[0] * factor, sums[1] * factor, sums[2] * factor)
```

```python
import math

import jax
import jax.numpy as jnp
from jax import lax
from jax.experimental import pallas as pl
from jax.experimental.pallas import tpu as pltpu
from jax.sharding import Mesh, PartitionSpec as P

EMBED = 640
HIDDEN = 1280
BASIS = 4
SPAN = 5
NLON = 64
NLAT = 96
MEMBERS = 8
WIDE = BASIS * EMBED

CYCLES = 12
LON = 16
CELLS = CYCLES * LON
OWNED = 3
HALO = 2

half_root = 0.7071067811865476
gauss_norm = 0.3989422804014327


VMEM = pltpu.CompilerParams(vmem_limit_bytes=56 * 1024 * 1024)
LAT = ("y", "core")
bf16 = jnp.bfloat16
f32 = jnp.float32


def dot(a, b, dims):
    return lax.dot_general(a, b, (dims, ((), ())), preferred_element_type=f32)


def shift(block, axis, count, step):
    return lax.ppermute(block, axis, [(i, (i + step) % count) for i in range(count)])


def struct(shape, dtype):
    return jax.ShapeDtypeStruct(shape, dtype)


def fill_window(win, tile, left, right, top, bottom, left_halo, right_halo, far, lat):
    far_zero = jnp.zeros((LON, EMBED), bf16)
    for group, (inner, halo) in enumerate(
        ((left, left_halo), (tile, None), (right, right_halo))
    ):
        for row in range(CYCLES):
            at = (row + HALO) * NLON + group * LON
            win[at : at + LON, :] = inner[row * LON : (row + 1) * LON, :]
        for row in range(HALO):
            upper = top if halo is None else halo
            lower = bottom if halo is None else halo
            shift_rows = 0 if halo is None else HALO * LON
            at = row * NLON + group * LON
            win[at : at + LON, :] = upper[row * LON : (row + 1) * LON, :]
            at = (row + HALO + CYCLES) * NLON + group * LON
            win[at : at + LON, :] = lower[
                shift_rows + row * LON : shift_rows + (row + 1) * LON, :
            ]
    for row in range(CYCLES + 2 * HALO):
        at = row * NLON + 3 * LON
        win[at : at + LON, :] = far_zero

    @pl.when(lat == 0)
    def _():
        for row in range(4):
            at = (row + HALO) * NLON + 3 * LON
            win[at : at + LON, :] = far[row * LON : (row + 1) * LON, :]

    @pl.when(lat == 7)
    def _():
        for row in range(4):
            at = (row + HALO + CYCLES - 4) * NLON + 3 * LON
            win[at : at + LON, :] = far[row * LON : (row + 1) * LON, :]


def set_rows(coef, at, rows):
    for d in range(SPAN):
        coef[d, at : at + rows.shape[0], :] = rows[:, d * 128 : (d + 1) * 128]


def band_rows(win, band, coef, cycle, row_of):
    low_half = lax.broadcasted_iota(jnp.int32, (LON, 2 * NLON), 1) < NLON
    for k in range(BASIS):
        rolled = []
        for d in range(SPAN):
            row, lane = row_of(d, k)
            values = coef[lane, pl.ds(row, 1), :]
            spread_row = jnp.broadcast_to(values, (LON, 2 * NLON))
            rolled.append(pltpu.roll(spread_row, LON, 1, stride=1, stride_axis=0))
        at = k * LON
        band[at : at + LON, 0:128] = jnp.where(low_half, rolled[0], rolled[1]).astype(bf16)
        band[at : at + LON, 128:256] = jnp.where(low_half, rolled[2], rolled[3]).astype(bf16)
        band[at : at + LON, 256:384] = rolled[4].astype(bf16)
    window = win[cycle * NLON : cycle * NLON + SPAN * NLON, :]
    return dot(band[:, 0 : SPAN * NLON], window, ((1,), (0,)))


def spread_kernel(
    place, tile, left, right, top, bottom, left_halo, right_halo, far,
    own_e, left_e, right_e, far_e, spread, edge, win, band, coef
):
    lat = place[0]
    lon = place[1]
    fill_window(win, tile, left, right, top, bottom, left_halo, right_halo, far, lat)
    for group, e in enumerate((left_e, own_e, right_e, far_e)):
        set_rows(coef, group * 32, e[...].astype(f32))

    def base(cycle):
        return lax.rem(cycle // OWNED - lon + 1 + 4, 4) * 32 + (cycle % OWNED) * BASIS

    for i in range(CYCLES):
        start = base(i)
        rows = band_rows(win, band.at[i % 2], coef, i, lambda d, k: (start + k, d))
        for k in range(BASIS):
            spread[i * LON : (i + 1) * LON, k * EMBED : (k + 1) * EMBED] = rows[
                k * LON : (k + 1) * LON, :
            ].astype(bf16)
    pieces = []
    for cycle in (0, 1, CYCLES - 2, CYCLES - 1):
        start = base(cycle) + 16
        for k in range(BASIS):
            pieces.append(
                jnp.concatenate([coef[d, pl.ds(start + k, 1), :] for d in range(SPAN)], axis=1)
            )
    edge[...] = jnp.concatenate(pieces, axis=0).astype(bf16)


def mlp_kernel(
    place, tile, tangent, spread, conv_weight, weight_in, weight_out, out, blend_grad, mine, theirs
):
    core = place[2]
    blended = (
        tile[...].astype(f32) + dot(spread[...], conv_weight[...], ((1,), (0,)))
    ).astype(bf16)
    preact = dot(blended, weight_in[...], ((1,), (0,)))
    cdf = 0.5 * (1.0 + lax.erf(preact * half_root))
    hidden = (preact * cdf).astype(bf16)
    out[...] = (
        blended.astype(f32) + dot(hidden, weight_out[...], ((1,), (0,)))
    ).astype(bf16)
    slope = cdf + preact * jnp.exp(-0.5 * preact * preact) * gauss_norm
    hidden_grad = dot(tangent[...], weight_out[...], ((1,), (1,)))
    preact_grad = (hidden_grad * slope).astype(bf16)
    grad = (
        tangent[...].astype(f32) + dot(preact_grad, weight_in[...], ((1,), (1,)))
    ).astype(bf16)
    blend_grad[...] = grad
    theirs[:, 0:EMBED] = blended
    theirs[:, EMBED : 2 * EMBED] = grad
    mine[:, 0:EMBED] = blended
    mine[:, EMBED : 2 * EMBED] = grad
    for c in range(2):
        half = slice(c * EMBED, (c + 1) * EMBED)

        @pl.when(core == c)
        def _():
            mine[:, 2 * EMBED : 3 * EMBED] = hidden[:, half]
            mine[:, 3 * EMBED : 4 * EMBED] = preact_grad[:, half]

        @pl.when(core != c)
        def _():
            theirs[:, 2 * EMBED : 3 * EMBED] = hidden[:, half]
            theirs[:, 3 * EMBED : 4 * EMBED] = preact_grad[:, half]


def mlp_grad_kernel(place, mine, other, tangent, other_tangent, o0, o1, o2, o3, acc):
    x = place[3]
    acc[0:EMBED, :] = dot(
        mine[:, 3 * EMBED : 4 * EMBED], mine[:, 0:EMBED], ((0,), (0,))
    ) + dot(other[:, 3 * EMBED : 4 * EMBED], other[:, 0:EMBED], ((0,), (0,)))
    acc[EMBED : 2 * EMBED, :] = dot(
        mine[:, 2 * EMBED : 3 * EMBED], tangent[...], ((0,), (0,))
    ) + dot(other[:, 2 * EMBED : 3 * EMBED], other_tangent[...], ((0,), (0,)))
    for s, o in enumerate((o0, o1, o2, o3)):
        at = pl.multiple_of(lax.rem(x + s, 4) * 160, 160)
        o[0:160, :] = acc[pl.ds(at, 160), :].astype(o.dtype)
        o[160:320, :] = acc[pl.ds(at + EMBED, 160), :].astype(o.dtype)


def conv_grad_kernel(place, spread, other_spread, mine, other, o0, o1, o2, o3, acc):
    y = place[4]
    core = place[2]
    half = pl.multiple_of(core * 320, 320)
    for s, o in enumerate((o0, o1, o2, o3)):
        lanes = pl.ds(pl.multiple_of(lax.rem(y + s, 4) * EMBED, EMBED), EMBED)
        acc[...] = dot(
            spread[:, lanes], mine[:, EMBED : 2 * EMBED], ((0,), (0,))
        ) + dot(other_spread[:, lanes], other[:, EMBED : 2 * EMBED], ((0,), (0,)))
        o[...] = acc[pl.ds(half, 320), :].astype(o.dtype)


def mlp_sum_kernel(place, r0, r1, r2, r3, o0, o1, o2, o3, acc):
    y = place[4]
    acc[...] = r0[...] + r1[...].astype(f32) + r2[...].astype(f32) + r3[...].astype(f32)
    for s, o in enumerate((o0, o1, o2, o3)):
        at = pl.multiple_of(lax.rem(y + s, 4) * 40, 40)
        o[0:40, :] = acc[pl.ds(at, 40), :].astype(o.dtype)
        o[40:80, :] = acc[pl.ds(at + 160, 40), :].astype(o.dtype)


def conv_sum_kernel(place, r0, r1, r2, r3, o0, o1, o2, o3, acc):
    x = place[3]
    total = r0[...] + r1[...].astype(f32) + r2[...].astype(f32) + r3[...].astype(f32)
    for lon in range(4):
        for to in range(4):
            at = lon * 80 + to * 20
            acc[to * 80 + lon * 20 : to * 80 + lon * 20 + 20, :] = total[at : at + 20, :]
    for s, o in enumerate((o0, o1, o2, o3)):
        at = pl.multiple_of(lax.rem(x + s, 4) * 80, 80)
        o[...] = acc[pl.ds(at, 80), :].astype(o.dtype)


def pack_kernel(m0, m1, m2, m3, c0, c1, c2, c3, o):
    mlp = m0[...] + m1[...].astype(f32) + m2[...].astype(f32) + m3[...].astype(f32)
    conv = c0[...] + c1[...].astype(f32) + c2[...].astype(f32) + c3[...].astype(f32)
    for to in range(8):
        o[to, 0:10, :] = conv[to * 10 : to * 10 + 10, :].astype(bf16)
        o[to, 10:15, :] = mlp[to * 5 : to * 5 + 5, :].astype(bf16)
        o[to, 15:20, :] = mlp[40 + to * 5 : 45 + to * 5, :].astype(bf16)


def final_kernel(parts, conv, w_in, w_out):
    total = parts[0].astype(f32)
    for i in range(1, 8):
        total = total + parts[i].astype(f32)
    total = total * (1.0 / math.sqrt(MEMBERS * NLAT * NLON))
    conv[...] = total[0:10, :]
    w_in[...] = total[10:15, :]
    w_out[...] = total[15:20, :]


def field_grad_kernel(
    place, tile, left, right, top, bottom, left_halo, right_halo, far,
    own_e, left_e, right_e, far_e, conv_weight, field_grad, win, band, coef, mixed
):
    lat = place[0]
    lon = place[1]
    fill_window(win, tile, left, right, top, bottom, left_halo, right_halo, far, lat)
    for group, e in enumerate((left_e, own_e, right_e, far_e)):
        set_rows(coef, group * 32, e[...].astype(f32))
    set_rows(coef, 128, top[HALO * LON : HALO * LON + 8, :].astype(f32))
    set_rows(coef, 136, bottom[HALO * LON : HALO * LON + 8, :].astype(f32))

    def base(cycle):
        if cycle < 0:
            return 128 + (cycle + HALO) * BASIS
        if cycle >= CYCLES:
            return 136 + (cycle - CYCLES) * BASIS
        return (
            lax.rem(cycle // OWNED - lon + 1 + 4, 4) * 32 + 16 + (cycle % OWNED) * BASIS
        )

    for j in range(CYCLES):
        starts = [base(j + e - HALO) for e in range(SPAN)]
        rows = band_rows(
            win, band.at[j % 2], coef, j, lambda e, k: (starts[e] + k, SPAN - 1 - e)
        )
        for k in range(BASIS):
            mixed[j * LON : (j + 1) * LON, k * EMBED : (k + 1) * EMBED] = rows[
                k * LON : (k + 1) * LON, :
            ].astype(bf16)
    total = tile[...].astype(f32)
    for k in range(BASIS):
        total = total + dot(
            mixed[:, k * EMBED : (k + 1) * EMBED],
            conv_weight[k * EMBED : (k + 1) * EMBED, :],
            ((1,), (1,)),
        )
    field_grad[...] = total.astype(bf16)


def call(kernel, outs, scratch, place, *args):
    in_specs = [pl.BlockSpec(memory_space=pltpu.VMEM)] * len(args)
    if place is not None:
        in_specs = [pl.BlockSpec(memory_space=pltpu.SMEM)] + in_specs
        args = (place,) + args
    return pl.pallas_call(
        kernel,
        out_shape=outs,
        in_specs=in_specs,
        scratch_shapes=scratch,
        compiler_params=VMEM,
    )(*args)


def polar_rows(tile, lat):
    return jnp.where(lat == 0, tile[: 4 * LON], tile[CELLS - 4 * LON :])


def far_pairs():
    pairs = []
    for lat in (0, 7):
        for lon in range(4):
            pairs.append((lat * 4 + lon, lat * 4 + (lon + 2) % 4))
    return pairs


def neighbours(tile, lat, to_up, to_down, side_extra):
    left = shift(tile, "zlo", 4, 1)
    right = shift(tile, "zlo", 4, 3)
    forward = [(i, i + 1) for i in range(7)]
    backward = [(i + 1, i) for i in range(7)]
    top = lax.ppermute(to_up, LAT, forward)
    bottom = lax.ppermute(to_down, LAT, backward)
    far = lax.ppermute(polar_rows(tile, lat), LAT + ("zlo",), far_pairs())
    rim = HALO * LON
    side = jnp.concatenate([top[:rim], bottom[:rim]] + side_extra, axis=0)
    left_side = shift(side, "zlo", 4, 1)
    right_side = shift(side, "zlo", 4, 3)
    return left, right, top, bottom, far, left_side, right_side


def coefficients(filter_basis, lon_offsets):
    lanes = jnp.arange(2 * NLON, dtype=jnp.int32) % NLON
    values = filter_basis.astype(f32)
    sides = []
    for sign in (1, -1):
        where_to = (sign * lon_offsets) % NLON
        hit = lanes[None, None, None, :] == where_to[:, :, :, None]
        kept = jnp.where(hit[:, None], values.transpose(0, 2, 1, 3)[..., None], 0.0)
        rows = kept.sum(axis=3).astype(bf16).reshape(OWNED * BASIS, SPAN * 2 * NLON)
        sides.append(jnp.pad(rows, ((0, 16 - OWNED * BASIS), (0, 0))))
    return jnp.concatenate(sides, axis=0)


def device_step(fields, filter_basis, lon_offsets, conv_weight, weight_in, weight_out, cotangent):
    y = lax.axis_index("y")
    core = lax.axis_index("core")
    lon = lax.axis_index("zlo")
    x = lax.axis_index("x")
    lat = 2 * y + core
    place = jnp.stack([lat, lon, core, x, y]).astype(jnp.int32)
    tile = fields.reshape(CELLS, EMBED)
    tangent = cotangent.reshape(CELLS, EMBED)
    rim = HALO * LON

    own_e = coefficients(filter_basis, lon_offsets)
    left, right, top, bottom, far, left_side, right_side = neighbours(
        tile, lat, tile[CELLS - rim :], tile[:rim], [own_e]
    )
    far_e = shift(own_e, "zlo", 4, 2)
    other_tangent = shift(tangent, "core", 2, 1)

    unit = jnp.arange(HIDDEN, dtype=jnp.int32)
    uc, ux, uy, ul, ur = unit // 640, unit // 160 % 4, unit // 40 % 4, unit // 10 % 4, unit % 10
    source = uy * 320 + uc * 160 + ul * 40 + ux * 10 + ur
    order = (unit[:, None] == source[None, :]).astype(bf16)
    weight_in = jnp.dot(weight_in, order, preferred_element_type=bf16)
    weight_out = dot(order, weight_out, ((0,), (0,))).astype(bf16)

    left_e, right_e = left_side[2 * rim :], right_side[2 * rim :]
    spread, edge = call(
        spread_kernel,
        (struct((CELLS, WIDE), bf16), struct((16, EMBED), bf16)),
        [
            pltpu.VMEM(((CYCLES + 2 * HALO) * NLON, EMBED), bf16),
            pltpu.VMEM((2, BASIS * LON, 384), bf16),
            pltpu.VMEM((SPAN, 128, 2 * NLON), f32),
        ],
        place, tile, left, right, top, bottom, left_side, right_side, far,
        own_e, left_e, right_e, far_e,
    )
    other_spread = shift(spread, "core", 2, 1)
    block_out, blend_grad, mine, theirs = call(
        mlp_kernel,
        (struct((CELLS, EMBED), bf16), struct((CELLS, EMBED), bf16))
        + (struct((CELLS, WIDE), bf16),) * 2,
        [],
        place, tile, tangent, spread, conv_weight, weight_in, weight_out,
    )
    other = shift(theirs, "core", 2, 1)

    chunk = (struct((320, EMBED), f32),) + (struct((320, EMBED), bf16),) * 3
    m = call(
        mlp_grad_kernel, chunk, [pltpu.VMEM((2 * EMBED, EMBED), f32)],
        place, mine, other, tangent, other_tangent,
    )
    m = (m[0],) + tuple(shift(m[s], "x", 4, s) for s in (1, 2, 3))
    c = call(
        conv_grad_kernel, chunk, [pltpu.VMEM((EMBED, EMBED), f32)],
        place, spread, other_spread, mine, other,
    )
    c = (c[0],) + tuple(shift(c[s], "y", 4, s) for s in (1, 2, 3))

    g_left, g_right, g_top, g_bottom, g_far, g_left_side, g_right_side = neighbours(
        blend_grad,
        lat,
        jnp.concatenate([blend_grad[CELLS - rim :], edge[8:16]], axis=0),
        jnp.concatenate([blend_grad[:rim], edge[0:8]], axis=0),
        [],
    )
    field_grad = call(
        field_grad_kernel,
        struct((CELLS, EMBED), bf16),
        [
            pltpu.VMEM(((CYCLES + 2 * HALO) * NLON, EMBED), bf16),
            pltpu.VMEM((2, BASIS * LON, 384), bf16),
            pltpu.VMEM((SPAN, 144, 2 * NLON), f32),
            pltpu.VMEM((CELLS, WIDE), bf16),
        ],
        place, blend_grad, g_left, g_right, g_top, g_bottom, g_left_side, g_right_side, g_far,
        own_e, left_e, right_e, far_e, conv_weight,
    )

    piece = (struct((80, EMBED), f32),) + (struct((80, EMBED), bf16),) * 3
    m = call(mlp_sum_kernel, piece, [pltpu.VMEM((320, EMBED), f32)], place, *m)
    m = (m[0],) + tuple(shift(m[s], "y", 4, s) for s in (1, 2, 3))
    c = call(conv_sum_kernel, piece, [pltpu.VMEM((320, EMBED), f32)], place, *c)
    c = (c[0],) + tuple(shift(c[s], "x", 4, s) for s in (1, 2, 3))
    packed = call(pack_kernel, struct((8, 20, EMBED), bf16), [], None, *m, *c)
    parts = lax.all_to_all(packed, ("zlo", "zhi"), split_axis=0, concat_axis=0, tiled=True)
    conv_grad, in_grad, out_grad = call(
        final_kernel,
        (struct((10, EMBED), f32), struct((5, EMBED), f32), struct((5, EMBED), f32)),
        [], None, parts,
    )
    return (
        block_out.reshape(fields.shape),
        field_grad.reshape(fields.shape),
        conv_grad,
        in_grad.T,
        out_grad,
    )


def solution(mesh):
    fine = Mesh(mesh.devices.reshape(4, 2, 4, 4, 2), ("y", "core", "zlo", "x", "zhi"))
    tile_spec = P(("x", "zhi"), LAT, "zlo", None)
    everyone = ("y", "core", "zlo", "x", "zhi")
    return jax.shard_map(
        device_step,
        mesh=fine,
        in_specs=(
            tile_spec,
            P(LAT + ("zlo",), None, None, None),
            P(LAT + ("zlo",), None, None),
            P(),
            P(),
            P(),
            tile_spec,
        ),
        out_specs=(
            tile_spec,
            tile_spec,
            P(everyone, None),
            P(None, everyone),
            P(everyone, None),
        ),
        check_vma=False,
    )
```

```python
import math

import jax
import jax.numpy as jnp
from jax import lax
from jax.experimental import pallas as pl
from jax.experimental.pallas import tpu as pltpu
from jax.sharding import Mesh, PartitionSpec as P

EMBED = 640
HIDDEN = 1280
BASIS = 4
SPAN = 5
NLON = 64
NLAT = 96
MEMBERS = 8
WIDE = BASIS * EMBED

CYCLES = 12
LON = 16
CELLS = CYCLES * LON
OWNED = 3
HALO = 2
RIM = HALO * LON
SHARED = WIDE + BASIS * 384

half_root = 0.7071067811865476
gauss_norm = 0.3989422804014327


LAT = ("y", "core")
bf16 = jnp.bfloat16
f32 = jnp.float32


def dot(a, b, dims):
    return lax.dot_general(a, b, (dims, ((), ())), preferred_element_type=f32)


def shift(block, axis, count, step):
    return lax.ppermute(block, axis, [(i, (i + step) % count) for i in range(count)])


def struct(shape, dtype):
    return jax.ShapeDtypeStruct(shape, dtype)


def fill_window(win, tile, left, right, top, bottom, left_halo, right_halo, far, lat):
    far_zero = jnp.zeros((LON, EMBED), bf16)
    for group, (inner, halo) in enumerate(
        ((left, left_halo), (tile, None), (right, right_halo))
    ):
        for row in range(CYCLES):
            at = (row + HALO) * NLON + group * LON
            win[at : at + LON, :] = inner[row * LON : (row + 1) * LON, :]
        for row in range(HALO):
            upper = top if halo is None else halo
            lower = bottom if halo is None else halo
            shift_rows = 0 if halo is None else HALO * LON
            at = row * NLON + group * LON
            win[at : at + LON, :] = upper[row * LON : (row + 1) * LON, :]
            at = (row + HALO + CYCLES) * NLON + group * LON
            win[at : at + LON, :] = lower[
                shift_rows + row * LON : shift_rows + (row + 1) * LON, :
            ]
    for row in range(CYCLES + 2 * HALO):
        at = row * NLON + 3 * LON
        win[at : at + LON, :] = far_zero

    @pl.when(lat == 0)
    def _():
        for row in range(4):
            at = (row + HALO) * NLON + 3 * LON
            win[at : at + LON, :] = far[row * LON : (row + 1) * LON, :]

    @pl.when(lat == 7)
    def _():
        for row in range(4):
            at = (row + HALO + CYCLES - 4) * NLON + 3 * LON
            win[at : at + LON, :] = far[row * LON : (row + 1) * LON, :]


def set_rows(coef, at, rows):
    for d in range(SPAN):
        coef[d, at : at + rows.shape[0], :] = rows[:, d * 128 : (d + 1) * 128]


def band_rows(win, band, coef, cycle, row_of):
    low_half = lax.broadcasted_iota(jnp.int32, (LON, 2 * NLON), 1) < NLON
    for k in range(BASIS):
        rolled = []
        for d in range(SPAN):
            row, lane = row_of(d, k)
            values = coef[lane, pl.ds(row, 1), :]
            spread_row = jnp.broadcast_to(values, (LON, 2 * NLON))
            rolled.append(pltpu.roll(spread_row, LON, 1, stride=1, stride_axis=0))
        at = k * LON
        band[at : at + LON, 0:128] = jnp.where(low_half, rolled[0], rolled[1]).astype(bf16)
        band[at : at + LON, 128:256] = jnp.where(low_half, rolled[2], rolled[3]).astype(bf16)
        band[at : at + LON, 256:384] = rolled[4].astype(bf16)
    window = win[cycle * NLON : cycle * NLON + SPAN * NLON, :]
    return dot(band[:, 0 : SPAN * NLON], window, ((1,), (0,)))


def forward_kernel(
    place, tile, left, right, top, bottom, left_side, right_side, far, own_e, far_e,
    tangent, conv_hbm, in_hbm, out_hbm,
    out, blend_grad, mine, theirs, to_up, to_down, to_far,
    win, band, coef, spread, conv_weight, weight_in, weight_out, sems
):
    lat = place[0]
    lon = place[1]
    core = place[2]
    loads = [
        pltpu.make_async_copy(source, target, sems.at[i])
        for i, (source, target) in enumerate(
            ((conv_hbm, conv_weight), (in_hbm, weight_in), (out_hbm, weight_out))
        )
    ]
    for load in loads:
        load.start()
    fill_window(win, tile, left, right, top, bottom, left_side, right_side, far, lat)
    set_rows(coef, 0, left_side[2 * RIM : 2 * RIM + 32, :].astype(f32))
    set_rows(coef, 32, own_e[...].astype(f32))
    set_rows(coef, 64, right_side[2 * RIM : 2 * RIM + 32, :].astype(f32))
    set_rows(coef, 96, far_e[...].astype(f32))

    def base(cycle):
        return lax.rem(cycle // OWNED - lon + 1 + 4, 4) * 32 + (cycle % OWNED) * BASIS

    for i in range(CYCLES):
        start = base(i)
        rows = band_rows(win, band.at[i % 2], coef, i, lambda d, k: (start + k, d))
        for k in range(BASIS):
            spread[i * LON : (i + 1) * LON, k * EMBED : (k + 1) * EMBED] = rows[
                k * LON : (k + 1) * LON, :
            ].astype(bf16)

    loads[0].wait()
    blended = (
        tile[...].astype(f32) + dot(spread[...], conv_weight[...], ((1,), (0,)))
    ).astype(bf16)
    loads[1].wait()
    preact = dot(blended, weight_in[...], ((1,), (0,)))
    cdf = 0.5 * (1.0 + lax.erf(preact * half_root))
    hidden = (preact * cdf).astype(bf16)
    loads[2].wait()
    out[...] = (
        blended.astype(f32) + dot(hidden, weight_out[...], ((1,), (0,)))
    ).astype(bf16)
    slope = cdf + preact * jnp.exp(-0.5 * preact * preact) * gauss_norm
    hidden_grad = dot(tangent[...], weight_out[...], ((1,), (1,)))
    preact_grad = (hidden_grad * slope).astype(bf16)
    grad = (
        tangent[...].astype(f32) + dot(preact_grad, weight_in[...], ((1,), (1,)))
    ).astype(bf16)
    blend_grad[...] = grad
    for side in (theirs, mine):
        side[:, 0:EMBED] = blended
        side[:, EMBED : 2 * EMBED] = grad
    for c in range(2):

        def store(side):
            half = slice(c * EMBED, (c + 1) * EMBED)
            side[:, 2 * EMBED : 3 * EMBED] = hidden[:, half]
            side[:, 3 * EMBED : 4 * EMBED] = preact_grad[:, half]
            for k in range(BASIS):
                at = k * EMBED + c * 320
                side[:, WIDE + k * 384 : WIDE + k * 384 + 320] = spread[:, at : at + 320]

        @pl.when(core == c)
        def _():
            store(mine)

        @pl.when(core != c)
        def _():
            store(theirs)

    edges = []
    for cycle in (0, 1, CYCLES - 2, CYCLES - 1):
        start = base(cycle) + 16
        for k in range(BASIS):
            edges.append(
                jnp.concatenate([coef[d, pl.ds(start + k, 1), :] for d in range(SPAN)], axis=1)
            )
    to_up[0:RIM, :] = grad[CELLS - RIM :, :]
    to_up[RIM : RIM + 8, :] = jnp.concatenate(edges[8:], axis=0).astype(bf16)
    to_down[0:RIM, :] = grad[:RIM, :]
    to_down[RIM : RIM + 8, :] = jnp.concatenate(edges[:8], axis=0).astype(bf16)
    to_far[...] = jnp.where(lat == 0, grad[: 4 * LON, :], grad[CELLS - 4 * LON :, :])


def mlp_grad_kernel(place, mine, other, tangent, other_tangent, o0, o1, o2, o3, acc):
    x = place[3]
    acc[0:EMBED, :] = dot(
        mine[:, 3 * EMBED : 4 * EMBED], mine[:, 0:EMBED], ((0,), (0,))
    ) + dot(other[:, 3 * EMBED : 4 * EMBED], other[:, 0:EMBED], ((0,), (0,)))
    acc[EMBED : 2 * EMBED, :] = dot(
        mine[:, 2 * EMBED : 3 * EMBED], tangent[...], ((0,), (0,))
    ) + dot(other[:, 2 * EMBED : 3 * EMBED], other_tangent[...], ((0,), (0,)))
    for s, o in enumerate((o0, o1, o2, o3)):
        at = pl.multiple_of(lax.rem(x + s, 4) * 160, 160)
        o[0:160, :] = acc[pl.ds(at, 160), :].astype(o.dtype)
        o[160:320, :] = acc[pl.ds(at + EMBED, 160), :].astype(o.dtype)


def conv_grad_kernel(place, mine, other, o0, o1, o2, o3):
    y = place[4]
    for s, o in enumerate((o0, o1, o2, o3)):
        lanes = pl.ds(pl.multiple_of(lax.rem(y + s, 4) * 384 + WIDE, 128), 384)
        rows = dot(mine[:, lanes], mine[:, EMBED : 2 * EMBED], ((0,), (0,))) + dot(
            other[:, lanes], other[:, EMBED : 2 * EMBED], ((0,), (0,))
        )
        o[...] = rows[0:320, :].astype(o.dtype)


def mlp_sum_kernel(place, r0, r1, r2, r3, o0, o1, o2, o3, acc):
    y = place[4]
    acc[...] = r0[...] + r1[...].astype(f32) + r2[...].astype(f32) + r3[...].astype(f32)
    for s, o in enumerate((o0, o1, o2, o3)):
        at = pl.multiple_of(lax.rem(y + s, 4) * 40, 40)
        o[0:40, :] = acc[pl.ds(at, 40), :].astype(o.dtype)
        o[40:80, :] = acc[pl.ds(at + 160, 40), :].astype(o.dtype)


def conv_sum_kernel(place, r0, r1, r2, r3, o0, o1, o2, o3, acc):
    x = place[3]
    total = r0[...] + r1[...].astype(f32) + r2[...].astype(f32) + r3[...].astype(f32)
    for lon in range(4):
        for to in range(4):
            at = lon * 80 + to * 20
            acc[to * 80 + lon * 20 : to * 80 + lon * 20 + 20, :] = total[at : at + 20, :]
    for s, o in enumerate((o0, o1, o2, o3)):
        at = pl.multiple_of(lax.rem(x + s, 4) * 80, 80)
        o[...] = acc[pl.ds(at, 80), :].astype(o.dtype)


def pack_kernel(m0, m1, m2, m3, c0, c1, c2, c3, o):
    mlp = m0[...] + m1[...].astype(f32) + m2[...].astype(f32) + m3[...].astype(f32)
    conv = c0[...] + c1[...].astype(f32) + c2[...].astype(f32) + c3[...].astype(f32)
    for to in range(8):
        o[to, 0:10, :] = conv[to * 10 : to * 10 + 10, :].astype(bf16)
        o[to, 10:15, :] = mlp[to * 5 : to * 5 + 5, :].astype(bf16)
        o[to, 15:20, :] = mlp[40 + to * 5 : 45 + to * 5, :].astype(bf16)


def final_kernel(parts, conv, w_in, w_out):
    total = parts[0].astype(f32)
    for i in range(1, 8):
        total = total + parts[i].astype(f32)
    total = total * (1.0 / math.sqrt(MEMBERS * NLAT * NLON))
    conv[...] = total[0:10, :]
    w_in[...] = total[10:15, :]
    w_out[...] = total[15:20, :]


def field_grad_kernel(
    place, tile, left, right, top, bottom, left_halo, right_halo, far,
    own_e, left_e, right_e, far_e, conv_hbm, field_grad, win, band, coef, mixed,
    conv_weight, sem
):
    lat = place[0]
    lon = place[1]
    load = pltpu.make_async_copy(conv_hbm, conv_weight, sem)
    load.start()
    fill_window(win, tile, left, right, top, bottom, left_halo, right_halo, far, lat)
    set_rows(coef, 0, left_e[2 * RIM : 2 * RIM + 32, :].astype(f32))
    set_rows(coef, 32, own_e[...].astype(f32))
    set_rows(coef, 64, right_e[2 * RIM : 2 * RIM + 32, :].astype(f32))
    set_rows(coef, 96, far_e[...].astype(f32))
    set_rows(coef, 128, top[HALO * LON : HALO * LON + 8, :].astype(f32))
    set_rows(coef, 136, bottom[HALO * LON : HALO * LON + 8, :].astype(f32))

    def base(cycle):
        if cycle < 0:
            return 128 + (cycle + HALO) * BASIS
        if cycle >= CYCLES:
            return 136 + (cycle - CYCLES) * BASIS
        return (
            lax.rem(cycle // OWNED - lon + 1 + 4, 4) * 32 + 16 + (cycle % OWNED) * BASIS
        )

    for j in range(CYCLES):
        starts = [base(j + e - HALO) for e in range(SPAN)]
        rows = band_rows(
            win, band.at[j % 2], coef, j, lambda e, k: (starts[e] + k, SPAN - 1 - e)
        )
        for k in range(BASIS):
            mixed[j * LON : (j + 1) * LON, k * EMBED : (k + 1) * EMBED] = rows[
                k * LON : (k + 1) * LON, :
            ].astype(bf16)
    total = tile[...].astype(f32)
    load.wait()
    for k in range(BASIS):
        total = total + dot(
            mixed[:, k * EMBED : (k + 1) * EMBED],
            conv_weight[k * EMBED : (k + 1) * EMBED, :],
            ((1,), (1,)),
        )
    field_grad[...] = total.astype(bf16)


def call(kernel, outs, scratch, mib, place, *args, in_hbm=()):
    vmem, hbm = pl.BlockSpec(memory_space=pltpu.VMEM), pl.BlockSpec(memory_space=pltpu.HBM)
    in_specs = [vmem] * len(args) + [hbm] * len(in_hbm)
    args = args + tuple(in_hbm)
    if place is not None:
        in_specs = [pl.BlockSpec(memory_space=pltpu.SMEM)] + in_specs
        args = (place,) + args
    return pl.pallas_call(
        kernel,
        out_shape=outs,
        in_specs=in_specs,
        scratch_shapes=scratch,
        compiler_params=pltpu.CompilerParams(vmem_limit_bytes=mib * 1024 * 1024),
    )(*args)


def polar_rows(tile, lat):
    return jnp.where(lat == 0, tile[: 4 * LON], tile[CELLS - 4 * LON :])


def far_pairs():
    pairs = []
    for lat in (0, 7):
        for lon in range(4):
            pairs.append((lat * 4 + lon, lat * 4 + (lon + 2) % 4))
    return pairs


def neighbours(tile, to_up, to_down, to_far, side_extra):
    left = shift(tile, "zlo", 4, 1)
    right = shift(tile, "zlo", 4, 3)
    forward = [(i, i + 1) for i in range(7)]
    backward = [(i + 1, i) for i in range(7)]
    top = lax.ppermute(to_up, LAT, forward)
    bottom = lax.ppermute(to_down, LAT, backward)
    far = lax.ppermute(to_far, LAT + ("zlo",), far_pairs())
    side = jnp.concatenate([top[:RIM], bottom[:RIM]] + side_extra, axis=0)
    return left, right, top, bottom, far, side


def coefficients(filter_basis, lon_offsets):
    lanes = jnp.arange(2 * NLON, dtype=jnp.int32) % NLON
    values = filter_basis.astype(f32)
    sides = []
    for sign in (1, -1):
        where_to = (sign * lon_offsets) % NLON
        hit = lanes[None, None, None, :] == where_to[:, :, :, None]
        kept = jnp.where(hit[:, None], values.transpose(0, 2, 1, 3)[..., None], 0.0)
        rows = kept.sum(axis=3).astype(bf16).reshape(OWNED * BASIS, SPAN * 2 * NLON)
        sides.append(jnp.pad(rows, ((0, 16 - OWNED * BASIS), (0, 0))))
    return jnp.concatenate(sides, axis=0)


def device_step(fields, filter_basis, lon_offsets, conv_weight, weight_in, weight_out, cotangent):
    y = lax.axis_index("y")
    core = lax.axis_index("core")
    lon = lax.axis_index("zlo")
    x = lax.axis_index("x")
    lat = 2 * y + core
    place = jnp.stack([lat, lon, core, x, y]).astype(jnp.int32)
    tile = fields.reshape(CELLS, EMBED)
    tangent = cotangent.reshape(CELLS, EMBED)

    own_e = coefficients(filter_basis, lon_offsets)
    left, right, top, bottom, far, side = neighbours(
        tile, tile[CELLS - RIM :], tile[:RIM], polar_rows(tile, lat), [own_e]
    )
    far_e = shift(own_e, "zlo", 4, 2)
    other_tangent = shift(tangent, "core", 2, 1)
    side, weight_in, weight_out = lax.optimization_barrier((side, weight_in, weight_out))
    left_side = shift(side, "zlo", 4, 1)
    right_side = shift(side, "zlo", 4, 3)

    unit = jnp.arange(HIDDEN, dtype=jnp.int32)
    uc, ux, uy, ul, ur = unit // 640, unit // 160 % 4, unit // 40 % 4, unit // 10 % 4, unit % 10
    source = uy * 320 + uc * 160 + ul * 40 + ux * 10 + ur
    order = (unit[:, None] == source[None, :]).astype(bf16)
    weight_in = jnp.dot(weight_in, order, preferred_element_type=bf16)
    weight_out = dot(order, weight_out, ((0,), (0,))).astype(bf16)

    other_tangent, far_e, far = lax.optimization_barrier((other_tangent, far_e, far))
    window = pltpu.VMEM(((CYCLES + 2 * HALO) * NLON, EMBED), bf16)
    band = pltpu.VMEM((2, BASIS * LON, 384), bf16)
    edge = struct((RIM + 8, EMBED), bf16)
    block_out, blend_grad, mine, theirs, to_up, to_down, to_far = call(
        forward_kernel,
        (struct((CELLS, EMBED), bf16), struct((CELLS, EMBED), bf16))
        + (struct((CELLS, SHARED), bf16),) * 2
        + (edge, edge, struct((4 * LON, EMBED), bf16)),
        [
            window,
            band,
            pltpu.VMEM((SPAN, 128, 2 * NLON), f32),
            pltpu.VMEM((CELLS, WIDE), bf16),
            pltpu.VMEM((WIDE, EMBED), bf16),
            pltpu.VMEM((EMBED, HIDDEN), bf16),
            pltpu.VMEM((HIDDEN, EMBED), bf16),
            pltpu.SemaphoreType.DMA((3,)),
        ],
        24, place, tile, left, right, top, bottom, left_side, right_side, far, own_e, far_e,
        tangent, in_hbm=(conv_weight, weight_in, weight_out),
    )
    other = shift(theirs, "core", 2, 1)
    g_left, g_right, g_top, g_bottom, g_far, g_side = neighbours(
        blend_grad, to_up, to_down, to_far, []
    )

    chunk = (struct((320, EMBED), f32),) + (struct((320, EMBED), bf16),) * 3
    c = call(conv_grad_kernel, chunk, [], 16, place, mine, other)
    c = (c[0],) + tuple(shift(c[s], "y", 4, s) for s in (1, 2, 3))
    m = call(
        mlp_grad_kernel, chunk, [pltpu.VMEM((2 * EMBED, EMBED), f32)],
        16, place, mine, other, tangent, other_tangent,
    )
    m = (m[0],) + tuple(shift(m[s], "x", 4, s) for s in (1, 2, 3))

    c0, g_side = lax.optimization_barrier((c[0], g_side))
    c = (c0,) + c[1:]
    g_left_side = shift(g_side, "zlo", 4, 1)
    g_right_side = shift(g_side, "zlo", 4, 3)
    piece = (struct((80, EMBED), f32),) + (struct((80, EMBED), bf16),) * 3
    c = call(conv_sum_kernel, piece, [pltpu.VMEM((320, EMBED), f32)], 8, place, *c)
    c = (c[0],) + tuple(shift(c[s], "x", 4, s) for s in (1, 2, 3))
    m = call(mlp_sum_kernel, piece, [pltpu.VMEM((320, EMBED), f32)], 8, place, *m)
    m = (m[0],) + tuple(shift(m[s], "y", 4, s) for s in (1, 2, 3))
    m0, g_left, g_right, g_far, g_left_side, g_right_side = lax.optimization_barrier(
        (m[0], g_left, g_right, g_far, g_left_side, g_right_side)
    )
    packed = call(pack_kernel, struct((8, 20, EMBED), bf16), [], 4, None, m0, *m[1:], *c)
    parts = lax.all_to_all(packed, ("zlo", "zhi"), split_axis=0, concat_axis=0, tiled=True)
    field_grad = call(
        field_grad_kernel,
        struct((CELLS, EMBED), bf16),
        [
            window,
            band,
            pltpu.VMEM((SPAN, 144, 2 * NLON), f32),
            pltpu.VMEM((CELLS, WIDE), bf16),
            pltpu.VMEM((WIDE, EMBED), bf16),
            pltpu.SemaphoreType.DMA,
        ],
        16, place, blend_grad, g_left, g_right, g_top, g_bottom, g_left_side, g_right_side, g_far,
        own_e, left_side, right_side, far_e, in_hbm=(conv_weight,),
    )
    conv_grad, in_grad, out_grad = call(
        final_kernel,
        (struct((10, EMBED), f32), struct((5, EMBED), f32), struct((5, EMBED), f32)),
        [], 4, None, parts,
    )
    return (
        block_out.reshape(fields.shape),
        field_grad.reshape(fields.shape),
        conv_grad,
        in_grad.T,
        out_grad,
    )


def solution(mesh):
    fine = Mesh(mesh.devices.reshape(4, 2, 4, 4, 2), ("y", "core", "zlo", "x", "zhi"))
    tile_spec = P(("x", "zhi"), LAT, "zlo", None)
    everyone = ("y", "core", "zlo", "x", "zhi")
    return jax.shard_map(
        device_step,
        mesh=fine,
        in_specs=(
            tile_spec,
            P(LAT + ("zlo",), None, None, None),
            P(LAT + ("zlo",), None, None),
            P(),
            P(),
            P(),
            tile_spec,
        ),
        out_specs=(
            tile_spec,
            tile_spec,
            P(everyone, None),
            P(None, everyone),
            P(everyone, None),
        ),
        check_vma=False,
    )
```

```python
import math

import jax
import jax.numpy as jnp
from jax import lax
from jax.experimental import pallas as pl
from jax.experimental.pallas import tpu as pltpu
from jax.sharding import Mesh, PartitionSpec as P


EMBED = 640
HIDDEN = 1280
BASIS = 4
SPAN = 5
NLON = 64
NLAT = 96
MEMBERS = 8
WIDE = BASIS * EMBED

CYCLES = 12
LON = 16
CELLS = CYCLES * LON
OWNED = 3
HALO = 2
RIM = HALO * LON
CONV_PART = EMBED + BASIS * 384
MLP_PART = 3 * EMBED

half_root = 0.7071067811865476
gauss_norm = 0.3989422804014327


LAT = ("y", "core")
bf16 = jnp.bfloat16
f32 = jnp.float32


def dot(a, b, dims):
    return lax.dot_general(a, b, (dims, ((), ())), preferred_element_type=f32)


def shift(block, axis, count, step):
    return lax.ppermute(block, axis, [(i, (i + step) % count) for i in range(count)])


def struct(shape, dtype):
    return jax.ShapeDtypeStruct(shape, dtype)


def fill_window(win, tile, left, right, top, bottom, left_halo, right_halo, far, lat):
    far_zero = jnp.zeros((LON, EMBED), bf16)
    for group, (inner, halo) in enumerate(
        ((left, left_halo), (tile, None), (right, right_halo))
    ):
        for row in range(CYCLES):
            at = (row + HALO) * NLON + group * LON
            win[at : at + LON, :] = inner[row * LON : (row + 1) * LON, :]
        for row in range(HALO):
            upper = top if halo is None else halo
            lower = bottom if halo is None else halo
            shift_rows = 0 if halo is None else bottom.shape[0]
            at = row * NLON + group * LON
            win[at : at + LON, :] = upper[row * LON : (row + 1) * LON, :]
            at = (row + HALO + CYCLES) * NLON + group * LON
            win[at : at + LON, :] = lower[
                shift_rows + row * LON : shift_rows + (row + 1) * LON, :
            ]
    for row in range(CYCLES + 2 * HALO):
        at = row * NLON + 3 * LON
        win[at : at + LON, :] = far_zero

    @pl.when(lat == 0)
    def _():
        for row in range(4):
            at = (row + HALO) * NLON + 3 * LON
            win[at : at + LON, :] = far[row * LON : (row + 1) * LON, :]

    @pl.when(lat == 7)
    def _():
        for row in range(4):
            at = (row + HALO + CYCLES - 4) * NLON + 3 * LON
            win[at : at + LON, :] = far[row * LON : (row + 1) * LON, :]


def set_rows(coef, at, rows):
    for d in range(SPAN):
        coef[d, at : at + rows.shape[0], :] = rows[:, d * 128 : (d + 1) * 128]


def band_rows(win, band, coef, cycle, row_of):
    low_half = lax.broadcasted_iota(jnp.int32, (LON, 2 * NLON), 1) < NLON
    for k in range(BASIS):
        rolled = []
        for d in range(SPAN):
            row, lane = row_of(d, k)
            values = coef[lane, pl.ds(row, 1), :]
            spread_row = jnp.broadcast_to(values, (LON, 2 * NLON))
            rolled.append(pltpu.roll(spread_row, LON, 1, stride=1, stride_axis=0))
        at = k * LON
        band[at : at + LON, 0:128] = jnp.where(low_half, rolled[0], rolled[1]).astype(bf16)
        band[at : at + LON, 128:256] = jnp.where(low_half, rolled[2], rolled[3]).astype(bf16)
        band[at : at + LON, 256:384] = rolled[4].astype(bf16)
    window = win[cycle * NLON : cycle * NLON + SPAN * NLON, :]
    return dot(band[:, 0 : SPAN * NLON], window, ((1,), (0,)))


def forward_kernel(
    place, tile, left, right, top, bottom, left_side, right_side, far, own_e,
    tangent, conv_hbm, in_hbm, out_hbm,
    out, blend_grad, mine, mine_mlp, theirs, theirs_mlp, to_up, to_down, to_far,
    win, band, coef, spread, conv_weight, weight_in, weight_out, sems
):
    lat = place[0]
    lon = place[1]
    core = place[2]
    loads = [
        pltpu.make_async_copy(source, target, sems.at[i])
        for i, (source, target) in enumerate(
            ((conv_hbm, conv_weight), (in_hbm, weight_in), (out_hbm, weight_out))
        )
    ]
    for load in loads:
        load.start()
    fill_window(win, tile, left, right, top, bottom, left_side, right_side, far, lat)
    set_rows(coef, 0, left_side[2 * RIM : 2 * RIM + 32, :].astype(f32))
    set_rows(coef, 32, own_e[...].astype(f32))
    set_rows(coef, 64, right_side[2 * RIM : 2 * RIM + 32, :].astype(f32))
    set_rows(coef, 96, far[4 * LON : 4 * LON + 32, :].astype(f32))

    def base(cycle):
        return lax.rem(cycle // OWNED - lon + 1 + 4, 4) * 32 + (cycle % OWNED) * BASIS

    for i in range(CYCLES):
        start = base(i)
        rows = band_rows(win, band.at[i % 2], coef, i, lambda d, k: (start + k, d))
        for k in range(BASIS):
            spread[i * LON : (i + 1) * LON, k * EMBED : (k + 1) * EMBED] = rows[
                k * LON : (k + 1) * LON, :
            ].astype(bf16)

    loads[0].wait()
    blended = (
        tile[...].astype(f32) + dot(spread[...], conv_weight[...], ((1,), (0,)))
    ).astype(bf16)
    loads[1].wait()
    preact = dot(blended, weight_in[...], ((1,), (0,)))
    cdf = 0.5 * (1.0 + lax.erf(preact * half_root))
    hidden = (preact * cdf).astype(bf16)
    loads[2].wait()
    out[...] = (
        blended.astype(f32) + dot(hidden, weight_out[...], ((1,), (0,)))
    ).astype(bf16)
    slope = cdf + preact * jnp.exp(-0.5 * preact * preact) * gauss_norm
    hidden_grad = dot(tangent[...], weight_out[...], ((1,), (1,)))
    preact_grad = (hidden_grad * slope).astype(bf16)
    grad = (
        tangent[...].astype(f32) + dot(preact_grad, weight_in[...], ((1,), (1,)))
    ).astype(bf16)
    blend_grad[...] = grad
    for side in (theirs, mine):
        side[:, 0:EMBED] = grad
    for side in (theirs_mlp, mine_mlp):
        side[:, 0:EMBED] = blended
    for c in range(2):

        def store(side, side_mlp):
            for k in range(BASIS):
                at = k * EMBED + c * 320
                to = EMBED + k * 384
                side[:, to : to + 320] = spread[:, at : at + 320]
                at = k * 320 + c * 160
                to = EMBED + k * 160
                side_mlp[:, to : to + 160] = hidden[:, at : at + 160]
                side_mlp[:, to + EMBED : to + EMBED + 160] = preact_grad[:, at : at + 160]

        @pl.when(core == c)
        def _():
            store(mine, mine_mlp)

        @pl.when(core != c)
        def _():
            store(theirs, theirs_mlp)

    edges = []
    for cycle in (0, 1, CYCLES - 2, CYCLES - 1):
        start = base(cycle) + 16
        for k in range(BASIS):
            edges.append(
                jnp.concatenate([coef[d, pl.ds(start + k, 1), :] for d in range(SPAN)], axis=1)
            )
    to_up[0:RIM, :] = grad[CELLS - RIM :, :]
    to_up[RIM : RIM + 8, :] = jnp.concatenate(edges[8:], axis=0).astype(bf16)
    to_down[0:RIM, :] = grad[:RIM, :]
    to_down[RIM : RIM + 8, :] = jnp.concatenate(edges[:8], axis=0).astype(bf16)
    to_far[...] = jnp.where(lat == 0, grad[: 4 * LON, :], grad[CELLS - 4 * LON :, :])


def mlp_grad_kernel(place, mine, other, tangent, other_tangent, order, o0, o1, o2, o3, acc):
    x = place[3]
    sides = []
    for side, cot in ((mine, tangent), (other, other_tangent)):
        hidden = dot(side[:, EMBED : 2 * EMBED], order[...], ((1,), (0,))).astype(bf16)
        grad = dot(side[:, 2 * EMBED : 3 * EMBED], order[...], ((1,), (0,))).astype(bf16)
        sides.append((hidden, grad, side[:, 0:EMBED], cot[...]))
    acc[0:EMBED, :] = dot(sides[0][1], sides[0][2], ((0,), (0,))) + dot(
        sides[1][1], sides[1][2], ((0,), (0,))
    )
    acc[EMBED : 2 * EMBED, :] = dot(sides[0][0], sides[0][3], ((0,), (0,))) + dot(
        sides[1][0], sides[1][3], ((0,), (0,))
    )
    for s, o in enumerate((o0, o1, o2, o3)):
        at = pl.multiple_of(lax.rem(x + s, 4) * 160, 160)
        o[0:160, :] = acc[pl.ds(at, 160), :].astype(o.dtype)
        o[160:320, :] = acc[pl.ds(at + EMBED, 160), :].astype(o.dtype)


def conv_grad_kernel(place, mine, other, o0, o1, o2, o3):
    y = place[4]
    for s, o in enumerate((o0, o1, o2, o3)):
        lanes = pl.ds(pl.multiple_of(lax.rem(y + s, 4) * 384 + EMBED, 128), 384)
        rows = dot(mine[:, lanes], mine[:, 0:EMBED], ((0,), (0,))) + dot(
            other[:, lanes], other[:, 0:EMBED], ((0,), (0,))
        )
        o[...] = rows[0:320, :].astype(o.dtype)


def mlp_sum_kernel(place, r0, r1, r2, r3, o0, o1, o2, o3, acc):
    y = place[4]
    acc[...] = r0[...] + r1[...].astype(f32) + r2[...].astype(f32) + r3[...].astype(f32)
    for s, o in enumerate((o0, o1, o2, o3)):
        at = pl.multiple_of(lax.rem(y + s, 4) * 40, 40)
        o[0:40, :] = acc[pl.ds(at, 40), :].astype(o.dtype)
        o[40:80, :] = acc[pl.ds(at + 160, 40), :].astype(o.dtype)


def conv_sum_kernel(place, r0, r1, r2, r3, o0, o1, o2, o3, acc):
    x = place[3]
    total = r0[...] + r1[...].astype(f32) + r2[...].astype(f32) + r3[...].astype(f32)
    for lon in range(4):
        for to in range(4):
            at = lon * 80 + to * 20
            acc[to * 80 + lon * 20 : to * 80 + lon * 20 + 20, :] = total[at : at + 20, :]
    for s, o in enumerate((o0, o1, o2, o3)):
        at = pl.multiple_of(lax.rem(x + s, 4) * 80, 80)
        o[...] = acc[pl.ds(at, 80), :].astype(o.dtype)


def pack_kernel(m0, m1, m2, m3, c0, c1, c2, c3, o):
    mlp = m0[...] + m1[...].astype(f32) + m2[...].astype(f32) + m3[...].astype(f32)
    conv = c0[...] + c1[...].astype(f32) + c2[...].astype(f32) + c3[...].astype(f32)
    for to in range(8):
        o[to, 0:10, :] = conv[to * 10 : to * 10 + 10, :].astype(bf16)
        o[to, 10:15, :] = mlp[to * 5 : to * 5 + 5, :].astype(bf16)
        o[to, 15:20, :] = mlp[40 + to * 5 : 45 + to * 5, :].astype(bf16)


def final_kernel(parts, conv, w_in, w_out):
    total = parts[0].astype(f32)
    for i in range(1, 8):
        total = total + parts[i].astype(f32)
    total = total * (1.0 / math.sqrt(MEMBERS * NLAT * NLON))
    conv[...] = total[0:10, :]
    w_in[...] = total[10:15, :]
    w_out[...] = total[15:20, :]


def field_grad_kernel(
    place, tile, left, right, top, bottom, left_halo, right_halo, far,
    own_e, left_e, right_e, far_e, conv_hbm, field_grad, win, band, coef, mixed,
    conv_weight, sem
):
    lat = place[0]
    lon = place[1]
    load = pltpu.make_async_copy(conv_hbm, conv_weight, sem)
    load.start()
    fill_window(win, tile, left, right, top, bottom, left_halo, right_halo, far, lat)
    set_rows(coef, 0, left_e[2 * RIM : 2 * RIM + 32, :].astype(f32))
    set_rows(coef, 32, own_e[...].astype(f32))
    set_rows(coef, 64, right_e[2 * RIM : 2 * RIM + 32, :].astype(f32))
    set_rows(coef, 96, far_e[4 * LON : 4 * LON + 32, :].astype(f32))
    set_rows(coef, 128, top[HALO * LON : HALO * LON + 8, :].astype(f32))
    set_rows(coef, 136, bottom[HALO * LON : HALO * LON + 8, :].astype(f32))

    def base(cycle):
        if cycle < 0:
            return 128 + (cycle + HALO) * BASIS
        if cycle >= CYCLES:
            return 136 + (cycle - CYCLES) * BASIS
        return (
            lax.rem(cycle // OWNED - lon + 1 + 4, 4) * 32 + 16 + (cycle % OWNED) * BASIS
        )

    for j in range(CYCLES):
        starts = [base(j + e - HALO) for e in range(SPAN)]
        rows = band_rows(
            win, band.at[j % 2], coef, j, lambda e, k: (starts[e] + k, SPAN - 1 - e)
        )
        for k in range(BASIS):
            mixed[j * LON : (j + 1) * LON, k * EMBED : (k + 1) * EMBED] = rows[
                k * LON : (k + 1) * LON, :
            ].astype(bf16)
    total = tile[...].astype(f32)
    load.wait()
    for k in range(BASIS):
        total = total + dot(
            mixed[:, k * EMBED : (k + 1) * EMBED],
            conv_weight[k * EMBED : (k + 1) * EMBED, :],
            ((1,), (1,)),
        )
    field_grad[...] = total.astype(bf16)


def call(kernel, outs, scratch, mib, place, *args, in_hbm=()):
    vmem, hbm = pl.BlockSpec(memory_space=pltpu.VMEM), pl.BlockSpec(memory_space=pltpu.HBM)
    in_specs = [vmem] * len(args) + [hbm] * len(in_hbm)
    args = args + tuple(pltpu.with_memory_space_constraint(a, pltpu.HBM) for a in in_hbm)
    if place is not None:
        in_specs = [pl.BlockSpec(memory_space=pltpu.SMEM)] + in_specs
        args = (place,) + args
    return pl.pallas_call(
        kernel,
        out_shape=outs,
        in_specs=in_specs,
        scratch_shapes=scratch,
        compiler_params=pltpu.CompilerParams(vmem_limit_bytes=mib * 1024 * 1024),
    )(*args)


def polar_rows(tile, lat):
    return jnp.where(lat == 0, tile[: 4 * LON], tile[CELLS - 4 * LON :])


def neighbours(tile, to_up, to_down):
    forward = [(i, i + 1) for i in range(7)]
    backward = [(i + 1, i) for i in range(7)]
    left = shift(tile, "zlo", 4, 1)
    right = shift(tile, "zlo", 4, 3)
    top = lax.ppermute(to_up, LAT, forward)
    bottom = lax.ppermute(to_down, LAT, backward)
    return left, right, top, bottom


def relay(side):
    left_side = shift(side, "zlo", 4, 1)
    right_side = shift(side, "zlo", 4, 3)
    return left_side, right_side


def spread_out(chunks, axis):
    parts = [chunks[0]]
    for s in (1, 2, 3):
        parts.append(shift(chunks[s], axis, 4, s))
    return tuple(parts)


def coefficients(filter_basis, lon_offsets):
    lanes = jnp.arange(2 * NLON, dtype=jnp.int32) % NLON
    values = filter_basis.astype(f32)
    sides = []
    for sign in (1, -1):
        where_to = (sign * lon_offsets) % NLON
        hit = lanes[None, None, None, :] == where_to[:, :, :, None]
        kept = jnp.where(hit[:, None], values.transpose(0, 2, 1, 3)[..., None], 0.0)
        rows = kept.sum(axis=3).astype(bf16).reshape(OWNED * BASIS, SPAN * 2 * NLON)
        sides.append(jnp.pad(rows, ((0, 16 - OWNED * BASIS), (0, 0))))
    return jnp.concatenate(sides, axis=0)


def block(fields, filter_basis, lon_offsets, conv_weight, weight_in, weight_out, cotangent):
    y = lax.axis_index("y")
    core = lax.axis_index("core")
    lon = lax.axis_index("zlo")
    x = lax.axis_index("x")
    lat = 2 * y + core
    place = jnp.stack([lat, lon, core, x, y]).astype(jnp.int32)
    tile = fields.reshape(CELLS, EMBED)
    tangent = cotangent.reshape(CELLS, EMBED)

    left, right, top, bottom = neighbours(tile, tile[CELLS - RIM :], tile[:RIM])
    own_e = coefficients(filter_basis, lon_offsets)
    to_far = jnp.concatenate([polar_rows(tile, lat), own_e], axis=0)
    far = shift(to_far, "zlo", 4, 2)
    left_side, right_side = relay(jnp.concatenate([top, bottom, own_e], axis=0))
    other_tangent = shift(tangent, "core", 2, 1)

    unit = jnp.arange(EMBED, dtype=jnp.int32)
    ux, uy, ul, ur = unit // 160, unit // 40 % 4, unit // 10 % 4, unit % 10
    source = uy * 160 + ul * 40 + ux * 10 + ur
    order = (unit[:, None] == source[None, :]).astype(bf16)

    far, other_tangent, order = lax.optimization_barrier((far, other_tangent, order))
    window = pltpu.VMEM(((CYCLES + 2 * HALO) * NLON, EMBED), bf16)
    band = pltpu.VMEM((2, BASIS * LON, 384), bf16)
    edge = struct((RIM + 8, EMBED), bf16)
    parts = (struct((CELLS, CONV_PART), bf16), struct((CELLS, MLP_PART), bf16))
    block_out, blend_grad, mine, mine_mlp, theirs, theirs_mlp, to_up, to_down, to_far = call(
        forward_kernel,
        (struct((CELLS, EMBED), bf16), struct((CELLS, EMBED), bf16))
        + parts
        + parts
        + (edge, edge, struct((4 * LON, EMBED), bf16)),
        [
            window,
            band,
            pltpu.VMEM((SPAN, 128, 2 * NLON), f32),
            pltpu.VMEM((CELLS, WIDE), bf16),
            pltpu.VMEM((WIDE, EMBED), bf16),
            pltpu.VMEM((EMBED, HIDDEN), bf16),
            pltpu.VMEM((HIDDEN, EMBED), bf16),
            pltpu.SemaphoreType.DMA((3,)),
        ],
        24, place, tile, left, right, top, bottom, left_side, right_side, far, own_e,
        tangent, in_hbm=(conv_weight, weight_in, weight_out),
    )
    other = shift(theirs, "core", 2, 1)
    other_mlp = shift(theirs_mlp, "core", 2, 1)
    g_left, g_right, g_top, g_bottom = neighbours(blend_grad, to_up, to_down)
    g_far = shift(to_far, "zlo", 4, 2)

    chunk = (struct((320, EMBED), f32),) + (struct((320, EMBED), bf16),) * 3
    c = call(conv_grad_kernel, chunk, [], 16, place, mine, other)
    c = spread_out(c, "y")
    m = call(
        mlp_grad_kernel, chunk, [pltpu.VMEM((2 * EMBED, EMBED), f32)],
        16, place, mine_mlp, other_mlp, tangent, other_tangent, order,
    )
    m = spread_out(m, "x")

    g_left_side, g_right_side = relay(jnp.concatenate([g_top, g_bottom], axis=0))
    piece = (struct((80, EMBED), f32),) + (struct((80, EMBED), bf16),) * 3
    total = pltpu.VMEM((320, EMBED), f32)
    c = call(conv_sum_kernel, piece, [total], 8, place, *c)
    c = spread_out(c, "x")
    m = call(mlp_sum_kernel, piece, [total], 8, place, *m)
    m = spread_out(m, "y")
    field_grad = call(
        field_grad_kernel,
        struct((CELLS, EMBED), bf16),
        [
            window,
            band,
            pltpu.VMEM((SPAN, 144, 2 * NLON), f32),
            pltpu.VMEM((CELLS, WIDE), bf16),
            pltpu.VMEM((WIDE, EMBED), bf16),
            pltpu.SemaphoreType.DMA,
        ],
        16, place, blend_grad, g_left, g_right, g_top, g_bottom, g_left_side, g_right_side,
        g_far, own_e, left_side, right_side, far, in_hbm=(conv_weight,),
    )
    m0, field_grad = lax.optimization_barrier((m[0], field_grad))
    packed = call(pack_kernel, struct((8, 20, EMBED), bf16), [], 4, None, m0, *m[1:], *c)
    parts = lax.all_to_all(packed, ("zlo", "zhi"), split_axis=0, concat_axis=0, tiled=True)
    conv_grad, in_grad, out_grad = call(
        final_kernel,
        (struct((10, EMBED), f32), struct((5, EMBED), f32), struct((5, EMBED), f32)),
        [], 4, None, parts,
    )
    return (
        block_out.reshape(fields.shape),
        field_grad.reshape(fields.shape),
        conv_grad,
        in_grad.T,
        out_grad,
    )


def solution(mesh):
    fine = Mesh(mesh.devices.reshape(4, 2, 4, 4, 2), ("y", "core", "zlo", "x", "zhi"))
    tile_spec = P(("x", "zhi"), LAT, "zlo", None)
    everyone = ("y", "core", "zlo", "x", "zhi")
    return jax.shard_map(
        block,
        mesh=fine,
        in_specs=(
            tile_spec,
            P(LAT + ("zlo",), None, None, None),
            P(LAT + ("zlo",), None, None),
            P(),
            P(),
            P(),
            tile_spec,
        ),
        out_specs=(
            tile_spec,
            tile_spec,
            P(everyone, None),
            P(None, everyone),
            P(everyone, None),
        ),
        check_vma=False,
    )
```

```python
import math

import jax
import jax.numpy as jnp
from jax import lax
from jax.experimental import pallas as pl
from jax.experimental.pallas import tpu as pltpu
from jax.sharding import Mesh, PartitionSpec as P


EMBED = 640
HIDDEN = 1280
BASIS = 4
SPAN = 5
NLON = 64
NLAT = 96
MEMBERS = 8
WIDE = BASIS * EMBED

CYCLES = 12
LON = 16
CELLS = CYCLES * LON
OWNED = 3
HALO = 2
RIM = HALO * LON
CONV_PART = EMBED + BASIS * 384
MLP_PART = 3 * EMBED

half_root = 0.7071067811865476
gauss_norm = 0.3989422804014327


LAT = ("y", "core")
bf16 = jnp.bfloat16
f32 = jnp.float32


def dot(a, b, dims):
    return lax.dot_general(a, b, (dims, ((), ())), preferred_element_type=f32)


def shift(block, axis, count, step):
    return lax.ppermute(block, axis, [(i, (i + step) % count) for i in range(count)])


def struct(shape, dtype):
    return jax.ShapeDtypeStruct(shape, dtype)


def fill_window(win, tile, left, right, top, bottom, left_side, right_side, lat):
    zero = jnp.zeros((LON, EMBED), bf16)

    def put(cycle, group, rows):
        at = (cycle + HALO) * NLON + group * LON
        win[at : at + LON, :] = rows

    for group, (inner, side) in enumerate(
        ((left, left_side), (tile, None), (right, right_side))
    ):
        for row in range(CYCLES):
            put(row, group, inner[row * LON : (row + 1) * LON, :])
        for row in range(HALO):
            upper, lower = (top, bottom) if side is None else (side, side)
            skip = 0 if side is None else RIM
            put(row - HALO, group, upper[row * LON : (row + 1) * LON, :])
            put(row + CYCLES, group, lower[skip + row * LON : skip + (row + 1) * LON, :])
    for row in range(-HALO, CYCLES + HALO):
        put(row, 3, zero)

    def polar(first, skip, missing):
        for row in range(HALO):
            rows = slice(skip + row * LON, skip + (row + 1) * LON)
            put(first + row, 3, left_side[rows, :])
            put(first + HALO + row, 3, right_side[rows, :])
            put(missing + row, 0, zero)
            put(missing + row, 2, zero)

    @pl.when(lat == 0)
    def _():
        polar(0, 0, -HALO)

    @pl.when(lat == 7)
    def _():
        polar(CYCLES - 4, RIM, CYCLES)


def side_kernel(place, left, right, top, bottom, *rest):
    *extra, to_right, to_left = rest
    lat = place[0]
    for to in (to_right, to_left):
        to[0:RIM, :] = top[0:RIM, :]
        to[RIM : 2 * RIM, :] = bottom[0:RIM, :]
        if extra:
            to[2 * RIM :, :] = extra[0][...]

    @pl.when(lat == 0)
    def _():
        to_right[0:RIM, :] = left[0:RIM, :]
        to_left[0:RIM, :] = right[RIM : 2 * RIM, :]

    @pl.when(lat == 7)
    def _():
        to_right[RIM : 2 * RIM, :] = left[CELLS - 2 * RIM : CELLS - RIM, :]
        to_left[RIM : 2 * RIM, :] = right[CELLS - RIM :, :]


def set_rows(coef, at, rows):
    for d in range(SPAN):
        coef[d, at : at + rows.shape[0], :] = rows[:, d * 128 : (d + 1) * 128]


def band_rows(win, band, coef, cycle, row_of):
    low_half = lax.broadcasted_iota(jnp.int32, (LON, 2 * NLON), 1) < NLON
    for k in range(BASIS):
        rolled = []
        for d in range(SPAN):
            row, lane = row_of(d, k)
            values = coef[lane, pl.ds(row, 1), :]
            spread_row = jnp.broadcast_to(values, (LON, 2 * NLON))
            rolled.append(pltpu.roll(spread_row, LON, 1, stride=1, stride_axis=0))
        at = k * LON
        band[at : at + LON, 0:128] = jnp.where(low_half, rolled[0], rolled[1]).astype(bf16)
        band[at : at + LON, 128:256] = jnp.where(low_half, rolled[2], rolled[3]).astype(bf16)
        band[at : at + LON, 256:384] = rolled[4].astype(bf16)
    window = win[cycle * NLON : cycle * NLON + SPAN * NLON, :]
    return dot(band[:, 0 : SPAN * NLON], window, ((1,), (0,)))


def forward_kernel(
    place, tile, left, right, top, bottom, left_side, right_side, far_e, own_e,
    tangent, conv_hbm, in_hbm, out_hbm,
    out, blend_grad, mine, mine_mlp, theirs, theirs_mlp, to_up, to_down,
    win, band, coef, spread, conv_weight, weight_in, weight_out, sems
):
    lat = place[0]
    lon = place[1]
    core = place[2]
    loads = [
        pltpu.make_async_copy(source, target, sems.at[i])
        for i, (source, target) in enumerate(
            ((conv_hbm, conv_weight), (in_hbm, weight_in), (out_hbm, weight_out))
        )
    ]
    for load in loads:
        load.start()
    fill_window(win, tile, left, right, top, bottom, left_side, right_side, lat)
    set_rows(coef, 0, left_side[2 * RIM :, :].astype(f32))
    set_rows(coef, 16, own_e[...].astype(f32))
    set_rows(coef, 32, right_side[2 * RIM :, :].astype(f32))
    set_rows(coef, 48, far_e[...].astype(f32))

    def base(cycle):
        return lax.rem(cycle // OWNED - lon + 1 + 4, 4) * 16 + (cycle % OWNED) * BASIS

    for i in range(CYCLES):
        start = base(i)
        rows = band_rows(win, band.at[i % 2], coef, i, lambda d, k: (start + k, d))
        for k in range(BASIS):
            spread[i * LON : (i + 1) * LON, k * EMBED : (k + 1) * EMBED] = rows[
                k * LON : (k + 1) * LON, :
            ].astype(bf16)

    loads[0].wait()
    blended = (
        tile[...].astype(f32) + dot(spread[...], conv_weight[...], ((1,), (0,)))
    ).astype(bf16)
    loads[1].wait()
    preact = dot(blended, weight_in[...], ((1,), (0,)))
    cdf = 0.5 * (1.0 + lax.erf(preact * half_root))
    hidden = (preact * cdf).astype(bf16)
    loads[2].wait()
    out[...] = (
        blended.astype(f32) + dot(hidden, weight_out[...], ((1,), (0,)))
    ).astype(bf16)
    slope = cdf + preact * jnp.exp(-0.5 * preact * preact) * gauss_norm
    hidden_grad = dot(tangent[...], weight_out[...], ((1,), (1,)))
    preact_grad = (hidden_grad * slope).astype(bf16)
    grad = (
        tangent[...].astype(f32) + dot(preact_grad, weight_in[...], ((1,), (1,)))
    ).astype(bf16)
    blend_grad[...] = grad
    for side in (theirs, mine):
        side[:, 0:EMBED] = grad
    for side in (theirs_mlp, mine_mlp):
        side[:, 0:EMBED] = blended
    for c in range(2):

        def store(side, side_mlp):
            for k in range(BASIS):
                at = k * EMBED + c * 320
                to = EMBED + k * 384
                side[:, to : to + 320] = spread[:, at : at + 320]
                at = k * 320 + c * 160
                to = EMBED + k * 160
                side_mlp[:, to : to + 160] = hidden[:, at : at + 160]
                side_mlp[:, to + EMBED : to + EMBED + 160] = preact_grad[:, at : at + 160]

        @pl.when(core == c)
        def _():
            store(mine, mine_mlp)

        @pl.when(core != c)
        def _():
            store(theirs, theirs_mlp)

    edges = []
    for cycle in (0, 1, CYCLES - 2, CYCLES - 1):
        start = base(cycle)
        for k in range(BASIS):
            edges.append(
                jnp.concatenate([coef[d, pl.ds(start + k, 1), :] for d in range(SPAN)], axis=1)
            )
    to_up[0:RIM, :] = grad[CELLS - RIM :, :]
    to_up[RIM : RIM + 8, :] = jnp.concatenate(edges[8:], axis=0).astype(bf16)
    to_down[0:RIM, :] = grad[:RIM, :]
    to_down[RIM : RIM + 8, :] = jnp.concatenate(edges[:8], axis=0).astype(bf16)


def mlp_grad_kernel(place, mine, other, tangent, other_tangent, order, o0, o1, o2, o3, acc):
    x = place[3]
    sides = []
    for side, cot in ((mine, tangent), (other, other_tangent)):
        hidden = dot(side[:, EMBED : 2 * EMBED], order[...], ((1,), (0,))).astype(bf16)
        grad = dot(side[:, 2 * EMBED : 3 * EMBED], order[...], ((1,), (0,))).astype(bf16)
        sides.append((hidden, grad, side[:, 0:EMBED], cot[...]))
    acc[0:EMBED, :] = dot(sides[0][1], sides[0][2], ((0,), (0,))) + dot(
        sides[1][1], sides[1][2], ((0,), (0,))
    )
    acc[EMBED : 2 * EMBED, :] = dot(sides[0][0], sides[0][3], ((0,), (0,))) + dot(
        sides[1][0], sides[1][3], ((0,), (0,))
    )
    for s, o in enumerate((o0, o1, o2, o3)):
        at = pl.multiple_of(lax.rem(x + s, 4) * 160, 160)
        o[0:160, :] = acc[pl.ds(at, 160), :].astype(o.dtype)
        o[160:320, :] = acc[pl.ds(at + EMBED, 160), :].astype(o.dtype)


def conv_grad_kernel(place, mine, other, o0, o1, o2, o3):
    y = place[4]
    for s, o in enumerate((o0, o1, o2, o3)):
        lanes = pl.ds(pl.multiple_of(lax.rem(y + s, 4) * 384 + EMBED, 128), 384)
        rows = dot(mine[:, lanes], mine[:, 0:EMBED], ((0,), (0,))) + dot(
            other[:, lanes], other[:, 0:EMBED], ((0,), (0,))
        )
        o[...] = rows[0:320, :].astype(o.dtype)


def mlp_sum_kernel(place, r0, r1, r2, r3, o0, o1, o2, o3, acc):
    y = place[4]
    acc[...] = r0[...] + r1[...].astype(f32) + r2[...].astype(f32) + r3[...].astype(f32)
    for s, o in enumerate((o0, o1, o2, o3)):
        at = pl.multiple_of(lax.rem(y + s, 4) * 40, 40)
        o[0:40, :] = acc[pl.ds(at, 40), :].astype(o.dtype)
        o[40:80, :] = acc[pl.ds(at + 160, 40), :].astype(o.dtype)


def conv_sum_kernel(place, r0, r1, r2, r3, o0, o1, o2, o3, acc):
    x = place[3]
    total = r0[...] + r1[...].astype(f32) + r2[...].astype(f32) + r3[...].astype(f32)
    for lon in range(4):
        for to in range(4):
            at = lon * 80 + to * 20
            acc[to * 80 + lon * 20 : to * 80 + lon * 20 + 20, :] = total[at : at + 20, :]
    for s, o in enumerate((o0, o1, o2, o3)):
        at = pl.multiple_of(lax.rem(x + s, 4) * 80, 80)
        o[...] = acc[pl.ds(at, 80), :].astype(o.dtype)


def pack_kernel(m0, m1, m2, m3, c0, c1, c2, c3, o):
    mlp = m0[...] + m1[...].astype(f32) + m2[...].astype(f32) + m3[...].astype(f32)
    conv = c0[...] + c1[...].astype(f32) + c2[...].astype(f32) + c3[...].astype(f32)
    for to in range(8):
        o[to, 0:10, :] = conv[to * 10 : to * 10 + 10, :].astype(bf16)
        o[to, 10:15, :] = mlp[to * 5 : to * 5 + 5, :].astype(bf16)
        o[to, 15:20, :] = mlp[40 + to * 5 : 45 + to * 5, :].astype(bf16)


def final_kernel(parts, conv, w_in, w_out):
    total = parts[0].astype(f32)
    for i in range(1, 8):
        total = total + parts[i].astype(f32)
    total = total * (1.0 / math.sqrt(MEMBERS * NLAT * NLON))
    conv[...] = total[0:10, :]
    w_in[...] = total[10:15, :]
    w_out[...] = total[15:20, :]


def field_grad_kernel(
    place, tile, left, right, top, bottom, left_side, right_side,
    own_e, left_e, right_e, far_e, conv_hbm, field_grad, win, band, coef, mixed,
    conv_weight, sem
):
    lat = place[0]
    lon = place[1]
    load = pltpu.make_async_copy(conv_hbm, conv_weight, sem)
    load.start()
    fill_window(win, tile, left, right, top, bottom, left_side, right_side, lat)
    rows = jnp.concatenate(
        [
            left_e[2 * RIM :, :], own_e[...], right_e[2 * RIM :, :], far_e[...],
            top[RIM:, :], bottom[RIM:, :],
        ],
        axis=0,
    )
    lane = lax.broadcasted_iota(jnp.int32, (2 * NLON, 2 * NLON), 0)
    to = lax.broadcasted_iota(jnp.int32, (2 * NLON, 2 * NLON), 1)
    flip = (lax.rem(lane + to, 2 * NLON) == 0).astype(f32).astype(bf16)
    for d in range(SPAN):
        coef[d, :, :] = dot(rows[:, d * 128 : (d + 1) * 128], flip, ((1,), (0,)))

    def base(cycle):
        if cycle < 0:
            return 64 + (cycle + HALO) * BASIS
        if cycle >= CYCLES:
            return 72 + (cycle - CYCLES) * BASIS
        return lax.rem(cycle // OWNED - lon + 1 + 4, 4) * 16 + (cycle % OWNED) * BASIS

    for j in range(CYCLES):
        starts = [base(j + e - HALO) for e in range(SPAN)]
        rows = band_rows(
            win, band.at[j % 2], coef, j, lambda e, k: (starts[e] + k, SPAN - 1 - e)
        )
        for k in range(BASIS):
            mixed[j * LON : (j + 1) * LON, k * EMBED : (k + 1) * EMBED] = rows[
                k * LON : (k + 1) * LON, :
            ].astype(bf16)
    total = tile[...].astype(f32)
    load.wait()
    for k in range(BASIS):
        total = total + dot(
            mixed[:, k * EMBED : (k + 1) * EMBED],
            conv_weight[k * EMBED : (k + 1) * EMBED, :],
            ((1,), (1,)),
        )
    field_grad[...] = total.astype(bf16)


def call(kernel, outs, scratch, mib, place, *args, in_hbm=()):
    vmem, hbm = pl.BlockSpec(memory_space=pltpu.VMEM), pl.BlockSpec(memory_space=pltpu.HBM)
    in_specs = [vmem] * len(args) + [hbm] * len(in_hbm)
    args = args + tuple(pltpu.with_memory_space_constraint(a, pltpu.HBM) for a in in_hbm)
    if place is not None:
        in_specs = [pl.BlockSpec(memory_space=pltpu.SMEM)] + in_specs
        args = (place,) + args
    return pl.pallas_call(
        kernel,
        out_shape=outs,
        in_specs=in_specs,
        scratch_shapes=scratch,
        compiler_params=pltpu.CompilerParams(vmem_limit_bytes=mib * 1024 * 1024),
    )(*args)


def neighbours(tile, to_up, to_down):
    forward = [(i, i + 1) for i in range(7)]
    backward = [(i + 1, i) for i in range(7)]
    left = shift(tile, "zlo", 4, 1)
    right = shift(tile, "zlo", 4, 3)
    top = lax.ppermute(to_up, LAT, forward)
    bottom = lax.ppermute(to_down, LAT, backward)
    return left, right, top, bottom


def relay(place, left, right, top, bottom, *extra):
    rows = 2 * RIM + sum(e.shape[0] for e in extra)
    to_right, to_left = call(
        side_kernel, (struct((rows, EMBED), bf16),) * 2, [], 4, place,
        left, right, top, bottom, *extra,
    )
    left_side = shift(to_right, "zlo", 4, 1)
    right_side = shift(to_left, "zlo", 4, 3)
    return left_side, right_side


def spread_out(chunks, axis):
    parts = [chunks[0]]
    for s in (1, 2, 3):
        parts.append(shift(chunks[s], axis, 4, s))
    return tuple(parts)


def coefficients(filter_basis, lon_offsets):
    lanes = jnp.arange(2 * NLON, dtype=jnp.int32) % NLON
    values = filter_basis.astype(f32).transpose(0, 2, 1, 3)
    hit = lanes[None, None, None, :] == (lon_offsets % NLON)[:, :, :, None]
    kept = jnp.where(hit[:, None], values[..., None], 0.0)
    rows = kept.sum(axis=3).astype(bf16).reshape(OWNED * BASIS, SPAN * 2 * NLON)
    return jnp.pad(rows, ((0, 16 - OWNED * BASIS), (0, 0)))


def block(fields, filter_basis, lon_offsets, conv_weight, weight_in, weight_out, cotangent):
    y = lax.axis_index("y")
    core = lax.axis_index("core")
    lon = lax.axis_index("zlo")
    x = lax.axis_index("x")
    lat = 2 * y + core
    place = jnp.stack([lat, lon, core, x, y]).astype(jnp.int32)
    tile = fields.reshape(CELLS, EMBED)
    tangent = cotangent.reshape(CELLS, EMBED)

    left, right, top, bottom = neighbours(tile, tile[CELLS - RIM :], tile[:RIM])
    own_e = coefficients(filter_basis, lon_offsets)
    far_e = shift(own_e, "zlo", 4, 2)
    left_side, right_side = relay(place, left, right, top, bottom, own_e)
    other_tangent = shift(tangent, "core", 2, 1)

    unit = jnp.arange(EMBED, dtype=jnp.int32)
    ux, uy, ul, ur = unit // 160, unit // 40 % 4, unit // 10 % 4, unit % 10
    source = uy * 160 + ul * 40 + ux * 10 + ur
    order = (unit[:, None] == source[None, :]).astype(bf16)

    far_e, other_tangent, order = lax.optimization_barrier((far_e, other_tangent, order))
    window = pltpu.VMEM(((CYCLES + 2 * HALO) * NLON, EMBED), bf16)
    band = pltpu.VMEM((2, BASIS * LON, 384), bf16)
    edge = struct((RIM + 8, EMBED), bf16)
    parts = (struct((CELLS, CONV_PART), bf16), struct((CELLS, MLP_PART), bf16))
    block_out, blend_grad, mine, mine_mlp, theirs, theirs_mlp, to_up, to_down = call(
        forward_kernel,
        (struct((CELLS, EMBED), bf16), struct((CELLS, EMBED), bf16))
        + parts
        + parts
        + (edge, edge),
        [
            window,
            band,
            pltpu.VMEM((SPAN, 64, 2 * NLON), f32),
            pltpu.VMEM((CELLS, WIDE), bf16),
            pltpu.VMEM((WIDE, EMBED), bf16),
            pltpu.VMEM((EMBED, HIDDEN), bf16),
            pltpu.VMEM((HIDDEN, EMBED), bf16),
            pltpu.SemaphoreType.DMA((3,)),
        ],
        24, place, tile, left, right, top, bottom, left_side, right_side, far_e, own_e,
        tangent, in_hbm=(conv_weight, weight_in, weight_out),
    )
    other = shift(theirs, "core", 2, 1)
    other_mlp = shift(theirs_mlp, "core", 2, 1)
    g_left, g_right, g_top, g_bottom = neighbours(blend_grad, to_up, to_down)

    chunk = (struct((320, EMBED), f32),) + (struct((320, EMBED), bf16),) * 3
    c = call(conv_grad_kernel, chunk, [], 16, place, mine, other)
    c = spread_out(c, "y")
    m = call(
        mlp_grad_kernel, chunk, [pltpu.VMEM((2 * EMBED, EMBED), f32)],
        16, place, mine_mlp, other_mlp, tangent, other_tangent, order,
    )
    m = spread_out(m, "x")

    g_left_side, g_right_side = relay(place, g_left, g_right, g_top, g_bottom)
    piece = (struct((80, EMBED), f32),) + (struct((80, EMBED), bf16),) * 3
    total = pltpu.VMEM((320, EMBED), f32)
    c = call(conv_sum_kernel, piece, [total], 8, place, *c)
    c = spread_out(c, "x")
    m = call(mlp_sum_kernel, piece, [total], 8, place, *m)
    m = spread_out(m, "y")
    field_grad = call(
        field_grad_kernel,
        struct((CELLS, EMBED), bf16),
        [
            window,
            band,
            pltpu.VMEM((SPAN, 80, 2 * NLON), f32),
            pltpu.VMEM((CELLS, WIDE), bf16),
            pltpu.VMEM((WIDE, EMBED), bf16),
            pltpu.SemaphoreType.DMA,
        ],
        16, place, blend_grad, g_left, g_right, g_top, g_bottom, g_left_side, g_right_side,
        own_e, left_side, right_side, far_e, in_hbm=(conv_weight,),
    )
    m0, field_grad = lax.optimization_barrier((m[0], field_grad))
    packed = call(pack_kernel, struct((8, 20, EMBED), bf16), [], 4, None, m0, *m[1:], *c)
    parts = lax.all_to_all(packed, ("zlo", "zhi"), split_axis=0, concat_axis=0, tiled=True)
    conv_grad, in_grad, out_grad = call(
        final_kernel,
        (struct((10, EMBED), f32), struct((5, EMBED), f32), struct((5, EMBED), f32)),
        [], 4, None, parts,
    )
    return (
        block_out.reshape(fields.shape),
        field_grad.reshape(fields.shape),
        conv_grad,
        in_grad.T,
        out_grad,
    )


def solution(mesh):
    fine = Mesh(mesh.devices.reshape(4, 2, 4, 4, 2), ("y", "core", "zlo", "x", "zhi"))
    tile_spec = P(("x", "zhi"), LAT, "zlo", None)
    everyone = ("y", "core", "zlo", "x", "zhi")
    return jax.shard_map(
        block,
        mesh=fine,
        in_specs=(
            tile_spec,
            P(LAT + ("zlo",), None, None, None),
            P(LAT + ("zlo",), None, None),
            P(),
            P(),
            P(),
            tile_spec,
        ),
        out_specs=(
            tile_spec,
            tile_spec,
            P(everyone, None),
            P(None, everyone),
            P(everyone, None),
        ),
        check_vma=False,
    )
```

```python
import math

import jax
import jax.numpy as jnp
from jax import lax
from jax.experimental import pallas as pl
from jax.experimental.pallas import tpu as pltpu
from jax.sharding import Mesh, PartitionSpec as P


EMBED = 640
HIDDEN = 1280
BASIS = 4
SPAN = 5
NLON = 64
NLAT = 96
MEMBERS = 8
WIDE = BASIS * EMBED

CYCLES = 12
LON = 16
CELLS = CYCLES * LON
OWNED = 3
HALO = 2
RIM = HALO * LON
CONV_PART = EMBED + BASIS * 384
MLP_PART = 3 * EMBED

half_root = 0.7071067811865476
gauss_norm = 0.3989422804014327


LAT = ("y", "core")
bf16 = jnp.bfloat16
f32 = jnp.float32


def dot(a, b, dims):
    return lax.dot_general(a, b, (dims, ((), ())), preferred_element_type=f32)


def shift(block, axis, count, step):
    return lax.ppermute(block, axis, [(i, (i + step) % count) for i in range(count)])


def struct(shape, dtype):
    return jax.ShapeDtypeStruct(shape, dtype)


def fill_window(win, tile, left, right, top, bottom, left_side, right_side, lat):
    zero = jnp.zeros((LON, EMBED), bf16)

    def put(cycle, group, rows):
        at = (cycle + HALO) * NLON + group * LON
        win[at : at + LON, :] = rows

    for group, (inner, side) in enumerate(
        ((left, left_side), (tile, None), (right, right_side))
    ):
        for row in range(CYCLES):
            put(row, group, inner[row * LON : (row + 1) * LON, :])
        for row in range(HALO):
            upper, lower = (top, bottom) if side is None else (side, side)
            skip = 0 if side is None else RIM
            put(row - HALO, group, upper[row * LON : (row + 1) * LON, :])
            put(row + CYCLES, group, lower[skip + row * LON : skip + (row + 1) * LON, :])
    for row in range(-HALO, CYCLES + HALO):
        put(row, 3, zero)

    def polar(first, skip, missing):
        for row in range(HALO):
            rows = slice(skip + row * LON, skip + (row + 1) * LON)
            put(first + row, 3, left_side[rows, :])
            put(first + HALO + row, 3, right_side[rows, :])
            put(missing + row, 0, zero)
            put(missing + row, 2, zero)

    @pl.when(lat == 0)
    def _():
        polar(0, 0, -HALO)

    @pl.when(lat == 7)
    def _():
        polar(CYCLES - 4, RIM, CYCLES)


def side_kernel(place, left, right, top, bottom, to_right, to_left):
    lat = place[0]
    for to in (to_right, to_left):
        to[0:RIM, :] = top[0:RIM, :]
        to[RIM : 2 * RIM, :] = bottom[0:RIM, :]

    @pl.when(lat == 0)
    def _():
        to_right[0:RIM, :] = left[0:RIM, :]
        to_left[0:RIM, :] = right[RIM : 2 * RIM, :]

    @pl.when(lat == 7)
    def _():
        to_right[RIM : 2 * RIM, :] = left[CELLS - 2 * RIM : CELLS - RIM, :]
        to_left[RIM : 2 * RIM, :] = right[CELLS - RIM :, :]


def set_rows(coef, at, rows):
    for d in range(SPAN):
        coef[d, at : at + rows.shape[0], :] = rows[:, d * 128 : (d + 1) * 128]


def fill_band(band, coef, row_of):
    low_half = lax.broadcasted_iota(jnp.int32, (LON, 2 * NLON), 1) < NLON
    for k in range(BASIS):
        rolled = []
        for d in range(SPAN):
            row, lane = row_of(d, k)
            values = jnp.broadcast_to(coef[lane, pl.ds(row, 1), :], (LON, 2 * NLON))
            rolled.append(pltpu.roll(values, LON, 1, stride=1, stride_axis=0))
        at = k * LON
        band[at : at + LON, 0:128] = jnp.where(low_half, rolled[0], rolled[1]).astype(bf16)
        band[at : at + LON, 128:256] = jnp.where(low_half, rolled[2], rolled[3]).astype(bf16)
        band[at : at + LON, 256:384] = rolled[4].astype(bf16)


def apply_band(band, win, cycle, out):
    window = win[cycle * NLON : cycle * NLON + SPAN * NLON, :]
    rows = dot(band[:, 0 : SPAN * NLON], window, ((1,), (0,)))
    for k in range(BASIS):
        out[cycle * LON : (cycle + 1) * LON, k * EMBED : (k + 1) * EMBED] = rows[
            k * LON : (k + 1) * LON, :
        ].astype(bf16)


def first_row(cycle, lon):
    return lax.rem(cycle // OWNED - lon + 1 + 4, 4) * 16 + (cycle % OWNED) * BASIS


def band_kernel(
    place, left_e, own_e, right_e, far_e, tangent, out_hbm,
    bands, hidden_grad, edge_down, edge_up, coef, weight_out, sem
):
    lon = place[1]
    load = pltpu.make_async_copy(out_hbm, weight_out, sem)
    load.start()
    for group, e in enumerate((left_e, own_e, right_e, far_e)):
        set_rows(coef, group * 16, e[...].astype(f32))
    for i in range(CYCLES):
        start = first_row(i, lon)
        fill_band(
            bands.at[i * BASIS * LON : (i + 1) * BASIS * LON], coef, lambda d, k: (start + k, d)
        )
    for edge, first in ((edge_down, 0), (edge_up, CYCLES - HALO)):
        rows = []
        for cycle in range(first, first + HALO):
            start = first_row(cycle, lon)
            for k in range(BASIS):
                rows.append(
                    jnp.concatenate([coef[d, pl.ds(start + k, 1), :] for d in range(SPAN)], axis=1)
                )
        edge[...] = jnp.concatenate(rows, axis=0).astype(bf16)
    load.wait()
    hidden_grad[...] = dot(tangent[...], weight_out[...], ((1,), (1,)))


def forward_kernel(
    place, tile, left, right, top, bottom, left_side, right_side, bands, hidden_grad,
    edge_down, edge_up, tangent, conv_hbm, in_hbm, out_hbm,
    out, blend_grad, mine, mine_mlp, theirs, theirs_mlp, to_up, to_down,
    win, spread, conv_weight, weight_in, weight_out, sems
):
    lat = place[0]
    core = place[2]
    loads = [
        pltpu.make_async_copy(source, target, sems.at[i])
        for i, (source, target) in enumerate(
            ((conv_hbm, conv_weight), (in_hbm, weight_in), (out_hbm, weight_out))
        )
    ]
    for load in loads:
        load.start()
    fill_window(win, tile, left, right, top, bottom, left_side, right_side, lat)
    for i in range(CYCLES):
        apply_band(bands.at[i * BASIS * LON : (i + 1) * BASIS * LON], win, i, spread)

    loads[0].wait()
    blended = (
        tile[...].astype(f32) + dot(spread[...], conv_weight[...], ((1,), (0,)))
    ).astype(bf16)
    loads[1].wait()
    preact = dot(blended, weight_in[...], ((1,), (0,)))
    cdf = 0.5 * (1.0 + lax.erf(preact * half_root))
    hidden = (preact * cdf).astype(bf16)
    loads[2].wait()
    out[...] = (
        blended.astype(f32) + dot(hidden, weight_out[...], ((1,), (0,)))
    ).astype(bf16)
    slope = cdf + preact * jnp.exp(-0.5 * preact * preact) * gauss_norm
    preact_grad = (hidden_grad[...] * slope).astype(bf16)
    grad = (
        tangent[...].astype(f32) + dot(preact_grad, weight_in[...], ((1,), (1,)))
    ).astype(bf16)
    blend_grad[...] = grad
    for side in (theirs, mine):
        side[:, 0:EMBED] = grad
    for side in (theirs_mlp, mine_mlp):
        side[:, 0:EMBED] = blended
    for c in range(2):

        def store(side, side_mlp):
            for k in range(BASIS):
                at = k * EMBED + c * 320
                to = EMBED + k * 384
                side[:, to : to + 320] = spread[:, at : at + 320]
                at = k * 320 + c * 160
                to = EMBED + k * 160
                side_mlp[:, to : to + 160] = hidden[:, at : at + 160]
                side_mlp[:, to + EMBED : to + EMBED + 160] = preact_grad[:, at : at + 160]

        @pl.when(core == c)
        def _():
            store(mine, mine_mlp)

        @pl.when(core != c)
        def _():
            store(theirs, theirs_mlp)

    to_up[0:RIM, :] = grad[CELLS - RIM :, :]
    to_up[RIM:, :] = edge_up[...]
    to_down[0:RIM, :] = grad[:RIM, :]
    to_down[RIM:, :] = edge_down[...]


def mlp_grad_kernel(place, mine, other, tangent, other_tangent, order, o0, o1, o2, o3, acc):
    x = place[3]
    sides = []
    for side, cot in ((mine, tangent), (other, other_tangent)):
        hidden = dot(side[:, EMBED : 2 * EMBED], order[...], ((1,), (0,))).astype(bf16)
        grad = dot(side[:, 2 * EMBED : 3 * EMBED], order[...], ((1,), (0,))).astype(bf16)
        sides.append((hidden, grad, side[:, 0:EMBED], cot[...]))
    acc[0:EMBED, :] = dot(sides[0][1], sides[0][2], ((0,), (0,))) + dot(
        sides[1][1], sides[1][2], ((0,), (0,))
    )
    acc[EMBED : 2 * EMBED, :] = dot(sides[0][0], sides[0][3], ((0,), (0,))) + dot(
        sides[1][0], sides[1][3], ((0,), (0,))
    )
    for s, o in enumerate((o0, o1, o2, o3)):
        at = pl.multiple_of(lax.rem(x + s, 4) * 160, 160)
        o[0:160, :] = acc[pl.ds(at, 160), :].astype(o.dtype)
        o[160:320, :] = acc[pl.ds(at + EMBED, 160), :].astype(o.dtype)


def conv_grad_kernel(place, mine, other, o0, o1, o2, o3):
    y = place[4]
    for s, o in enumerate((o0, o1, o2, o3)):
        lanes = pl.ds(pl.multiple_of(lax.rem(y + s, 4) * 384 + EMBED, 128), 384)
        rows = dot(mine[:, lanes], mine[:, 0:EMBED], ((0,), (0,))) + dot(
            other[:, lanes], other[:, 0:EMBED], ((0,), (0,))
        )
        o[...] = rows[0:320, :].astype(o.dtype)


def mlp_sum_kernel(place, r0, r1, r2, r3, o0, o1, o2, o3, acc):
    y = place[4]
    acc[...] = r0[...] + r1[...].astype(f32) + r2[...].astype(f32) + r3[...].astype(f32)
    for s, o in enumerate((o0, o1, o2, o3)):
        at = pl.multiple_of(lax.rem(y + s, 4) * 40, 40)
        o[0:40, :] = acc[pl.ds(at, 40), :].astype(o.dtype)
        o[40:80, :] = acc[pl.ds(at + 160, 40), :].astype(o.dtype)


def conv_sum_kernel(place, r0, r1, r2, r3, o0, o1, o2, o3, acc):
    x = place[3]
    total = r0[...] + r1[...].astype(f32) + r2[...].astype(f32) + r3[...].astype(f32)
    for lon in range(4):
        for to in range(4):
            at = lon * 80 + to * 20
            acc[to * 80 + lon * 20 : to * 80 + lon * 20 + 20, :] = total[at : at + 20, :]
    for s, o in enumerate((o0, o1, o2, o3)):
        at = pl.multiple_of(lax.rem(x + s, 4) * 80, 80)
        o[...] = acc[pl.ds(at, 80), :].astype(o.dtype)


def pack_kernel(m0, m1, m2, m3, c0, c1, c2, c3, o):
    mlp = m0[...] + m1[...].astype(f32) + m2[...].astype(f32) + m3[...].astype(f32)
    conv = c0[...] + c1[...].astype(f32) + c2[...].astype(f32) + c3[...].astype(f32)
    for to in range(8):
        o[to, 0:10, :] = conv[to * 10 : to * 10 + 10, :].astype(bf16)
        o[to, 10:15, :] = mlp[to * 5 : to * 5 + 5, :].astype(bf16)
        o[to, 15:20, :] = mlp[40 + to * 5 : 45 + to * 5, :].astype(bf16)


def final_kernel(parts, conv, w_in, w_out):
    total = parts[0].astype(f32)
    for i in range(1, 8):
        total = total + parts[i].astype(f32)
    total = total * (1.0 / math.sqrt(MEMBERS * NLAT * NLON))
    conv[...] = total[0:10, :]
    w_in[...] = total[10:15, :]
    w_out[...] = total[15:20, :]


def field_grad_kernel(
    place, tile, left, right, top, bottom, left_side, right_side,
    own_e, left_e, right_e, far_e, conv_hbm, field_grad, win, band, coef, mixed,
    conv_weight, sem
):
    lat = place[0]
    lon = place[1]
    load = pltpu.make_async_copy(conv_hbm, conv_weight, sem)
    load.start()
    fill_window(win, tile, left, right, top, bottom, left_side, right_side, lat)
    rows = jnp.concatenate(
        [left_e[...], own_e[...], right_e[...], far_e[...], top[RIM:, :], bottom[RIM:, :]],
        axis=0,
    )
    lane = lax.broadcasted_iota(jnp.int32, (2 * NLON, 2 * NLON), 0)
    to = lax.broadcasted_iota(jnp.int32, (2 * NLON, 2 * NLON), 1)
    flip = (lax.rem(lane + to, 2 * NLON) == 0).astype(f32).astype(bf16)
    for d in range(SPAN):
        coef[d, :, :] = dot(rows[:, d * 128 : (d + 1) * 128], flip, ((1,), (0,)))

    def base(cycle):
        if cycle < 0:
            return 64 + (cycle + HALO) * BASIS
        if cycle >= CYCLES:
            return 72 + (cycle - CYCLES) * BASIS
        return first_row(cycle, lon)

    for j in range(CYCLES):
        starts = [base(j + e - HALO) for e in range(SPAN)]
        fill_band(band.at[j % 2], coef, lambda e, k: (starts[e] + k, SPAN - 1 - e))
        apply_band(band.at[j % 2], win, j, mixed)
    total = tile[...].astype(f32)
    load.wait()
    for k in range(BASIS):
        total = total + dot(
            mixed[:, k * EMBED : (k + 1) * EMBED],
            conv_weight[k * EMBED : (k + 1) * EMBED, :],
            ((1,), (1,)),
        )
    field_grad[...] = total.astype(bf16)


def call(kernel, outs, scratch, mib, place, *args, in_hbm=()):
    vmem, hbm = pl.BlockSpec(memory_space=pltpu.VMEM), pl.BlockSpec(memory_space=pltpu.HBM)
    in_specs = [vmem] * len(args) + [hbm] * len(in_hbm)
    args = args + tuple(pltpu.with_memory_space_constraint(a, pltpu.HBM) for a in in_hbm)
    if place is not None:
        in_specs = [pl.BlockSpec(memory_space=pltpu.SMEM)] + in_specs
        args = (place,) + args
    return pl.pallas_call(
        kernel,
        out_shape=outs,
        in_specs=in_specs,
        scratch_shapes=scratch,
        compiler_params=pltpu.CompilerParams(vmem_limit_bytes=mib * 1024 * 1024),
    )(*args)


def neighbours(tile, to_up, to_down):
    forward = [(i, i + 1) for i in range(7)]
    backward = [(i + 1, i) for i in range(7)]
    left = shift(tile, "zlo", 4, 1)
    right = shift(tile, "zlo", 4, 3)
    top = lax.ppermute(to_up, LAT, forward)
    bottom = lax.ppermute(to_down, LAT, backward)
    return left, right, top, bottom


def relay(place, left, right, top, bottom):
    to_right, to_left = call(
        side_kernel, (struct((2 * RIM, EMBED), bf16),) * 2, [], 4, place,
        left, right, top, bottom,
    )
    left_side = shift(to_right, "zlo", 4, 1)
    right_side = shift(to_left, "zlo", 4, 3)
    return left_side, right_side


def spread_out(chunks, axis):
    parts = [chunks[0]]
    for s in (1, 2, 3):
        parts.append(shift(chunks[s], axis, 4, s))
    return tuple(parts)


def coefficients(filter_basis, lon_offsets):
    lanes = jnp.arange(2 * NLON, dtype=jnp.int32) % NLON
    values = filter_basis.astype(f32).transpose(0, 2, 1, 3)
    hit = lanes[None, None, None, :] == (lon_offsets % NLON)[:, :, :, None]
    kept = jnp.where(hit[:, None], values[..., None], 0.0)
    rows = kept.sum(axis=3).astype(bf16).reshape(OWNED * BASIS, SPAN * 2 * NLON)
    return jnp.pad(rows, ((0, 16 - OWNED * BASIS), (0, 0)))


def block(fields, filter_basis, lon_offsets, conv_weight, weight_in, weight_out, cotangent):
    y = lax.axis_index("y")
    core = lax.axis_index("core")
    lon = lax.axis_index("zlo")
    x = lax.axis_index("x")
    lat = 2 * y + core
    place = jnp.stack([lat, lon, core, x, y]).astype(jnp.int32)
    tile = fields.reshape(CELLS, EMBED)
    tangent = cotangent.reshape(CELLS, EMBED)

    left, right, top, bottom = neighbours(tile, tile[CELLS - RIM :], tile[:RIM])
    own_e = coefficients(filter_basis, lon_offsets)
    left_e = shift(own_e, "zlo", 4, 1)
    right_e = shift(own_e, "zlo", 4, 3)
    far_e = shift(own_e, "zlo", 4, 2)
    left_side, right_side = relay(place, left, right, top, bottom)
    other_tangent = shift(tangent, "core", 2, 1)

    unit = jnp.arange(EMBED, dtype=jnp.int32)
    ux, uy, ul, ur = unit // 160, unit // 40 % 4, unit // 10 % 4, unit % 10
    source = uy * 160 + ul * 40 + ux * 10 + ur
    order = (unit[:, None] == source[None, :]).astype(bf16)

    window = pltpu.VMEM(((CYCLES + 2 * HALO) * NLON, EMBED), bf16)
    edge = struct((8, EMBED), bf16)
    bands, hidden_grad, edge_down, edge_up = call(
        band_kernel,
        (struct((CELLS * BASIS, 384), bf16), struct((CELLS, HIDDEN), f32), edge, edge),
        [
            pltpu.VMEM((SPAN, 64, 2 * NLON), f32),
            pltpu.VMEM((HIDDEN, EMBED), bf16),
            pltpu.SemaphoreType.DMA,
        ],
        12, place, left_e, own_e, right_e, far_e, tangent, in_hbm=(weight_out,),
    )
    bands, other_tangent, order = lax.optimization_barrier((bands, other_tangent, order))
    edge_rows = struct((RIM + 8, EMBED), bf16)
    parts = (struct((CELLS, CONV_PART), bf16), struct((CELLS, MLP_PART), bf16))
    block_out, blend_grad, mine, mine_mlp, theirs, theirs_mlp, to_up, to_down = call(
        forward_kernel,
        (struct((CELLS, EMBED), bf16), struct((CELLS, EMBED), bf16))
        + parts
        + parts
        + (edge_rows, edge_rows),
        [
            window,
            pltpu.VMEM((CELLS, WIDE), bf16),
            pltpu.VMEM((WIDE, EMBED), bf16),
            pltpu.VMEM((EMBED, HIDDEN), bf16),
            pltpu.VMEM((HIDDEN, EMBED), bf16),
            pltpu.SemaphoreType.DMA((3,)),
        ],
        24, place, tile, left, right, top, bottom, left_side, right_side, bands,
        hidden_grad, edge_down, edge_up, tangent, in_hbm=(conv_weight, weight_in, weight_out),
    )
    other = shift(theirs, "core", 2, 1)
    other_mlp = shift(theirs_mlp, "core", 2, 1)
    g_left, g_right, g_top, g_bottom = neighbours(blend_grad, to_up, to_down)

    chunk = (struct((320, EMBED), f32),) + (struct((320, EMBED), bf16),) * 3
    c = call(conv_grad_kernel, chunk, [], 16, place, mine, other)
    c = spread_out(c, "y")
    m = call(
        mlp_grad_kernel, chunk, [pltpu.VMEM((2 * EMBED, EMBED), f32)],
        16, place, mine_mlp, other_mlp, tangent, other_tangent, order,
    )
    m = spread_out(m, "x")

    g_left_side, g_right_side = relay(place, g_left, g_right, g_top, g_bottom)
    piece = (struct((80, EMBED), f32),) + (struct((80, EMBED), bf16),) * 3
    total = pltpu.VMEM((320, EMBED), f32)
    c = call(conv_sum_kernel, piece, [total], 8, place, *c)
    c = spread_out(c, "x")
    m = call(mlp_sum_kernel, piece, [total], 8, place, *m)
    m = spread_out(m, "y")
    field_grad = call(
        field_grad_kernel,
        struct((CELLS, EMBED), bf16),
        [
            window,
            pltpu.VMEM((2, BASIS * LON, 384), bf16),
            pltpu.VMEM((SPAN, 80, 2 * NLON), f32),
            pltpu.VMEM((CELLS, WIDE), bf16),
            pltpu.VMEM((WIDE, EMBED), bf16),
            pltpu.SemaphoreType.DMA,
        ],
        16, place, blend_grad, g_left, g_right, g_top, g_bottom, g_left_side, g_right_side,
        own_e, left_e, right_e, far_e, in_hbm=(conv_weight,),
    )
    m0, field_grad = lax.optimization_barrier((m[0], field_grad))
    packed = call(pack_kernel, struct((8, 20, EMBED), bf16), [], 4, None, m0, *m[1:], *c)
    parts = lax.all_to_all(packed, ("zlo", "zhi"), split_axis=0, concat_axis=0, tiled=True)
    conv_grad, in_grad, out_grad = call(
        final_kernel,
        (struct((10, EMBED), f32), struct((5, EMBED), f32), struct((5, EMBED), f32)),
        [], 4, None, parts,
    )
    return (
        block_out.reshape(fields.shape),
        field_grad.reshape(fields.shape),
        conv_grad,
        in_grad.T,
        out_grad,
    )


def solution(mesh):
    fine = Mesh(mesh.devices.reshape(4, 2, 4, 4, 2), ("y", "core", "zlo", "x", "zhi"))
    tile_spec = P(("x", "zhi"), LAT, "zlo", None)
    everyone = ("y", "core", "zlo", "x", "zhi")
    return jax.shard_map(
        block,
        mesh=fine,
        in_specs=(
            tile_spec,
            P(LAT + ("zlo",), None, None, None),
            P(LAT + ("zlo",), None, None),
            P(),
            P(),
            P(),
            tile_spec,
        ),
        out_specs=(
            tile_spec,
            tile_spec,
            P(everyone, None),
            P(None, everyone),
            P(everyone, None),
        ),
        check_vma=False,
    )
```

```python
import math

import jax
import jax.numpy as jnp
from jax import lax
from jax.experimental import pallas as pl
from jax.experimental.pallas import tpu as pltpu
from jax.sharding import Mesh, PartitionSpec as P


EMBED = 640
HIDDEN = 1280
BASIS = 4
SPAN = 5
NLON = 64
NLAT = 96
MEMBERS = 8
WIDE = BASIS * EMBED

CYCLES = 12
LON = 16
CELLS = CYCLES * LON
OWNED = 3
HALO = 2
RIM = HALO * LON
CONV_PART = EMBED + BASIS * 384
MLP_PART = 3 * EMBED

half_root = 0.7071067811865476
gauss_norm = 0.3989422804014327


LAT = ("y", "core")
bf16 = jnp.bfloat16
f32 = jnp.float32


def dot(a, b, dims):
    return lax.dot_general(a, b, (dims, ((), ())), preferred_element_type=f32)


def shift(block, axis, count, step):
    return lax.ppermute(block, axis, [(i, (i + step) % count) for i in range(count)])


def struct(shape, dtype):
    return jax.ShapeDtypeStruct(shape, dtype)


def fill_window(win, tile, left, right, top, bottom, left_side, right_side, lat):
    zero = jnp.zeros((LON, EMBED), bf16)

    def put(cycle, group, rows):
        at = (cycle + HALO) * NLON + group * LON
        win[at : at + LON, :] = rows

    for group, (inner, side) in enumerate(
        ((left, left_side), (tile, None), (right, right_side))
    ):
        for row in range(CYCLES):
            put(row, group, inner[row * LON : (row + 1) * LON, :])
        for row in range(HALO):
            upper, lower = (top, bottom) if side is None else (side, side)
            skip = 0 if side is None else RIM
            put(row - HALO, group, upper[row * LON : (row + 1) * LON, :])
            put(row + CYCLES, group, lower[skip + row * LON : skip + (row + 1) * LON, :])
    for row in range(-HALO, CYCLES + HALO):
        put(row, 3, zero)

    def polar(first, skip, missing):
        for row in range(HALO):
            rows = slice(skip + row * LON, skip + (row + 1) * LON)
            put(first + row, 3, left_side[rows, :])
            put(first + HALO + row, 3, right_side[rows, :])
            put(missing + row, 0, zero)
            put(missing + row, 2, zero)

    @pl.when(lat == 0)
    def _():
        polar(0, 0, -HALO)

    @pl.when(lat == 7)
    def _():
        polar(CYCLES - 4, RIM, CYCLES)


def side_kernel(place, left, right, top, bottom, *rest):
    *extra, to_right, to_left = rest
    lat = place[0]
    for to in (to_right, to_left):
        to[0:RIM, :] = top[0:RIM, :]
        to[RIM : 2 * RIM, :] = bottom[0:RIM, :]
        if extra:
            to[2 * RIM :, :] = extra[0][...]

    @pl.when(lat == 0)
    def _():
        to_right[0:RIM, :] = left[0:RIM, :]
        to_left[0:RIM, :] = right[RIM : 2 * RIM, :]

    @pl.when(lat == 7)
    def _():
        to_right[RIM : 2 * RIM, :] = left[CELLS - 2 * RIM : CELLS - RIM, :]
        to_left[RIM : 2 * RIM, :] = right[CELLS - RIM :, :]


def set_rows(coef, at, rows):
    for d in range(SPAN):
        coef[d, at : at + rows.shape[0], :] = rows[:, d * 128 : (d + 1) * 128]


def band_rows(win, band, coef, cycle, row_of):
    low_half = lax.broadcasted_iota(jnp.int32, (LON, 2 * NLON), 1) < NLON
    for k in range(BASIS):
        rolled = []
        for d in range(SPAN):
            row, lane = row_of(d, k)
            values = coef[lane, pl.ds(row, 1), :]
            spread_row = jnp.broadcast_to(values, (LON, 2 * NLON))
            rolled.append(pltpu.roll(spread_row, LON, 1, stride=1, stride_axis=0))
        at = k * LON
        band[at : at + LON, 0:128] = jnp.where(low_half, rolled[0], rolled[1]).astype(bf16)
        band[at : at + LON, 128:256] = jnp.where(low_half, rolled[2], rolled[3]).astype(bf16)
        band[at : at + LON, 256:384] = rolled[4].astype(bf16)
    window = win[cycle * NLON : cycle * NLON + SPAN * NLON, :]
    return dot(band[:, 0 : SPAN * NLON], window, ((1,), (0,)))


def hidden_grad_kernel(tangent, weight_out, hidden_grad):
    hidden_grad[...] = dot(tangent[...], weight_out[...], ((1,), (1,)))


def forward_kernel(
    place, tile, left, right, top, bottom, left_side, right_side, far_e, own_e,
    tangent, hidden_grad, conv_hbm, in_hbm, out_hbm,
    out, blend_grad, mine, mine_mlp, theirs, theirs_mlp, to_up, to_down,
    win, band, coef, spread, conv_weight, weight_in, weight_out, sems
):
    lat = place[0]
    lon = place[1]
    core = place[2]
    loads = [
        pltpu.make_async_copy(source, target, sems.at[i])
        for i, (source, target) in enumerate(
            ((conv_hbm, conv_weight), (in_hbm, weight_in), (out_hbm, weight_out))
        )
    ]
    for load in loads:
        load.start()
    fill_window(win, tile, left, right, top, bottom, left_side, right_side, lat)
    set_rows(coef, 0, left_side[2 * RIM :, :].astype(f32))
    set_rows(coef, 16, own_e[...].astype(f32))
    set_rows(coef, 32, right_side[2 * RIM :, :].astype(f32))
    set_rows(coef, 48, far_e[...].astype(f32))

    def base(cycle):
        return lax.rem(cycle // OWNED - lon + 1 + 4, 4) * 16 + (cycle % OWNED) * BASIS

    for i in range(CYCLES):
        start = base(i)
        rows = band_rows(win, band.at[i % 2], coef, i, lambda d, k: (start + k, d))
        for k in range(BASIS):
            spread[i * LON : (i + 1) * LON, k * EMBED : (k + 1) * EMBED] = rows[
                k * LON : (k + 1) * LON, :
            ].astype(bf16)

    loads[0].wait()
    blended = (
        tile[...].astype(f32) + dot(spread[...], conv_weight[...], ((1,), (0,)))
    ).astype(bf16)
    loads[1].wait()
    preact = dot(blended, weight_in[...], ((1,), (0,)))
    cdf = 0.5 * (1.0 + lax.erf(preact * half_root))
    hidden = (preact * cdf).astype(bf16)
    loads[2].wait()
    out[...] = (
        blended.astype(f32) + dot(hidden, weight_out[...], ((1,), (0,)))
    ).astype(bf16)
    slope = cdf + preact * jnp.exp(-0.5 * preact * preact) * gauss_norm
    preact_grad = (hidden_grad[...] * slope).astype(bf16)
    grad = (
        tangent[...].astype(f32) + dot(preact_grad, weight_in[...], ((1,), (1,)))
    ).astype(bf16)
    blend_grad[...] = grad
    for side in (theirs, mine):
        side[:, 0:EMBED] = grad
    for side in (theirs_mlp, mine_mlp):
        side[:, 0:EMBED] = blended
    for c in range(2):

        def store(side, side_mlp):
            for k in range(BASIS):
                at = k * EMBED + c * 320
                to = EMBED + k * 384
                side[:, to : to + 320] = spread[:, at : at + 320]
                at = k * 320 + c * 160
                to = EMBED + k * 160
                side_mlp[:, to : to + 160] = hidden[:, at : at + 160]
                side_mlp[:, to + EMBED : to + EMBED + 160] = preact_grad[:, at : at + 160]

        @pl.when(core == c)
        def _():
            store(mine, mine_mlp)

        @pl.when(core != c)
        def _():
            store(theirs, theirs_mlp)

    edges = []
    for cycle in (0, 1, CYCLES - 2, CYCLES - 1):
        start = base(cycle)
        for k in range(BASIS):
            edges.append(
                jnp.concatenate([coef[d, pl.ds(start + k, 1), :] for d in range(SPAN)], axis=1)
            )
    to_up[0:RIM, :] = grad[CELLS - RIM :, :]
    to_up[RIM : RIM + 8, :] = jnp.concatenate(edges[8:], axis=0).astype(bf16)
    to_down[0:RIM, :] = grad[:RIM, :]
    to_down[RIM : RIM + 8, :] = jnp.concatenate(edges[:8], axis=0).astype(bf16)


def mlp_grad_kernel(place, mine, other, tangent, other_tangent, order, o0, o1, o2, o3, acc):
    x = place[3]
    hidden, grad = slice(EMBED, 2 * EMBED), slice(2 * EMBED, 3 * EMBED)
    units = jnp.concatenate([mine[:, grad], other[:, grad], mine[:, hidden], other[:, hidden]])
    units = dot(units, order[...], ((1,), (0,))).astype(bf16)
    blended = jnp.concatenate([mine[:, 0:EMBED], other[:, 0:EMBED]])
    cots = jnp.concatenate([tangent[...], other_tangent[...]])
    acc[0:EMBED, :] = dot(units[0 : 2 * CELLS], blended, ((0,), (0,)))
    acc[EMBED : 2 * EMBED, :] = dot(units[2 * CELLS :], cots, ((0,), (0,)))
    for s, o in enumerate((o0, o1, o2, o3)):
        at = pl.multiple_of(lax.rem(x + s, 4) * 160, 160)
        o[0:160, :] = acc[pl.ds(at, 160), :].astype(o.dtype)
        o[160:320, :] = acc[pl.ds(at + EMBED, 160), :].astype(o.dtype)


def conv_grad_kernel(place, mine, other, o0, o1, o2, o3):
    y = place[4]
    grads = jnp.concatenate([mine[:, 0:EMBED], other[:, 0:EMBED]])
    for s, o in enumerate((o0, o1, o2, o3)):
        lanes = pl.ds(pl.multiple_of(lax.rem(y + s, 4) * 384 + EMBED, 128), 384)
        spread = jnp.concatenate([mine[:, lanes], other[:, lanes]])
        rows = dot(spread, grads, ((0,), (0,)))
        o[...] = rows[0:320, :].astype(o.dtype)


def mlp_sum_kernel(place, r0, r1, r2, r3, o0, o1, o2, o3, acc):
    y = place[4]
    acc[...] = r0[...] + r1[...].astype(f32) + r2[...].astype(f32) + r3[...].astype(f32)
    for s, o in enumerate((o0, o1, o2, o3)):
        at = pl.multiple_of(lax.rem(y + s, 4) * 40, 40)
        o[0:40, :] = acc[pl.ds(at, 40), :].astype(o.dtype)
        o[40:80, :] = acc[pl.ds(at + 160, 40), :].astype(o.dtype)


def conv_sum_kernel(place, r0, r1, r2, r3, o0, o1, o2, o3, acc):
    x = place[3]
    total = r0[...] + r1[...].astype(f32) + r2[...].astype(f32) + r3[...].astype(f32)
    for lon in range(4):
        for to in range(4):
            at = lon * 80 + to * 20
            acc[to * 80 + lon * 20 : to * 80 + lon * 20 + 20, :] = total[at : at + 20, :]
    for s, o in enumerate((o0, o1, o2, o3)):
        at = pl.multiple_of(lax.rem(x + s, 4) * 80, 80)
        o[...] = acc[pl.ds(at, 80), :].astype(o.dtype)


def pack_kernel(m0, m1, m2, m3, c0, c1, c2, c3, o):
    mlp = m0[...] + m1[...].astype(f32) + m2[...].astype(f32) + m3[...].astype(f32)
    conv = c0[...] + c1[...].astype(f32) + c2[...].astype(f32) + c3[...].astype(f32)
    for to in range(8):
        o[to, 0:10, :] = conv[to * 10 : to * 10 + 10, :].astype(bf16)
        o[to, 10:15, :] = mlp[to * 5 : to * 5 + 5, :].astype(bf16)
        o[to, 15:20, :] = mlp[40 + to * 5 : 45 + to * 5, :].astype(bf16)


def final_kernel(parts, conv, w_in, w_out):
    total = parts[0].astype(f32)
    for i in range(1, 8):
        total = total + parts[i].astype(f32)
    total = total * (1.0 / math.sqrt(MEMBERS * NLAT * NLON))
    conv[...] = total[0:10, :]
    w_in[...] = total[10:15, :]
    w_out[...] = total[15:20, :]


def field_grad_kernel(
    place, tile, left, right, top, bottom, left_side, right_side,
    own_e, left_e, right_e, far_e, conv_hbm, field_grad, win, band, coef, mixed,
    conv_weight, sem
):
    lat = place[0]
    lon = place[1]
    load = pltpu.make_async_copy(conv_hbm, conv_weight, sem)
    load.start()
    fill_window(win, tile, left, right, top, bottom, left_side, right_side, lat)
    rows = jnp.concatenate(
        [
            left_e[2 * RIM :, :], own_e[...], right_e[2 * RIM :, :], far_e[...],
            top[RIM:, :], bottom[RIM:, :],
        ],
        axis=0,
    )
    lane = lax.broadcasted_iota(jnp.int32, (2 * NLON, 2 * NLON), 0)
    to = lax.broadcasted_iota(jnp.int32, (2 * NLON, 2 * NLON), 1)
    flip = (lax.rem(lane + to, 2 * NLON) == 0).astype(f32).astype(bf16)
    for d in range(SPAN):
        coef[d, :, :] = dot(rows[:, d * 128 : (d + 1) * 128], flip, ((1,), (0,)))

    def base(cycle):
        if cycle < 0:
            return 64 + (cycle + HALO) * BASIS
        if cycle >= CYCLES:
            return 72 + (cycle - CYCLES) * BASIS
        return lax.rem(cycle // OWNED - lon + 1 + 4, 4) * 16 + (cycle % OWNED) * BASIS

    for j in range(CYCLES):
        starts = [base(j + e - HALO) for e in range(SPAN)]
        rows = band_rows(
            win, band.at[j % 2], coef, j, lambda e, k: (starts[e] + k, SPAN - 1 - e)
        )
        for k in range(BASIS):
            mixed[j * LON : (j + 1) * LON, k * EMBED : (k + 1) * EMBED] = rows[
                k * LON : (k + 1) * LON, :
            ].astype(bf16)
    total = tile[...].astype(f32)
    load.wait()
    for k in range(BASIS):
        total = total + dot(
            mixed[:, k * EMBED : (k + 1) * EMBED],
            conv_weight[k * EMBED : (k + 1) * EMBED, :],
            ((1,), (1,)),
        )
    field_grad[...] = total.astype(bf16)


def call(kernel, outs, scratch, mib, place, *args, in_hbm=()):
    vmem, hbm = pl.BlockSpec(memory_space=pltpu.VMEM), pl.BlockSpec(memory_space=pltpu.HBM)
    in_specs = [vmem] * len(args) + [hbm] * len(in_hbm)
    args = args + tuple(pltpu.with_memory_space_constraint(a, pltpu.HBM) for a in in_hbm)
    if place is not None:
        in_specs = [pl.BlockSpec(memory_space=pltpu.SMEM)] + in_specs
        args = (place,) + args
    return pl.pallas_call(
        kernel,
        out_shape=outs,
        in_specs=in_specs,
        scratch_shapes=scratch,
        compiler_params=pltpu.CompilerParams(vmem_limit_bytes=mib * 1024 * 1024),
    )(*args)


def neighbours(tile, to_up, to_down):
    forward = [(i, i + 1) for i in range(7)]
    backward = [(i + 1, i) for i in range(7)]
    left = shift(tile, "zlo", 4, 1)
    right = shift(tile, "zlo", 4, 3)
    top = lax.ppermute(to_up, LAT, forward)
    bottom = lax.ppermute(to_down, LAT, backward)
    return left, right, top, bottom


def relay(place, left, right, top, bottom, *extra):
    rows = 2 * RIM + sum(e.shape[0] for e in extra)
    to_right, to_left = call(
        side_kernel, (struct((rows, EMBED), bf16),) * 2, [], 4, place,
        left, right, top, bottom, *extra,
    )
    left_side = shift(to_right, "zlo", 4, 1)
    right_side = shift(to_left, "zlo", 4, 3)
    return left_side, right_side


def spread_out(chunks, axis):
    parts = [chunks[0]]
    for s in (1, 2, 3):
        parts.append(shift(chunks[s], axis, 4, s))
    return tuple(parts)


def coefficients(filter_basis, lon_offsets):
    lanes = jnp.arange(2 * NLON, dtype=jnp.int32) % NLON
    values = filter_basis.astype(f32).transpose(0, 2, 1, 3)
    hit = lanes[None, None, None, :] == (lon_offsets % NLON)[:, :, :, None]
    kept = jnp.where(hit[:, None], values[..., None], 0.0)
    rows = kept.sum(axis=3).astype(bf16).reshape(OWNED * BASIS, SPAN * 2 * NLON)
    return jnp.pad(rows, ((0, 16 - OWNED * BASIS), (0, 0)))


def block(fields, filter_basis, lon_offsets, conv_weight, weight_in, weight_out, cotangent):
    y = lax.axis_index("y")
    core = lax.axis_index("core")
    lon = lax.axis_index("zlo")
    x = lax.axis_index("x")
    lat = 2 * y + core
    place = jnp.stack([lat, lon, core, x, y]).astype(jnp.int32)
    tile = fields.reshape(CELLS, EMBED)
    tangent = cotangent.reshape(CELLS, EMBED)

    left, right, top, bottom = neighbours(tile, tile[CELLS - RIM :], tile[:RIM])
    own_e = coefficients(filter_basis, lon_offsets)
    far_e = shift(own_e, "zlo", 4, 2)
    left_side, right_side = relay(place, left, right, top, bottom, own_e)
    other_tangent = shift(tangent, "core", 2, 1)

    unit = jnp.arange(EMBED, dtype=jnp.int32)
    ux, uy, ul, ur = unit // 160, unit // 40 % 4, unit // 10 % 4, unit % 10
    source = uy * 160 + ul * 40 + ux * 10 + ur
    order = (unit[:, None] == source[None, :]).astype(bf16)

    hidden_grad = call(
        hidden_grad_kernel, struct((CELLS, HIDDEN), f32), [], 8, None, tangent, weight_out
    )
    far_e, other_tangent, order = lax.optimization_barrier((far_e, other_tangent, order))
    window = pltpu.VMEM(((CYCLES + 2 * HALO) * NLON, EMBED), bf16)
    band = pltpu.VMEM((2, BASIS * LON, 384), bf16)
    edge = struct((RIM + 8, EMBED), bf16)
    parts = (struct((CELLS, CONV_PART), bf16), struct((CELLS, MLP_PART), bf16))
    block_out, blend_grad, mine, mine_mlp, theirs, theirs_mlp, to_up, to_down = call(
        forward_kernel,
        (struct((CELLS, EMBED), bf16), struct((CELLS, EMBED), bf16))
        + parts
        + parts
        + (edge, edge),
        [
            window,
            band,
            pltpu.VMEM((SPAN, 64, 2 * NLON), f32),
            pltpu.VMEM((CELLS, WIDE), bf16),
            pltpu.VMEM((WIDE, EMBED), bf16),
            pltpu.VMEM((EMBED, HIDDEN), bf16),
            pltpu.VMEM((HIDDEN, EMBED), bf16),
            pltpu.SemaphoreType.DMA((3,)),
        ],
        24, place, tile, left, right, top, bottom, left_side, right_side, far_e, own_e,
        tangent, hidden_grad, in_hbm=(conv_weight, weight_in, weight_out),
    )
    other = shift(theirs, "core", 2, 1)
    other_mlp = shift(theirs_mlp, "core", 2, 1)
    g_left, g_right, g_top, g_bottom = neighbours(blend_grad, to_up, to_down)

    chunk = (struct((320, EMBED), f32),) + (struct((320, EMBED), bf16),) * 3
    c = call(conv_grad_kernel, chunk, [], 16, place, mine, other)
    c = spread_out(c, "y")
    m = call(
        mlp_grad_kernel, chunk, [pltpu.VMEM((2 * EMBED, EMBED), f32)],
        16, place, mine_mlp, other_mlp, tangent, other_tangent, order,
    )
    m = spread_out(m, "x")

    g_left_side, g_right_side = relay(place, g_left, g_right, g_top, g_bottom)
    piece = (struct((80, EMBED), f32),) + (struct((80, EMBED), bf16),) * 3
    total = pltpu.VMEM((320, EMBED), f32)
    c = call(conv_sum_kernel, piece, [total], 8, place, *c)
    c = spread_out(c, "x")
    m = call(mlp_sum_kernel, piece, [total], 8, place, *m)
    m = spread_out(m, "y")
    field_grad = call(
        field_grad_kernel,
        struct((CELLS, EMBED), bf16),
        [
            window,
            band,
            pltpu.VMEM((SPAN, 80, 2 * NLON), f32),
            pltpu.VMEM((CELLS, WIDE), bf16),
            pltpu.VMEM((WIDE, EMBED), bf16),
            pltpu.SemaphoreType.DMA,
        ],
        16, place, blend_grad, g_left, g_right, g_top, g_bottom, g_left_side, g_right_side,
        own_e, left_side, right_side, far_e, in_hbm=(conv_weight,),
    )
    packed = call(pack_kernel, struct((8, 20, EMBED), bf16), [], 4, None, *m, *c)
    parts = lax.all_to_all(packed, ("zlo", "zhi"), split_axis=0, concat_axis=0, tiled=True)
    conv_grad, in_grad, out_grad = call(
        final_kernel,
        (struct((10, EMBED), f32), struct((5, EMBED), f32), struct((5, EMBED), f32)),
        [], 4, None, parts,
    )
    return (
        block_out.reshape(fields.shape),
        field_grad.reshape(fields.shape),
        conv_grad,
        in_grad.T,
        out_grad,
    )


def solution(mesh):
    fine = Mesh(mesh.devices.reshape(4, 2, 4, 4, 2), ("y", "core", "zlo", "x", "zhi"))
    tile_spec = P(("x", "zhi"), LAT, "zlo", None)
    everyone = ("y", "core", "zlo", "x", "zhi")
    return jax.shard_map(
        block,
        mesh=fine,
        in_specs=(
            tile_spec,
            P(LAT + ("zlo",), None, None, None),
            P(LAT + ("zlo",), None, None),
            P(),
            P(),
            P(),
            tile_spec,
        ),
        out_specs=(
            tile_spec,
            tile_spec,
            P(everyone, None),
            P(None, everyone),
            P(everyone, None),
        ),
        check_vma=False,
    )
```

```python
import math

import jax
import jax.numpy as jnp
from jax import lax
from jax.experimental import pallas as pl
from jax.experimental.pallas import tpu as pltpu
from jax.sharding import Mesh, PartitionSpec as P


EMBED = 640
HIDDEN = 1280
BASIS = 4
SPAN = 5
NLON = 64
NLAT = 96
MEMBERS = 8
WIDE = BASIS * EMBED

CYCLES = 12
LON = 16
CELLS = CYCLES * LON
OWNED = 3
HALO = 2
RIM = HALO * LON
CONV_PART = EMBED + BASIS * 384
MLP_PART = 3 * EMBED

half_root = 0.7071067811865476
gauss_norm = 0.3989422804014327


LAT = ("y", "core")
bf16 = jnp.bfloat16
f32 = jnp.float32


def dot(a, b, dims):
    return lax.dot_general(a, b, (dims, ((), ())), preferred_element_type=f32)


def shift(block, axis, count, step):
    return lax.ppermute(block, axis, [(i, (i + step) % count) for i in range(count)])


def struct(shape, dtype):
    return jax.ShapeDtypeStruct(shape, dtype)


def fill_window(win, tile, left, right, top, bottom, left_side, right_side, lat):
    zero = jnp.zeros((LON, EMBED), bf16)

    def put(cycle, group, rows):
        at = (cycle + HALO) * NLON + group * LON
        win[at : at + LON, :] = rows

    for group, (inner, side) in enumerate(
        ((left, left_side), (tile, None), (right, right_side))
    ):
        for row in range(CYCLES):
            put(row, group, inner[row * LON : (row + 1) * LON, :])
        for row in range(HALO):
            upper, lower = (top, bottom) if side is None else (side, side)
            skip = 0 if side is None else RIM
            put(row - HALO, group, upper[row * LON : (row + 1) * LON, :])
            put(row + CYCLES, group, lower[skip + row * LON : skip + (row + 1) * LON, :])
    for row in range(-HALO, CYCLES + HALO):
        put(row, 3, zero)

    def polar(first, skip, missing):
        for row in range(HALO):
            rows = slice(skip + row * LON, skip + (row + 1) * LON)
            put(first + row, 3, left_side[rows, :])
            put(first + HALO + row, 3, right_side[rows, :])
            put(missing + row, 0, zero)
            put(missing + row, 2, zero)

    @pl.when(lat == 0)
    def _():
        polar(0, 0, -HALO)

    @pl.when(lat == 7)
    def _():
        polar(CYCLES - 4, RIM, CYCLES)


def side_kernel(place, left, right, top, bottom, *rest):
    *extra, to_right, to_left = rest
    lat = place[0]
    for to in (to_right, to_left):
        to[0:RIM, :] = top[0:RIM, :]
        to[RIM : 2 * RIM, :] = bottom[0:RIM, :]
        if extra:
            to[2 * RIM :, :] = extra[0][...]

    @pl.when(lat == 0)
    def _():
        to_right[0:RIM, :] = left[0:RIM, :]
        to_left[0:RIM, :] = right[RIM : 2 * RIM, :]

    @pl.when(lat == 7)
    def _():
        to_right[RIM : 2 * RIM, :] = left[CELLS - 2 * RIM : CELLS - RIM, :]
        to_left[RIM : 2 * RIM, :] = right[CELLS - RIM :, :]


def set_rows(coef, at, rows):
    for d in range(SPAN):
        coef[d, at : at + rows.shape[0], :] = rows[:, d * 128 : (d + 1) * 128]


def band_rows(win, band, coef, cycle, row_of):
    low_half = lax.broadcasted_iota(jnp.int32, (LON, 2 * NLON), 1) < NLON
    for k in range(BASIS):
        rolled = []
        for d in range(SPAN):
            row, lane = row_of(d, k)
            values = coef[lane, pl.ds(row, 1), :]
            spread_row = jnp.broadcast_to(values, (LON, 2 * NLON))
            rolled.append(pltpu.roll(spread_row, LON, 1, stride=1, stride_axis=0))
        at = k * LON
        band[at : at + LON, 0:128] = jnp.where(low_half, rolled[0], rolled[1]).astype(bf16)
        band[at : at + LON, 128:256] = jnp.where(low_half, rolled[2], rolled[3]).astype(bf16)
        band[at : at + LON, 256:384] = rolled[4].astype(bf16)
    window = win[cycle * NLON : cycle * NLON + SPAN * NLON, :]
    return dot(band[:, 0 : SPAN * NLON], window, ((1,), (0,)))


def hidden_grad_kernel(tangent, weight_out, hidden_grad):
    hidden_grad[...] = dot(tangent[...], weight_out[...], ((1,), (1,)))


def forward_kernel(
    place, tile, left, right, top, bottom, left_side, right_side, far_e, own_e,
    tangent, hidden_grad, conv_hbm, in_hbm, out_hbm,
    out, blend_grad, mine, mine_mlp, theirs, theirs_mlp, to_up, to_down,
    win, band, coef, spread, conv_weight, weight_in, weight_out, sems
):
    lat = place[0]
    lon = place[1]
    core = place[2]
    loads = [
        pltpu.make_async_copy(source, target, sems.at[i])
        for i, (source, target) in enumerate(
            ((conv_hbm, conv_weight), (in_hbm, weight_in), (out_hbm, weight_out))
        )
    ]
    for load in loads:
        load.start()
    fill_window(win, tile, left, right, top, bottom, left_side, right_side, lat)
    set_rows(coef, 0, left_side[2 * RIM :, :].astype(f32))
    set_rows(coef, 16, own_e[...].astype(f32))
    set_rows(coef, 32, right_side[2 * RIM :, :].astype(f32))
    set_rows(coef, 48, far_e[...].astype(f32))

    def base(cycle):
        return lax.rem(cycle // OWNED - lon + 1 + 4, 4) * 16 + (cycle % OWNED) * BASIS

    for i in range(CYCLES):
        start = base(i)
        rows = band_rows(win, band.at[i % 2], coef, i, lambda d, k: (start + k, d))
        for k in range(BASIS):
            spread[i * LON : (i + 1) * LON, k * EMBED : (k + 1) * EMBED] = rows[
                k * LON : (k + 1) * LON, :
            ].astype(bf16)

    loads[0].wait()
    blended = (
        tile[...].astype(f32) + dot(spread[...], conv_weight[...], ((1,), (0,)))
    ).astype(bf16)
    loads[1].wait()
    preact = dot(blended, weight_in[...], ((1,), (0,)))
    cdf = 0.5 * (1.0 + lax.erf(preact * half_root))
    hidden = (preact * cdf).astype(bf16)
    loads[2].wait()
    out[...] = (
        blended.astype(f32) + dot(hidden, weight_out[...], ((1,), (0,)))
    ).astype(bf16)
    slope = cdf + preact * jnp.exp(-0.5 * preact * preact) * gauss_norm
    preact_grad = (hidden_grad[...] * slope).astype(bf16)
    grad = (
        tangent[...].astype(f32) + dot(preact_grad, weight_in[...], ((1,), (1,)))
    ).astype(bf16)
    blend_grad[...] = grad
    for side in (theirs, mine):
        side[:, 0:EMBED] = grad
    for side in (theirs_mlp, mine_mlp):
        side[:, 0:EMBED] = blended
    for c in range(2):

        def store(side, side_mlp):
            for k in range(BASIS):
                at = k * EMBED + c * 320
                to = EMBED + k * 384
                side[:, to : to + 320] = spread[:, at : at + 320]
                at = k * 320 + c * 160
                to = EMBED + k * 160
                side_mlp[:, to : to + 160] = hidden[:, at : at + 160]
                side_mlp[:, to + EMBED : to + EMBED + 160] = preact_grad[:, at : at + 160]

        @pl.when(core == c)
        def _():
            store(mine, mine_mlp)

        @pl.when(core != c)
        def _():
            store(theirs, theirs_mlp)

    edges = []
    for cycle in (0, 1, CYCLES - 2, CYCLES - 1):
        start = base(cycle)
        for k in range(BASIS):
            edges.append(
                jnp.concatenate([coef[d, pl.ds(start + k, 1), :] for d in range(SPAN)], axis=1)
            )
    to_up[0:RIM, :] = grad[CELLS - RIM :, :]
    to_up[RIM : RIM + 8, :] = jnp.concatenate(edges[8:], axis=0).astype(bf16)
    to_down[0:RIM, :] = grad[:RIM, :]
    to_down[RIM : RIM + 8, :] = jnp.concatenate(edges[:8], axis=0).astype(bf16)


def mlp_grad_kernel(place, mine, other, tangent, other_tangent, order, o0, o1, o2, o3, acc):
    x = place[3]
    hidden, grad = slice(EMBED, 2 * EMBED), slice(2 * EMBED, 3 * EMBED)
    units = jnp.concatenate([mine[:, grad], other[:, grad], mine[:, hidden], other[:, hidden]])
    units = dot(order[...], units, ((1,), (1,))).astype(bf16)
    blended = jnp.concatenate([mine[:, 0:EMBED], other[:, 0:EMBED]])
    cots = jnp.concatenate([tangent[...], other_tangent[...]])
    acc[0:EMBED, :] = dot(units[:, 0 : 2 * CELLS], blended, ((1,), (0,)))
    acc[EMBED : 2 * EMBED, :] = dot(units[:, 2 * CELLS :], cots, ((1,), (0,)))
    for s, o in enumerate((o0, o1, o2, o3)):
        at = pl.multiple_of(lax.rem(x + s, 4) * 160, 160)
        o[0:160, :] = acc[pl.ds(at, 160), :].astype(o.dtype)
        o[160:320, :] = acc[pl.ds(at + EMBED, 160), :].astype(o.dtype)


def conv_grad_kernel(place, mine, other, o0, o1, o2, o3):
    y = place[4]
    grads = jnp.concatenate([mine[:, 0:EMBED], other[:, 0:EMBED]])
    for s, o in enumerate((o0, o1, o2, o3)):
        lanes = pl.ds(pl.multiple_of(lax.rem(y + s, 4) * 384 + EMBED, 128), 384)
        spread = jnp.concatenate([mine[:, lanes], other[:, lanes]])
        rows = dot(spread, grads, ((0,), (0,)))
        o[...] = rows[0:320, :].astype(o.dtype)


def mlp_sum_kernel(place, r0, r1, r2, r3, o0, o1, o2, o3, acc):
    y = place[4]
    acc[...] = r0[...] + r1[...].astype(f32) + r2[...].astype(f32) + r3[...].astype(f32)
    for s, o in enumerate((o0, o1, o2, o3)):
        at = pl.multiple_of(lax.rem(y + s, 4) * 40, 40)
        o[0:40, :] = acc[pl.ds(at, 40), :].astype(o.dtype)
        o[40:80, :] = acc[pl.ds(at + 160, 40), :].astype(o.dtype)


def conv_sum_kernel(place, r0, r1, r2, r3, o0, o1, o2, o3, acc):
    x = place[3]
    total = r0[...] + r1[...].astype(f32) + r2[...].astype(f32) + r3[...].astype(f32)
    for lon in range(4):
        for to in range(4):
            at = lon * 80 + to * 20
            acc[to * 80 + lon * 20 : to * 80 + lon * 20 + 20, :] = total[at : at + 20, :]
    for s, o in enumerate((o0, o1, o2, o3)):
        at = pl.multiple_of(lax.rem(x + s, 4) * 80, 80)
        o[...] = acc[pl.ds(at, 80), :].astype(o.dtype)


def pack_kernel(m0, m1, m2, m3, c0, c1, c2, c3, o):
    mlp = m0[...] + m1[...].astype(f32) + m2[...].astype(f32) + m3[...].astype(f32)
    conv = c0[...] + c1[...].astype(f32) + c2[...].astype(f32) + c3[...].astype(f32)
    for to in range(8):
        o[to, 0:10, :] = conv[to * 10 : to * 10 + 10, :].astype(bf16)
        o[to, 10:15, :] = mlp[to * 5 : to * 5 + 5, :].astype(bf16)
        o[to, 15:20, :] = mlp[40 + to * 5 : 45 + to * 5, :].astype(bf16)


def final_kernel(parts, conv, w_in, w_out):
    total = parts[0].astype(f32)
    for i in range(1, 8):
        total = total + parts[i].astype(f32)
    total = total * (1.0 / math.sqrt(MEMBERS * NLAT * NLON))
    conv[...] = total[0:10, :]
    w_in[...] = total[10:15, :]
    w_out[...] = total[15:20, :]


def field_grad_kernel(
    place, tile, left, right, top, bottom, left_side, right_side,
    own_e, left_e, right_e, far_e, conv_hbm, field_grad, win, band, coef, mixed,
    conv_weight, sem
):
    lat = place[0]
    lon = place[1]
    load = pltpu.make_async_copy(conv_hbm, conv_weight, sem)
    load.start()
    fill_window(win, tile, left, right, top, bottom, left_side, right_side, lat)
    rows = jnp.concatenate(
        [
            left_e[2 * RIM :, :], own_e[...], right_e[2 * RIM :, :], far_e[...],
            top[RIM:, :], bottom[RIM:, :],
        ],
        axis=0,
    )
    lane = lax.broadcasted_iota(jnp.int32, (2 * NLON, 2 * NLON), 0)
    to = lax.broadcasted_iota(jnp.int32, (2 * NLON, 2 * NLON), 1)
    flip = (lax.rem(lane + to, 2 * NLON) == 0).astype(f32).astype(bf16)
    for d in range(SPAN):
        coef[d, :, :] = dot(rows[:, d * 128 : (d + 1) * 128], flip, ((1,), (0,)))

    def base(cycle):
        if cycle < 0:
            return 64 + (cycle + HALO) * BASIS
        if cycle >= CYCLES:
            return 72 + (cycle - CYCLES) * BASIS
        return lax.rem(cycle // OWNED - lon + 1 + 4, 4) * 16 + (cycle % OWNED) * BASIS

    for j in range(CYCLES):
        starts = [base(j + e - HALO) for e in range(SPAN)]
        rows = band_rows(
            win, band.at[j % 2], coef, j, lambda e, k: (starts[e] + k, SPAN - 1 - e)
        )
        for k in range(BASIS):
            mixed[j * LON : (j + 1) * LON, k * EMBED : (k + 1) * EMBED] = rows[
                k * LON : (k + 1) * LON, :
            ].astype(bf16)
    total = tile[...].astype(f32)
    load.wait()
    for k in range(BASIS):
        total = total + dot(
            mixed[:, k * EMBED : (k + 1) * EMBED],
            conv_weight[k * EMBED : (k + 1) * EMBED, :],
            ((1,), (1,)),
        )
    field_grad[...] = total.astype(bf16)


def call(kernel, outs, scratch, mib, place, *args, in_hbm=()):
    vmem, hbm = pl.BlockSpec(memory_space=pltpu.VMEM), pl.BlockSpec(memory_space=pltpu.HBM)
    in_specs = [vmem] * len(args) + [hbm] * len(in_hbm)
    args = args + tuple(pltpu.with_memory_space_constraint(a, pltpu.HBM) for a in in_hbm)
    if place is not None:
        in_specs = [pl.BlockSpec(memory_space=pltpu.SMEM)] + in_specs
        args = (place,) + args
    return pl.pallas_call(
        kernel,
        out_shape=outs,
        in_specs=in_specs,
        scratch_shapes=scratch,
        compiler_params=pltpu.CompilerParams(vmem_limit_bytes=mib * 1024 * 1024),
    )(*args)


def neighbours(tile, to_up, to_down):
    forward = [(i, i + 1) for i in range(7)]
    backward = [(i + 1, i) for i in range(7)]
    left = shift(tile, "zlo", 4, 1)
    right = shift(tile, "zlo", 4, 3)
    top = lax.ppermute(to_up, LAT, forward)
    bottom = lax.ppermute(to_down, LAT, backward)
    return left, right, top, bottom


def relay(place, left, right, top, bottom, *extra):
    rows = 2 * RIM + sum(e.shape[0] for e in extra)
    to_right, to_left = call(
        side_kernel, (struct((rows, EMBED), bf16),) * 2, [], 4, place,
        left, right, top, bottom, *extra,
    )
    left_side = shift(to_right, "zlo", 4, 1)
    right_side = shift(to_left, "zlo", 4, 3)
    return left_side, right_side


def spread_out(chunks, axis):
    parts = [chunks[0]]
    for s in (1, 2, 3):
        parts.append(shift(chunks[s], axis, 4, s))
    return tuple(parts)


def coefficients(filter_basis, lon_offsets):
    lanes = jnp.arange(2 * NLON, dtype=jnp.int32) % NLON
    values = filter_basis.astype(f32).transpose(0, 2, 1, 3)
    hit = lanes[None, None, None, :] == (lon_offsets % NLON)[:, :, :, None]
    kept = jnp.where(hit[:, None], values[..., None], 0.0)
    rows = kept.sum(axis=3).astype(bf16).reshape(OWNED * BASIS, SPAN * 2 * NLON)
    return jnp.pad(rows, ((0, 16 - OWNED * BASIS), (0, 0)))


def block(fields, filter_basis, lon_offsets, conv_weight, weight_in, weight_out, cotangent):
    y = lax.axis_index("y")
    core = lax.axis_index("core")
    lon = lax.axis_index("zlo")
    x = lax.axis_index("x")
    lat = 2 * y + core
    place = jnp.stack([lat, lon, core, x, y]).astype(jnp.int32)
    tile = fields.reshape(CELLS, EMBED)
    tangent = cotangent.reshape(CELLS, EMBED)

    left, right, top, bottom = neighbours(tile, tile[CELLS - RIM :], tile[:RIM])
    own_e = coefficients(filter_basis, lon_offsets)
    far_e = shift(own_e, "zlo", 4, 2)
    left_side, right_side = relay(place, left, right, top, bottom, own_e)
    other_tangent = shift(tangent, "core", 2, 1)

    unit = jnp.arange(EMBED, dtype=jnp.int32)
    ux, uy, ul, ur = unit // 160, unit // 40 % 4, unit // 10 % 4, unit % 10
    source = uy * 160 + ul * 40 + ux * 10 + ur
    order = (source[:, None] == unit[None, :]).astype(bf16)

    hidden_grad = call(
        hidden_grad_kernel, struct((CELLS, HIDDEN), f32), [], 8, None, tangent, weight_out
    )
    far_e, other_tangent, order = lax.optimization_barrier((far_e, other_tangent, order))
    window = pltpu.VMEM(((CYCLES + 2 * HALO) * NLON, EMBED), bf16)
    band = pltpu.VMEM((2, BASIS * LON, 384), bf16)
    edge = struct((RIM + 8, EMBED), bf16)
    parts = (struct((CELLS, CONV_PART), bf16), struct((CELLS, MLP_PART), bf16))
    block_out, blend_grad, mine, mine_mlp, theirs, theirs_mlp, to_up, to_down = call(
        forward_kernel,
        (struct((CELLS, EMBED), bf16), struct((CELLS, EMBED), bf16))
        + parts
        + parts
        + (edge, edge),
        [
            window,
            band,
            pltpu.VMEM((SPAN, 64, 2 * NLON), f32),
            pltpu.VMEM((CELLS, WIDE), bf16),
            pltpu.VMEM((WIDE, EMBED), bf16),
            pltpu.VMEM((EMBED, HIDDEN), bf16),
            pltpu.VMEM((HIDDEN, EMBED), bf16),
            pltpu.SemaphoreType.DMA((3,)),
        ],
        24, place, tile, left, right, top, bottom, left_side, right_side, far_e, own_e,
        tangent, hidden_grad, in_hbm=(conv_weight, weight_in, weight_out),
    )
    other = shift(theirs, "core", 2, 1)
    other_mlp = shift(theirs_mlp, "core", 2, 1)
    g_left, g_right, g_top, g_bottom = neighbours(blend_grad, to_up, to_down)

    chunk = (struct((320, EMBED), f32),) + (struct((320, EMBED), bf16),) * 3
    c = call(conv_grad_kernel, chunk, [], 16, place, mine, other)
    c = spread_out(c, "y")
    m = call(
        mlp_grad_kernel, chunk, [pltpu.VMEM((2 * EMBED, EMBED), f32)],
        16, place, mine_mlp, other_mlp, tangent, other_tangent, order,
    )
    m = spread_out(m, "x")

    g_left_side, g_right_side = relay(place, g_left, g_right, g_top, g_bottom)
    piece = (struct((80, EMBED), f32),) + (struct((80, EMBED), bf16),) * 3
    total = pltpu.VMEM((320, EMBED), f32)
    c = call(conv_sum_kernel, piece, [total], 8, place, *c)
    c = spread_out(c, "x")
    m = call(mlp_sum_kernel, piece, [total], 8, place, *m)
    m = spread_out(m, "y")
    field_grad = call(
        field_grad_kernel,
        struct((CELLS, EMBED), bf16),
        [
            window,
            band,
            pltpu.VMEM((SPAN, 80, 2 * NLON), f32),
            pltpu.VMEM((CELLS, WIDE), bf16),
            pltpu.VMEM((WIDE, EMBED), bf16),
            pltpu.SemaphoreType.DMA,
        ],
        16, place, blend_grad, g_left, g_right, g_top, g_bottom, g_left_side, g_right_side,
        own_e, left_side, right_side, far_e, in_hbm=(conv_weight,),
    )
    packed = call(pack_kernel, struct((8, 20, EMBED), bf16), [], 4, None, *m, *c)
    parts = lax.all_to_all(packed, ("zlo", "zhi"), split_axis=0, concat_axis=0, tiled=True)
    conv_grad, in_grad, out_grad = call(
        final_kernel,
        (struct((10, EMBED), f32), struct((5, EMBED), f32), struct((5, EMBED), f32)),
        [], 4, None, parts,
    )
    return (
        block_out.reshape(fields.shape),
        field_grad.reshape(fields.shape),
        conv_grad,
        in_grad.T,
        out_grad,
    )


def solution(mesh):
    fine = Mesh(mesh.devices.reshape(4, 2, 4, 4, 2), ("y", "core", "zlo", "x", "zhi"))
    tile_spec = P(("x", "zhi"), LAT, "zlo", None)
    everyone = ("y", "core", "zlo", "x", "zhi")
    return jax.shard_map(
        block,
        mesh=fine,
        in_specs=(
            tile_spec,
            P(LAT + ("zlo",), None, None, None),
            P(LAT + ("zlo",), None, None),
            P(),
            P(),
            P(),
            tile_spec,
        ),
        out_specs=(
            tile_spec,
            tile_spec,
            P(everyone, None),
            P(None, everyone),
            P(everyone, None),
        ),
        check_vma=False,
    )
```

```python
import math

import jax
import jax.numpy as jnp
from jax import lax
from jax.experimental import pallas as pl
from jax.experimental.pallas import tpu as pltpu
from jax.sharding import Mesh, PartitionSpec as P


EMBED = 640
HIDDEN = 1280
BASIS = 4
SPAN = 5
NLON = 64
NLAT = 96
MEMBERS = 8
WIDE = BASIS * EMBED

CYCLES = 12
LON = 16
CELLS = CYCLES * LON
OWNED = 3
HALO = 2
RIM = HALO * LON
CONV_PART = EMBED + BASIS * 384
MLP_PART = 3 * EMBED

half_root = 0.7071067811865476
gauss_norm = 0.3989422804014327


LAT = ("y", "core")
bf16 = jnp.bfloat16
f32 = jnp.float32


def dot(a, b, dims):
    return lax.dot_general(a, b, (dims, ((), ())), preferred_element_type=f32)


def shift(block, axis, count, step):
    return lax.ppermute(block, axis, [(i, (i + step) % count) for i in range(count)])


def struct(shape, dtype):
    return jax.ShapeDtypeStruct(shape, dtype)


def fill_window(win, tile, left, right, top, bottom, left_side, right_side, lat):
    zero = jnp.zeros((LON, EMBED), bf16)

    def put(cycle, group, rows):
        at = (cycle + HALO) * NLON + group * LON
        win[at : at + LON, :] = rows

    for group, (inner, side) in enumerate(
        ((left, left_side), (tile, None), (right, right_side))
    ):
        for row in range(CYCLES):
            put(row, group, inner[row * LON : (row + 1) * LON, :])
        for row in range(HALO):
            upper, lower = (top, bottom) if side is None else (side, side)
            skip = 0 if side is None else RIM
            put(row - HALO, group, upper[row * LON : (row + 1) * LON, :])
            put(row + CYCLES, group, lower[skip + row * LON : skip + (row + 1) * LON, :])
    for row in range(-HALO, CYCLES + HALO):
        put(row, 3, zero)

    def polar(first, skip, missing):
        for row in range(HALO):
            rows = slice(skip + row * LON, skip + (row + 1) * LON)
            put(first + row, 3, left_side[rows, :])
            put(first + HALO + row, 3, right_side[rows, :])
            put(missing + row, 0, zero)
            put(missing + row, 2, zero)

    @pl.when(lat == 0)
    def _():
        polar(0, 0, -HALO)

    @pl.when(lat == 7)
    def _():
        polar(CYCLES - 4, RIM, CYCLES)


def side_kernel(place, left, right, top, bottom, *rest):
    *extra, to_right, to_left = rest
    lat = place[0]
    for to in (to_right, to_left):
        to[0:RIM, :] = top[0:RIM, :]
        to[RIM : 2 * RIM, :] = bottom[0:RIM, :]
        if extra:
            to[2 * RIM :, :] = extra[0][...]

    @pl.when(lat == 0)
    def _():
        to_right[0:RIM, :] = left[0:RIM, :]
        to_left[0:RIM, :] = right[RIM : 2 * RIM, :]

    @pl.when(lat == 7)
    def _():
        to_right[RIM : 2 * RIM, :] = left[CELLS - 2 * RIM : CELLS - RIM, :]
        to_left[RIM : 2 * RIM, :] = right[CELLS - RIM :, :]


def set_rows(coef, at, rows):
    for d in range(SPAN):
        coef[d, at : at + rows.shape[0], :] = rows[:, d * 128 : (d + 1) * 128]


def band_rows(win, band, coef, cycle, row_of):
    low_half = lax.broadcasted_iota(jnp.int32, (LON, 2 * NLON), 1) < NLON
    for k in range(BASIS):
        rolled = []
        for d in range(SPAN):
            row, lane = row_of(d, k)
            values = coef[lane, pl.ds(row, 1), :]
            spread_row = jnp.broadcast_to(values, (LON, 2 * NLON))
            rolled.append(pltpu.roll(spread_row, LON, 1, stride=1, stride_axis=0))
        at = k * LON
        band[at : at + LON, 0:128] = jnp.where(low_half, rolled[0], rolled[1]).astype(bf16)
        band[at : at + LON, 128:256] = jnp.where(low_half, rolled[2], rolled[3]).astype(bf16)
        band[at : at + LON, 256:384] = rolled[4].astype(bf16)
    window = win[cycle * NLON : cycle * NLON + SPAN * NLON, :]
    return dot(band[:, 0 : SPAN * NLON], window, ((1,), (0,)))


def hidden_grad_kernel(tangent, weight_out, hidden_grad):
    hidden_grad[...] = dot(tangent[...], weight_out[...], ((1,), (1,)))


def forward_kernel(
    place, tile, left, right, top, bottom, left_side, right_side, far_e, own_e,
    tangent, hidden_grad, conv_hbm, in_hbm, out_hbm,
    out, blend_grad, mine, mine_mlp, theirs, theirs_mlp, to_up, to_down,
    win, band, coef, spread, conv_weight, weight_in, weight_out, sems
):
    lat = place[0]
    lon = place[1]
    core = place[2]
    loads = [
        pltpu.make_async_copy(source, target, sems.at[i])
        for i, (source, target) in enumerate(
            ((conv_hbm, conv_weight), (in_hbm, weight_in), (out_hbm, weight_out))
        )
    ]
    for load in loads:
        load.start()
    fill_window(win, tile, left, right, top, bottom, left_side, right_side, lat)
    set_rows(coef, 0, left_side[2 * RIM :, :].astype(f32))
    set_rows(coef, 16, own_e[...].astype(f32))
    set_rows(coef, 32, right_side[2 * RIM :, :].astype(f32))
    set_rows(coef, 48, far_e[...].astype(f32))

    def base(cycle):
        return lax.rem(cycle // OWNED - lon + 1 + 4, 4) * 16 + (cycle % OWNED) * BASIS

    for i in range(CYCLES):
        start = base(i)
        rows = band_rows(win, band.at[i % 2], coef, i, lambda d, k: (start + k, d))
        for k in range(BASIS):
            spread[i * LON : (i + 1) * LON, k * EMBED : (k + 1) * EMBED] = rows[
                k * LON : (k + 1) * LON, :
            ].astype(bf16)

    loads[0].wait()
    blended = (
        tile[...].astype(f32) + dot(spread[...], conv_weight[...], ((1,), (0,)))
    ).astype(bf16)
    loads[1].wait()
    preact = dot(blended, weight_in[...], ((1,), (0,)))
    cdf = 0.5 * (1.0 + lax.erf(preact * half_root))
    hidden = (preact * cdf).astype(bf16)
    loads[2].wait()
    out[...] = (
        blended.astype(f32) + dot(hidden, weight_out[...], ((1,), (0,)))
    ).astype(bf16)
    slope = cdf + preact * jnp.exp(-0.5 * preact * preact) * gauss_norm
    preact_grad = (hidden_grad[...] * slope).astype(bf16)
    grad = (
        tangent[...].astype(f32) + dot(preact_grad, weight_in[...], ((1,), (1,)))
    ).astype(bf16)
    blend_grad[...] = grad
    for side in (theirs, mine):
        side[:, 0:EMBED] = grad
    for side in (theirs_mlp, mine_mlp):
        side[:, 0:EMBED] = blended
    for c in range(2):

        def store(side, side_mlp):
            for k in range(BASIS):
                at = k * EMBED + c * 320
                to = EMBED + k * 384
                side[:, to : to + 320] = spread[:, at : at + 320]
                at = k * 320 + c * 160
                to = EMBED + k * 160
                side_mlp[:, to : to + 160] = hidden[:, at : at + 160]
                side_mlp[:, to + EMBED : to + EMBED + 160] = preact_grad[:, at : at + 160]

        @pl.when(core == c)
        def _():
            store(mine, mine_mlp)

        @pl.when(core != c)
        def _():
            store(theirs, theirs_mlp)

    edges = []
    for cycle in (0, 1, CYCLES - 2, CYCLES - 1):
        start = base(cycle)
        for k in range(BASIS):
            edges.append(
                jnp.concatenate([coef[d, pl.ds(start + k, 1), :] for d in range(SPAN)], axis=1)
            )
    to_up[0:RIM, :] = grad[CELLS - RIM :, :]
    to_up[RIM : RIM + 8, :] = jnp.concatenate(edges[8:], axis=0).astype(bf16)
    to_down[0:RIM, :] = grad[:RIM, :]
    to_down[RIM : RIM + 8, :] = jnp.concatenate(edges[:8], axis=0).astype(bf16)


def mlp_grad_kernel(place, mine, other, tangent, other_tangent, order, o0, o1, o2, o3, acc):
    x = place[3]
    hidden, grad = slice(EMBED, 2 * EMBED), slice(2 * EMBED, 3 * EMBED)
    units = jnp.concatenate([mine[:, grad], other[:, grad], mine[:, hidden], other[:, hidden]])
    units = dot(order[...], units, ((1,), (1,))).astype(bf16)
    blended = jnp.concatenate([mine[:, 0:EMBED], other[:, 0:EMBED]])
    cots = jnp.concatenate([tangent[...], other_tangent[...]])
    acc[0:EMBED, :] = dot(units[:, 0 : 2 * CELLS], blended, ((1,), (0,)))
    acc[EMBED : 2 * EMBED, :] = dot(units[:, 2 * CELLS :], cots, ((1,), (0,)))
    for s, o in enumerate((o0, o1, o2, o3)):
        at = pl.multiple_of(lax.rem(x + s, 4) * 160, 160)
        o[0:160, :] = acc[pl.ds(at, 160), :].astype(o.dtype)
        o[160:320, :] = acc[pl.ds(at + EMBED, 160), :].astype(o.dtype)


def conv_grad_kernel(place, mine, other, o0, o1, o2, o3):
    y = place[4]
    grads = jnp.concatenate([mine[:, 0:EMBED], other[:, 0:EMBED]])
    for s, o in enumerate((o0, o1, o2, o3)):
        lanes = pl.ds(pl.multiple_of(lax.rem(y + s, 4) * 384 + EMBED, 128), 384)
        spread = jnp.concatenate([mine[:, lanes], other[:, lanes]])
        rows = dot(spread, grads, ((0,), (0,)))
        o[...] = rows[0:320, :].astype(o.dtype)


def mlp_sum_kernel(place, r0, r1, r2, r3, o0, o1, o2, o3, acc):
    y = place[4]
    acc[...] = r0[...] + r1[...].astype(f32) + r2[...].astype(f32) + r3[...].astype(f32)
    for s, o in enumerate((o0, o1, o2, o3)):
        at = pl.multiple_of(lax.rem(y + s, 4) * 40, 40)
        o[0:40, :] = acc[pl.ds(at, 40), :].astype(o.dtype)
        o[40:80, :] = acc[pl.ds(at + 160, 40), :].astype(o.dtype)


def conv_sum_kernel(place, r0, r1, r2, r3, o0, o1, o2, o3, acc):
    x = place[3]
    total = r0[...] + r1[...].astype(f32) + r2[...].astype(f32) + r3[...].astype(f32)
    for lon in range(4):
        for to in range(4):
            at = lon * 80 + to * 20
            acc[to * 80 + lon * 20 : to * 80 + lon * 20 + 20, :] = total[at : at + 20, :]
    for s, o in enumerate((o0, o1, o2, o3)):
        at = pl.multiple_of(lax.rem(x + s, 4) * 80, 80)
        o[...] = acc[pl.ds(at, 80), :].astype(o.dtype)


def pack_kernel(m0, m1, m2, m3, c0, c1, c2, c3, o):
    mlp = m0[...] + m1[...].astype(f32) + m2[...].astype(f32) + m3[...].astype(f32)
    conv = c0[...] + c1[...].astype(f32) + c2[...].astype(f32) + c3[...].astype(f32)
    for to in range(8):
        rows = to % 4 * 2 + to // 4
        o[to, 0:10, :] = conv[rows * 10 : rows * 10 + 10, :].astype(bf16)
        o[to, 10:15, :] = mlp[rows * 5 : rows * 5 + 5, :].astype(bf16)
        o[to, 15:20, :] = mlp[40 + rows * 5 : 45 + rows * 5, :].astype(bf16)


def final_kernel(parts, conv, w_in, w_out):
    total = parts[0].astype(f32)
    for i in range(1, 8):
        total = total + parts[i].astype(f32)
    total = total * (1.0 / math.sqrt(MEMBERS * NLAT * NLON))
    conv[...] = total[0:10, :]
    w_in[...] = total[10:15, :]
    w_out[...] = total[15:20, :]


def field_grad_kernel(
    place, tile, left, right, top, bottom, left_side, right_side,
    own_e, left_e, right_e, far_e, conv_hbm, field_grad, win, band, coef, mixed,
    conv_weight, sem
):
    lat = place[0]
    lon = place[1]
    load = pltpu.make_async_copy(conv_hbm, conv_weight, sem)
    load.start()
    fill_window(win, tile, left, right, top, bottom, left_side, right_side, lat)
    rows = jnp.concatenate(
        [
            left_e[2 * RIM :, :], own_e[...], right_e[2 * RIM :, :], far_e[...],
            top[RIM:, :], bottom[RIM:, :],
        ],
        axis=0,
    )
    lane = lax.broadcasted_iota(jnp.int32, (2 * NLON, 2 * NLON), 0)
    to = lax.broadcasted_iota(jnp.int32, (2 * NLON, 2 * NLON), 1)
    flip = (lax.rem(lane + to, 2 * NLON) == 0).astype(f32).astype(bf16)
    for d in range(SPAN):
        coef[d, :, :] = dot(rows[:, d * 128 : (d + 1) * 128], flip, ((1,), (0,)))

    def base(cycle):
        if cycle < 0:
            return 64 + (cycle + HALO) * BASIS
        if cycle >= CYCLES:
            return 72 + (cycle - CYCLES) * BASIS
        return lax.rem(cycle // OWNED - lon + 1 + 4, 4) * 16 + (cycle % OWNED) * BASIS

    for j in range(CYCLES):
        starts = [base(j + e - HALO) for e in range(SPAN)]
        rows = band_rows(
            win, band.at[j % 2], coef, j, lambda e, k: (starts[e] + k, SPAN - 1 - e)
        )
        for k in range(BASIS):
            mixed[j * LON : (j + 1) * LON, k * EMBED : (k + 1) * EMBED] = rows[
                k * LON : (k + 1) * LON, :
            ].astype(bf16)
    total = tile[...].astype(f32)
    load.wait()
    for k in range(BASIS):
        total = total + dot(
            mixed[:, k * EMBED : (k + 1) * EMBED],
            conv_weight[k * EMBED : (k + 1) * EMBED, :],
            ((1,), (1,)),
        )
    field_grad[...] = total.astype(bf16)


def call(kernel, outs, scratch, mib, place, *args, in_hbm=()):
    vmem, hbm = pl.BlockSpec(memory_space=pltpu.VMEM), pl.BlockSpec(memory_space=pltpu.HBM)
    in_specs = [vmem] * len(args) + [hbm] * len(in_hbm)
    args = args + tuple(pltpu.with_memory_space_constraint(a, pltpu.HBM) for a in in_hbm)
    if place is not None:
        in_specs = [pl.BlockSpec(memory_space=pltpu.SMEM)] + in_specs
        args = (place,) + args
    return pl.pallas_call(
        kernel,
        out_shape=outs,
        in_specs=in_specs,
        scratch_shapes=scratch,
        compiler_params=pltpu.CompilerParams(vmem_limit_bytes=mib * 1024 * 1024),
    )(*args)


def neighbours(tile, to_up, to_down):
    forward = [(i, i + 1) for i in range(7)]
    backward = [(i + 1, i) for i in range(7)]
    left = shift(tile, "zlo", 4, 1)
    right = shift(tile, "zlo", 4, 3)
    top = lax.ppermute(to_up, LAT, forward)
    bottom = lax.ppermute(to_down, LAT, backward)
    return left, right, top, bottom


def relay(place, left, right, top, bottom, *extra):
    rows = 2 * RIM + sum(e.shape[0] for e in extra)
    to_right, to_left = call(
        side_kernel, (struct((rows, EMBED), bf16),) * 2, [], 4, place,
        left, right, top, bottom, *extra,
    )
    left_side = shift(to_right, "zlo", 4, 1)
    right_side = shift(to_left, "zlo", 4, 3)
    return left_side, right_side


def spread_out(chunks, axis):
    parts = [chunks[0]]
    for s in (1, 2, 3):
        parts.append(shift(chunks[s], axis, 4, s))
    return tuple(parts)


def coefficients(filter_basis, lon_offsets):
    lanes = jnp.arange(2 * NLON, dtype=jnp.int32) % NLON
    values = filter_basis.astype(f32).transpose(0, 2, 1, 3)
    hit = lanes[None, None, None, :] == (lon_offsets % NLON)[:, :, :, None]
    kept = jnp.where(hit[:, None], values[..., None], 0.0)
    rows = kept.sum(axis=3).astype(bf16).reshape(OWNED * BASIS, SPAN * 2 * NLON)
    return jnp.pad(rows, ((0, 16 - OWNED * BASIS), (0, 0)))


def block(fields, filter_basis, lon_offsets, conv_weight, weight_in, weight_out, cotangent):
    y = lax.axis_index("y")
    core = lax.axis_index("core")
    lon = lax.axis_index("zlo")
    x = lax.axis_index("x")
    lat = 2 * y + core
    place = jnp.stack([lat, lon, core, x, y]).astype(jnp.int32)
    tile = fields.reshape(CELLS, EMBED)
    tangent = cotangent.reshape(CELLS, EMBED)

    left, right, top, bottom = neighbours(tile, tile[CELLS - RIM :], tile[:RIM])
    own_e = coefficients(filter_basis, lon_offsets)
    far_e = shift(own_e, "zlo", 4, 2)
    left_side, right_side = relay(place, left, right, top, bottom, own_e)
    other_tangent = shift(tangent, "core", 2, 1)

    unit = jnp.arange(EMBED, dtype=jnp.int32)
    ux, uy, ul, ur = unit // 160, unit // 40 % 4, unit // 10 % 4, unit % 10
    source = uy * 160 + ul * 40 + ux * 10 + ur
    order = (source[:, None] == unit[None, :]).astype(bf16)

    hidden_grad = call(
        hidden_grad_kernel, struct((CELLS, HIDDEN), f32), [], 8, None, tangent, weight_out
    )
    far_e, other_tangent, order = lax.optimization_barrier((far_e, other_tangent, order))
    window = pltpu.VMEM(((CYCLES + 2 * HALO) * NLON, EMBED), bf16)
    band = pltpu.VMEM((2, BASIS * LON, 384), bf16)
    edge = struct((RIM + 8, EMBED), bf16)
    parts = (struct((CELLS, CONV_PART), bf16), struct((CELLS, MLP_PART), bf16))
    block_out, blend_grad, mine, mine_mlp, theirs, theirs_mlp, to_up, to_down = call(
        forward_kernel,
        (struct((CELLS, EMBED), bf16), struct((CELLS, EMBED), bf16))
        + parts
        + parts
        + (edge, edge),
        [
            window,
            band,
            pltpu.VMEM((SPAN, 64, 2 * NLON), f32),
            pltpu.VMEM((CELLS, WIDE), bf16),
            pltpu.VMEM((WIDE, EMBED), bf16),
            pltpu.VMEM((EMBED, HIDDEN), bf16),
            pltpu.VMEM((HIDDEN, EMBED), bf16),
            pltpu.SemaphoreType.DMA((3,)),
        ],
        24, place, tile, left, right, top, bottom, left_side, right_side, far_e, own_e,
        tangent, hidden_grad, in_hbm=(conv_weight, weight_in, weight_out),
    )
    other = shift(theirs, "core", 2, 1)
    other_mlp = shift(theirs_mlp, "core", 2, 1)
    g_left, g_right, g_top, g_bottom = neighbours(blend_grad, to_up, to_down)

    chunk = (struct((320, EMBED), f32),) + (struct((320, EMBED), bf16),) * 3
    c = call(conv_grad_kernel, chunk, [], 16, place, mine, other)
    c = spread_out(c, "y")
    m = call(
        mlp_grad_kernel, chunk, [pltpu.VMEM((2 * EMBED, EMBED), f32)],
        16, place, mine_mlp, other_mlp, tangent, other_tangent, order,
    )
    m = spread_out(m, "x")

    g_left_side, g_right_side = relay(place, g_left, g_right, g_top, g_bottom)
    piece = (struct((80, EMBED), f32),) + (struct((80, EMBED), bf16),) * 3
    total = pltpu.VMEM((320, EMBED), f32)
    c = call(conv_sum_kernel, piece, [total], 8, place, *c)
    c = spread_out(c, "x")
    m = call(mlp_sum_kernel, piece, [total], 8, place, *m)
    m = spread_out(m, "y")
    field_grad = call(
        field_grad_kernel,
        struct((CELLS, EMBED), bf16),
        [
            window,
            band,
            pltpu.VMEM((SPAN, 80, 2 * NLON), f32),
            pltpu.VMEM((CELLS, WIDE), bf16),
            pltpu.VMEM((WIDE, EMBED), bf16),
            pltpu.SemaphoreType.DMA,
        ],
        16, place, blend_grad, g_left, g_right, g_top, g_bottom, g_left_side, g_right_side,
        own_e, left_side, right_side, far_e, in_hbm=(conv_weight,),
    )
    packed = call(pack_kernel, struct((8, 20, EMBED), bf16), [], 4, None, *m, *c)
    parts = lax.all_to_all(packed, ("zhi", "zlo"), split_axis=0, concat_axis=0, tiled=True)
    conv_grad, in_grad, out_grad = call(
        final_kernel,
        (struct((10, EMBED), f32), struct((5, EMBED), f32), struct((5, EMBED), f32)),
        [], 4, None, parts,
    )
    return (
        block_out.reshape(fields.shape),
        field_grad.reshape(fields.shape),
        conv_grad,
        in_grad.T,
        out_grad,
    )


def solution(mesh):
    fine = Mesh(mesh.devices.reshape(4, 2, 4, 4, 2), ("y", "core", "zlo", "x", "zhi"))
    tile_spec = P(("x", "zhi"), LAT, "zlo", None)
    everyone = ("y", "core", "zlo", "x", "zhi")
    return jax.shard_map(
        block,
        mesh=fine,
        in_specs=(
            tile_spec,
            P(LAT + ("zlo",), None, None, None),
            P(LAT + ("zlo",), None, None),
            P(),
            P(),
            P(),
            tile_spec,
        ),
        out_specs=(
            tile_spec,
            tile_spec,
            P(everyone, None),
            P(None, everyone),
            P(everyone, None),
        ),
        check_vma=False,
    )
```

```python
import math

import jax
import jax.numpy as jnp
from jax import lax
from jax.experimental import pallas as pl
from jax.experimental.pallas import tpu as pltpu
from jax.sharding import Mesh, PartitionSpec as P


EMBED = 640
HIDDEN = 1280
BASIS = 4
SPAN = 5
NLON = 64
NLAT = 96
MEMBERS = 8
WIDE = BASIS * EMBED

CYCLES = 12
LON = 16
CELLS = CYCLES * LON
OWNED = 3
HALO = 2
RIM = HALO * LON
CONV_PART = EMBED + BASIS * 384
MLP_PART = 3 * EMBED

half_root = 0.7071067811865476
gauss_norm = 0.3989422804014327


LAT = ("y", "core")
LINE = ("zl1", "zl0")
bf16 = jnp.bfloat16
f32 = jnp.float32


def dot(a, b, dims):
    return lax.dot_general(a, b, (dims, ((), ())), preferred_element_type=f32)


def shift(block, axis, count, step):
    return lax.ppermute(block, axis, [(i, (i + step) % count) for i in range(count)])


def struct(shape, dtype):
    return jax.ShapeDtypeStruct(shape, dtype)


def fill_window(win, tile, left, right, top, bottom, left_side, right_side, lat):
    zero = jnp.zeros((LON, EMBED), bf16)

    def put(cycle, group, rows):
        at = (cycle + HALO) * NLON + group * LON
        win[at : at + LON, :] = rows

    for group, (inner, side) in enumerate(
        ((left, left_side), (tile, None), (right, right_side))
    ):
        for row in range(CYCLES):
            put(row, group, inner[row * LON : (row + 1) * LON, :])
        for row in range(HALO):
            upper, lower = (top, bottom) if side is None else (side, side)
            skip = 0 if side is None else RIM
            put(row - HALO, group, upper[row * LON : (row + 1) * LON, :])
            put(row + CYCLES, group, lower[skip + row * LON : skip + (row + 1) * LON, :])
    for row in range(-HALO, CYCLES + HALO):
        put(row, 3, zero)

    def polar(first, skip, missing):
        for row in range(HALO):
            rows = slice(skip + row * LON, skip + (row + 1) * LON)
            put(first + row, 3, left_side[rows, :])
            put(first + HALO + row, 3, right_side[rows, :])
            put(missing + row, 0, zero)
            put(missing + row, 2, zero)

    @pl.when(lat == 0)
    def _():
        polar(0, 0, -HALO)

    @pl.when(lat == 7)
    def _():
        polar(CYCLES - 4, RIM, CYCLES)


def side_kernel(place, left, right, top, bottom, *rest):
    *extra, to_right, to_left = rest
    lat = place[0]
    for to in (to_right, to_left):
        to[0:RIM, :] = top[0:RIM, :]
        to[RIM : 2 * RIM, :] = bottom[0:RIM, :]
        if extra:
            to[2 * RIM :, :] = extra[0][...]

    @pl.when(lat == 0)
    def _():
        to_right[0:RIM, :] = left[0:RIM, :]
        to_left[0:RIM, :] = right[RIM : 2 * RIM, :]

    @pl.when(lat == 7)
    def _():
        to_right[RIM : 2 * RIM, :] = left[CELLS - 2 * RIM : CELLS - RIM, :]
        to_left[RIM : 2 * RIM, :] = right[CELLS - RIM :, :]


def set_rows(coef, at, rows):
    for d in range(SPAN):
        coef[d, at : at + rows.shape[0], :] = rows[:, d * 128 : (d + 1) * 128]


def band_rows(win, band, coef, cycle, row_of):
    low_half = lax.broadcasted_iota(jnp.int32, (LON, 2 * NLON), 1) < NLON
    for k in range(BASIS):
        rolled = []
        for d in range(SPAN):
            row, lane = row_of(d, k)
            values = coef[lane, pl.ds(row, 1), :]
            spread_row = jnp.broadcast_to(values, (LON, 2 * NLON))
            rolled.append(pltpu.roll(spread_row, LON, 1, stride=1, stride_axis=0))
        at = k * LON
        band[at : at + LON, 0:128] = jnp.where(low_half, rolled[0], rolled[1]).astype(bf16)
        band[at : at + LON, 128:256] = jnp.where(low_half, rolled[2], rolled[3]).astype(bf16)
        band[at : at + LON, 256:384] = rolled[4].astype(bf16)
    window = win[cycle * NLON : cycle * NLON + SPAN * NLON, :]
    return dot(band[:, 0 : SPAN * NLON], window, ((1,), (0,)))


def hidden_grad_kernel(tangent, weight_out, hidden_grad):
    hidden_grad[...] = dot(tangent[...], weight_out[...], ((1,), (1,)))


def forward_kernel(
    place, tile, left, right, top, bottom, left_side, right_side, far_e, own_e,
    tangent, hidden_grad, conv_hbm, in_hbm, out_hbm,
    out, blend_grad, mine, mine_mlp, theirs, theirs_mlp, to_up, to_down,
    win, band, coef, spread, conv_weight, weight_in, weight_out, sems
):
    lat = place[0]
    lon = place[1]
    core = place[2]
    loads = [
        pltpu.make_async_copy(source, target, sems.at[i])
        for i, (source, target) in enumerate(
            ((conv_hbm, conv_weight), (in_hbm, weight_in), (out_hbm, weight_out))
        )
    ]
    for load in loads:
        load.start()
    fill_window(win, tile, left, right, top, bottom, left_side, right_side, lat)
    set_rows(coef, 0, left_side[2 * RIM :, :].astype(f32))
    set_rows(coef, 16, own_e[...].astype(f32))
    set_rows(coef, 32, right_side[2 * RIM :, :].astype(f32))
    set_rows(coef, 48, far_e[...].astype(f32))

    def base(cycle):
        return lax.rem(cycle // OWNED - lon + 1 + 4, 4) * 16 + (cycle % OWNED) * BASIS

    for i in range(CYCLES):
        start = base(i)
        rows = band_rows(win, band.at[i % 2], coef, i, lambda d, k: (start + k, d))
        for k in range(BASIS):
            spread[i * LON : (i + 1) * LON, k * EMBED : (k + 1) * EMBED] = rows[
                k * LON : (k + 1) * LON, :
            ].astype(bf16)

    loads[0].wait()
    blended = (
        tile[...].astype(f32) + dot(spread[...], conv_weight[...], ((1,), (0,)))
    ).astype(bf16)
    loads[1].wait()
    preact = dot(blended, weight_in[...], ((1,), (0,)))
    cdf = 0.5 * (1.0 + lax.erf(preact * half_root))
    hidden = (preact * cdf).astype(bf16)
    loads[2].wait()
    out[...] = (
        blended.astype(f32) + dot(hidden, weight_out[...], ((1,), (0,)))
    ).astype(bf16)
    slope = cdf + preact * jnp.exp(-0.5 * preact * preact) * gauss_norm
    preact_grad = (hidden_grad[...] * slope).astype(bf16)
    grad = (
        tangent[...].astype(f32) + dot(preact_grad, weight_in[...], ((1,), (1,)))
    ).astype(bf16)
    blend_grad[...] = grad
    for side in (theirs, mine):
        side[:, 0:EMBED] = grad
    for side in (theirs_mlp, mine_mlp):
        side[:, 0:EMBED] = blended
    for c in range(2):

        def store(side, side_mlp):
            for k in range(BASIS):
                at = k * EMBED + c * 320
                to = EMBED + k * 384
                side[:, to : to + 320] = spread[:, at : at + 320]
                at = k * 320 + c * 160
                to = EMBED + k * 160
                side_mlp[:, to : to + 160] = hidden[:, at : at + 160]
                side_mlp[:, to + EMBED : to + EMBED + 160] = preact_grad[:, at : at + 160]

        @pl.when(core == c)
        def _():
            store(mine, mine_mlp)

        @pl.when(core != c)
        def _():
            store(theirs, theirs_mlp)

    edges = []
    for cycle in (0, 1, CYCLES - 2, CYCLES - 1):
        start = base(cycle)
        for k in range(BASIS):
            edges.append(
                jnp.concatenate([coef[d, pl.ds(start + k, 1), :] for d in range(SPAN)], axis=1)
            )
    to_up[0:RIM, :] = grad[CELLS - RIM :, :]
    to_up[RIM : RIM + 8, :] = jnp.concatenate(edges[8:], axis=0).astype(bf16)
    to_down[0:RIM, :] = grad[:RIM, :]
    to_down[RIM : RIM + 8, :] = jnp.concatenate(edges[:8], axis=0).astype(bf16)


def mlp_grad_kernel(place, mine, other, tangent, other_tangent, order, o0, o1, o2, o3, acc):
    x = place[3]
    hidden, grad = slice(EMBED, 2 * EMBED), slice(2 * EMBED, 3 * EMBED)
    units = jnp.concatenate([mine[:, grad], other[:, grad], mine[:, hidden], other[:, hidden]])
    units = dot(order[...], units, ((1,), (1,))).astype(bf16)
    blended = jnp.concatenate([mine[:, 0:EMBED], other[:, 0:EMBED]])
    cots = jnp.concatenate([tangent[...], other_tangent[...]])
    acc[0:EMBED, :] = dot(units[:, 0 : 2 * CELLS], blended, ((1,), (0,)))
    acc[EMBED : 2 * EMBED, :] = dot(units[:, 2 * CELLS :], cots, ((1,), (0,)))
    for s, o in enumerate((o0, o1, o2, o3)):
        at = pl.multiple_of(lax.rem(x + s, 4) * 160, 160)
        o[0:160, :] = acc[pl.ds(at, 160), :].astype(o.dtype)
        o[160:320, :] = acc[pl.ds(at + EMBED, 160), :].astype(o.dtype)


def conv_grad_kernel(place, mine, other, o0, o1, o2, o3):
    y = place[4]
    grads = jnp.concatenate([mine[:, 0:EMBED], other[:, 0:EMBED]])
    for s, o in enumerate((o0, o1, o2, o3)):
        lanes = pl.ds(pl.multiple_of(lax.rem(y + s, 4) * 384 + EMBED, 128), 384)
        spread = jnp.concatenate([mine[:, lanes], other[:, lanes]])
        rows = dot(spread, grads, ((0,), (0,)))
        o[...] = rows[0:320, :].astype(o.dtype)


def mlp_sum_kernel(place, r0, r1, r2, r3, o0, o1, o2, o3, acc):
    y = place[4]
    acc[...] = r0[...] + r1[...].astype(f32) + r2[...].astype(f32) + r3[...].astype(f32)
    for s, o in enumerate((o0, o1, o2, o3)):
        at = pl.multiple_of(lax.rem(y + s, 4) * 40, 40)
        o[0:40, :] = acc[pl.ds(at, 40), :].astype(o.dtype)
        o[40:80, :] = acc[pl.ds(at + 160, 40), :].astype(o.dtype)


def conv_sum_kernel(place, r0, r1, r2, r3, o0, o1, o2, o3, acc):
    x = place[3]
    total = r0[...] + r1[...].astype(f32) + r2[...].astype(f32) + r3[...].astype(f32)
    for lon in range(4):
        for to in range(4):
            at = lon * 80 + to * 20
            acc[to * 80 + lon * 20 : to * 80 + lon * 20 + 20, :] = total[at : at + 20, :]
    for s, o in enumerate((o0, o1, o2, o3)):
        at = pl.multiple_of(lax.rem(x + s, 4) * 80, 80)
        o[...] = acc[pl.ds(at, 80), :].astype(o.dtype)


def pack_kernel(m0, m1, m2, m3, c0, c1, c2, c3, o):
    mlp = m0[...] + m1[...].astype(f32) + m2[...].astype(f32) + m3[...].astype(f32)
    conv = c0[...] + c1[...].astype(f32) + c2[...].astype(f32) + c3[...].astype(f32)
    for to in range(8):
        rows = to // 2 % 2 * 4 + to // 4 * 2 + to % 2
        o[to, 0:10, :] = conv[rows * 10 : rows * 10 + 10, :].astype(bf16)
        o[to, 10:15, :] = mlp[rows * 5 : rows * 5 + 5, :].astype(bf16)
        o[to, 15:20, :] = mlp[40 + rows * 5 : 45 + rows * 5, :].astype(bf16)


def final_kernel(parts, conv, w_in, w_out):
    total = parts[0].astype(f32)
    for i in range(1, 8):
        total = total + parts[i].astype(f32)
    total = total * (1.0 / math.sqrt(MEMBERS * NLAT * NLON))
    conv[...] = total[0:10, :]
    w_in[...] = total[10:15, :]
    w_out[...] = total[15:20, :]


def field_grad_kernel(
    place, tile, left, right, top, bottom, left_side, right_side,
    own_e, left_e, right_e, far_e, conv_hbm, field_grad, win, band, coef, mixed,
    conv_weight, sem
):
    lat = place[0]
    lon = place[1]
    load = pltpu.make_async_copy(conv_hbm, conv_weight, sem)
    load.start()
    fill_window(win, tile, left, right, top, bottom, left_side, right_side, lat)
    rows = jnp.concatenate(
        [
            left_e[2 * RIM :, :], own_e[...], right_e[2 * RIM :, :], far_e[...],
            top[RIM:, :], bottom[RIM:, :],
        ],
        axis=0,
    )
    lane = lax.broadcasted_iota(jnp.int32, (2 * NLON, 2 * NLON), 0)
    to = lax.broadcasted_iota(jnp.int32, (2 * NLON, 2 * NLON), 1)
    flip = (lax.rem(lane + to, 2 * NLON) == 0).astype(f32).astype(bf16)
    for d in range(SPAN):
        coef[d, :, :] = dot(rows[:, d * 128 : (d + 1) * 128], flip, ((1,), (0,)))

    def base(cycle):
        if cycle < 0:
            return 64 + (cycle + HALO) * BASIS
        if cycle >= CYCLES:
            return 72 + (cycle - CYCLES) * BASIS
        return lax.rem(cycle // OWNED - lon + 1 + 4, 4) * 16 + (cycle % OWNED) * BASIS

    for j in range(CYCLES):
        starts = [base(j + e - HALO) for e in range(SPAN)]
        rows = band_rows(
            win, band.at[j % 2], coef, j, lambda e, k: (starts[e] + k, SPAN - 1 - e)
        )
        for k in range(BASIS):
            mixed[j * LON : (j + 1) * LON, k * EMBED : (k + 1) * EMBED] = rows[
                k * LON : (k + 1) * LON, :
            ].astype(bf16)
    total = tile[...].astype(f32)
    load.wait()
    for k in range(BASIS):
        total = total + dot(
            mixed[:, k * EMBED : (k + 1) * EMBED],
            conv_weight[k * EMBED : (k + 1) * EMBED, :],
            ((1,), (1,)),
        )
    field_grad[...] = total.astype(bf16)


def call(kernel, outs, scratch, mib, place, *args, in_hbm=()):
    vmem, hbm = pl.BlockSpec(memory_space=pltpu.VMEM), pl.BlockSpec(memory_space=pltpu.HBM)
    in_specs = [vmem] * len(args) + [hbm] * len(in_hbm)
    args = args + tuple(pltpu.with_memory_space_constraint(a, pltpu.HBM) for a in in_hbm)
    if place is not None:
        in_specs = [pl.BlockSpec(memory_space=pltpu.SMEM)] + in_specs
        args = (place,) + args
    return pl.pallas_call(
        kernel,
        out_shape=outs,
        in_specs=in_specs,
        scratch_shapes=scratch,
        compiler_params=pltpu.CompilerParams(vmem_limit_bytes=mib * 1024 * 1024),
    )(*args)


def neighbours(tile, to_up, to_down):
    forward = [(i, i + 1) for i in range(7)]
    backward = [(i + 1, i) for i in range(7)]
    left = shift(tile, LINE, 4, 1)
    right = shift(tile, LINE, 4, 3)
    top = lax.ppermute(to_up, LAT, forward)
    bottom = lax.ppermute(to_down, LAT, backward)
    return left, right, top, bottom


def relay(place, left, right, top, bottom, *extra):
    rows = 2 * RIM + sum(e.shape[0] for e in extra)
    to_right, to_left = call(
        side_kernel, (struct((rows, EMBED), bf16),) * 2, [], 4, place,
        left, right, top, bottom, *extra,
    )
    left_side = shift(to_right, LINE, 4, 1)
    right_side = shift(to_left, LINE, 4, 3)
    return left_side, right_side


def spread_out(chunks, axis):
    parts = [chunks[0]]
    for s in (1, 2, 3):
        parts.append(shift(chunks[s], axis, 4, s))
    return tuple(parts)


def coefficients(filter_basis, lon_offsets):
    lanes = jnp.arange(2 * NLON, dtype=jnp.int32) % NLON
    values = filter_basis.astype(f32).transpose(0, 2, 1, 3)
    hit = lanes[None, None, None, :] == (lon_offsets % NLON)[:, :, :, None]
    kept = jnp.where(hit[:, None], values[..., None], 0.0)
    rows = kept.sum(axis=3).astype(bf16).reshape(OWNED * BASIS, SPAN * 2 * NLON)
    return jnp.pad(rows, ((0, 16 - OWNED * BASIS), (0, 0)))


def block(fields, filter_basis, lon_offsets, conv_weight, weight_in, weight_out, cotangent):
    y = lax.axis_index("y")
    core = lax.axis_index("core")
    lon = lax.axis_index(LINE)
    x = lax.axis_index("x")
    lat = 2 * y + core
    place = jnp.stack([lat, lon, core, x, y]).astype(jnp.int32)
    tile = fields.reshape(CELLS, EMBED)
    tangent = cotangent.reshape(CELLS, EMBED)

    left, right, top, bottom = neighbours(tile, tile[CELLS - RIM :], tile[:RIM])
    own_e = coefficients(filter_basis, lon_offsets)
    far_e = shift(own_e, LINE, 4, 2)
    left_side, right_side = relay(place, left, right, top, bottom, own_e)
    other_tangent = shift(tangent, "core", 2, 1)

    unit = jnp.arange(EMBED, dtype=jnp.int32)
    ux, uy, ul, ur = unit // 160, unit // 40 % 4, unit // 10 % 4, unit % 10
    source = uy * 160 + ul * 40 + ux * 10 + ur
    order = (source[:, None] == unit[None, :]).astype(bf16)

    hidden_grad = call(
        hidden_grad_kernel, struct((CELLS, HIDDEN), f32), [], 8, None, tangent, weight_out
    )
    far_e, other_tangent, order = lax.optimization_barrier((far_e, other_tangent, order))
    window = pltpu.VMEM(((CYCLES + 2 * HALO) * NLON, EMBED), bf16)
    band = pltpu.VMEM((2, BASIS * LON, 384), bf16)
    edge = struct((RIM + 8, EMBED), bf16)
    parts = (struct((CELLS, CONV_PART), bf16), struct((CELLS, MLP_PART), bf16))
    block_out, blend_grad, mine, mine_mlp, theirs, theirs_mlp, to_up, to_down = call(
        forward_kernel,
        (struct((CELLS, EMBED), bf16), struct((CELLS, EMBED), bf16))
        + parts
        + parts
        + (edge, edge),
        [
            window,
            band,
            pltpu.VMEM((SPAN, 64, 2 * NLON), f32),
            pltpu.VMEM((CELLS, WIDE), bf16),
            pltpu.VMEM((WIDE, EMBED), bf16),
            pltpu.VMEM((EMBED, HIDDEN), bf16),
            pltpu.VMEM((HIDDEN, EMBED), bf16),
            pltpu.SemaphoreType.DMA((3,)),
        ],
        24, place, tile, left, right, top, bottom, left_side, right_side, far_e, own_e,
        tangent, hidden_grad, in_hbm=(conv_weight, weight_in, weight_out),
    )
    other = shift(theirs, "core", 2, 1)
    other_mlp = shift(theirs_mlp, "core", 2, 1)
    g_left, g_right, g_top, g_bottom = neighbours(blend_grad, to_up, to_down)

    chunk = (struct((320, EMBED), f32),) + (struct((320, EMBED), bf16),) * 3
    c = call(conv_grad_kernel, chunk, [], 16, place, mine, other)
    c = spread_out(c, "y")
    m = call(
        mlp_grad_kernel, chunk, [pltpu.VMEM((2 * EMBED, EMBED), f32)],
        16, place, mine_mlp, other_mlp, tangent, other_tangent, order,
    )
    m = spread_out(m, "x")

    g_left_side, g_right_side = relay(place, g_left, g_right, g_top, g_bottom)
    piece = (struct((80, EMBED), f32),) + (struct((80, EMBED), bf16),) * 3
    total = pltpu.VMEM((320, EMBED), f32)
    c = call(conv_sum_kernel, piece, [total], 8, place, *c)
    c = spread_out(c, "x")
    m = call(mlp_sum_kernel, piece, [total], 8, place, *m)
    m = spread_out(m, "y")
    field_grad = call(
        field_grad_kernel,
        struct((CELLS, EMBED), bf16),
        [
            window,
            band,
            pltpu.VMEM((SPAN, 80, 2 * NLON), f32),
            pltpu.VMEM((CELLS, WIDE), bf16),
            pltpu.VMEM((WIDE, EMBED), bf16),
            pltpu.SemaphoreType.DMA,
        ],
        16, place, blend_grad, g_left, g_right, g_top, g_bottom, g_left_side, g_right_side,
        own_e, left_side, right_side, far_e, in_hbm=(conv_weight,),
    )
    packed = call(pack_kernel, struct((8, 20, EMBED), bf16), [], 4, None, *m, *c)
    parts = lax.all_to_all(packed, ("zl0", "zl1", "zhi"), split_axis=0, concat_axis=0, tiled=True)
    conv_grad, in_grad, out_grad = call(
        final_kernel,
        (struct((10, EMBED), f32), struct((5, EMBED), f32), struct((5, EMBED), f32)),
        [], 4, None, parts,
    )
    return (
        block_out.reshape(fields.shape),
        field_grad.reshape(fields.shape),
        conv_grad,
        in_grad.T,
        out_grad,
    )


def solution(mesh):
    everyone = LAT + LINE + ("x", "zhi")
    fine = Mesh(mesh.devices.reshape(4, 2, 2, 2, 4, 2), everyone)
    tile_spec = P(("x", "zhi"), LAT, LINE, None)
    return jax.shard_map(
        block,
        mesh=fine,
        in_specs=(
            tile_spec,
            P(LAT + LINE, None, None, None),
            P(LAT + LINE, None, None),
            P(),
            P(),
            P(),
            tile_spec,
        ),
        out_specs=(
            tile_spec,
            tile_spec,
            P(everyone, None),
            P(None, everyone),
            P(everyone, None),
        ),
        check_vma=False,
    )
```

```python
import math

import jax
import jax.numpy as jnp
from jax import lax
from jax.experimental import pallas as pl
from jax.experimental.pallas import tpu as pltpu
from jax.sharding import Mesh, PartitionSpec as P


EMBED = 640
HIDDEN = 1280
BASIS = 4
SPAN = 5
NLON = 64
NLAT = 96
MEMBERS = 8
WIDE = BASIS * EMBED

CYCLES = 12
LON = 16
CELLS = CYCLES * LON
OWNED = 3
HALO = 2
RIM = HALO * LON
CONV_PART = EMBED + BASIS * 384
MLP_PART = 3 * EMBED

half_root = 0.7071067811865476
gauss_norm = 0.3989422804014327


LAT = ("y", "core")
LINE = ("zl1", "zl0")
bf16 = jnp.bfloat16
f32 = jnp.float32


def dot(a, b, dims):
    return lax.dot_general(a, b, (dims, ((), ())), preferred_element_type=f32)


def shift(block, axis, count, step):
    return lax.ppermute(block, axis, [(i, (i + step) % count) for i in range(count)])


def struct(shape, dtype):
    return jax.ShapeDtypeStruct(shape, dtype)


def fill_window(win, tile, left, right, top, bottom, left_side, right_side, lat):
    zero = jnp.zeros((LON, EMBED), bf16)

    def put(cycle, group, rows):
        at = (cycle + HALO) * NLON + group * LON
        win[at : at + LON, :] = rows

    for group, (inner, side) in enumerate(
        ((left, left_side), (tile, None), (right, right_side))
    ):
        for row in range(CYCLES):
            put(row, group, inner[row * LON : (row + 1) * LON, :])
        for row in range(HALO):
            upper, lower = (top, bottom) if side is None else (side, side)
            skip = 0 if side is None else RIM
            put(row - HALO, group, upper[row * LON : (row + 1) * LON, :])
            put(row + CYCLES, group, lower[skip + row * LON : skip + (row + 1) * LON, :])
    for row in range(-HALO, CYCLES + HALO):
        put(row, 3, zero)

    def polar(first, skip, missing):
        for row in range(HALO):
            rows = slice(skip + row * LON, skip + (row + 1) * LON)
            put(first + row, 3, left_side[rows, :])
            put(first + HALO + row, 3, right_side[rows, :])
            put(missing + row, 0, zero)
            put(missing + row, 2, zero)

    @pl.when(lat == 0)
    def _():
        polar(0, 0, -HALO)

    @pl.when(lat == 7)
    def _():
        polar(CYCLES - 4, RIM, CYCLES)


def side_kernel(place, left, right, top, bottom, *rest):
    *extra, to_right, to_left = rest
    lat = place[0]
    for to in (to_right, to_left):
        to[0:RIM, :] = top[0:RIM, :]
        to[RIM : 2 * RIM, :] = bottom[0:RIM, :]
        if extra:
            to[2 * RIM :, :] = extra[0][...]

    @pl.when(lat == 0)
    def _():
        to_right[0:RIM, :] = left[0:RIM, :]
        to_left[0:RIM, :] = right[RIM : 2 * RIM, :]

    @pl.when(lat == 7)
    def _():
        to_right[RIM : 2 * RIM, :] = left[CELLS - 2 * RIM : CELLS - RIM, :]
        to_left[RIM : 2 * RIM, :] = right[CELLS - RIM :, :]


def set_rows(coef, at, rows):
    for d in range(SPAN):
        coef[d, at : at + rows.shape[0], :] = rows[:, d * 128 : (d + 1) * 128]


def band_rows(win, band, coef, cycle, row_of):
    low_half = lax.broadcasted_iota(jnp.int32, (LON, 2 * NLON), 1) < NLON
    for k in range(BASIS):
        rolled = []
        for d in range(SPAN):
            row, lane = row_of(d, k)
            values = coef[lane, pl.ds(row, 1), :]
            spread_row = jnp.broadcast_to(values, (LON, 2 * NLON))
            rolled.append(pltpu.roll(spread_row, LON, 1, stride=1, stride_axis=0))
        at = k * LON
        band[at : at + LON, 0:128] = jnp.where(low_half, rolled[0], rolled[1]).astype(bf16)
        band[at : at + LON, 128:256] = jnp.where(low_half, rolled[2], rolled[3]).astype(bf16)
        band[at : at + LON, 256:384] = rolled[4].astype(bf16)
    window = win[cycle * NLON : cycle * NLON + SPAN * NLON, :]
    return dot(band[:, 0 : SPAN * NLON], window, ((1,), (0,)))


def hidden_grad_kernel(tangent, weight_out, hidden_grad):
    hidden_grad[...] = dot(tangent[...], weight_out[...], ((1,), (1,)))


def forward_kernel(
    place, tile, left, right, top, bottom, left_side, right_side, far_e, own_e,
    tangent, hidden_grad, conv_hbm, in_hbm,
    hidden_all, blend_grad, mine, mine_mlp, theirs, theirs_mlp, to_up, to_down,
    win, band, coef, spread, conv_weight, weight_in, sems
):
    lat = place[0]
    lon = place[1]
    core = place[2]
    loads = [
        pltpu.make_async_copy(source, target, sems.at[i])
        for i, (source, target) in enumerate(
            ((conv_hbm, conv_weight), (in_hbm, weight_in))
        )
    ]
    for load in loads:
        load.start()
    fill_window(win, tile, left, right, top, bottom, left_side, right_side, lat)
    set_rows(coef, 0, left_side[2 * RIM :, :].astype(f32))
    set_rows(coef, 16, own_e[...].astype(f32))
    set_rows(coef, 32, right_side[2 * RIM :, :].astype(f32))
    set_rows(coef, 48, far_e[...].astype(f32))

    def base(cycle):
        return lax.rem(cycle // OWNED - lon + 1 + 4, 4) * 16 + (cycle % OWNED) * BASIS

    for i in range(CYCLES):
        start = base(i)
        rows = band_rows(win, band.at[i % 2], coef, i, lambda d, k: (start + k, d))
        for k in range(BASIS):
            spread[i * LON : (i + 1) * LON, k * EMBED : (k + 1) * EMBED] = rows[
                k * LON : (k + 1) * LON, :
            ].astype(bf16)

    loads[0].wait()
    blended = (
        tile[...].astype(f32) + dot(spread[...], conv_weight[...], ((1,), (0,)))
    ).astype(bf16)
    loads[1].wait()
    preact = dot(blended, weight_in[...], ((1,), (0,)))
    cdf = 0.5 * (1.0 + lax.erf(preact * half_root))
    hidden = (preact * cdf).astype(bf16)
    hidden_all[...] = hidden
    slope = cdf + preact * jnp.exp(-0.5 * preact * preact) * gauss_norm
    preact_grad = (hidden_grad[...] * slope).astype(bf16)
    grad = (
        tangent[...].astype(f32) + dot(preact_grad, weight_in[...], ((1,), (1,)))
    ).astype(bf16)
    blend_grad[...] = grad
    for side in (theirs, mine):
        side[:, 0:EMBED] = grad
    for side in (theirs_mlp, mine_mlp):
        side[:, 0:EMBED] = blended
    for c in range(2):

        def store(side, side_mlp):
            for k in range(BASIS):
                at = k * EMBED + c * 320
                to = EMBED + k * 384
                side[:, to : to + 320] = spread[:, at : at + 320]
                at = k * 320 + c * 160
                to = EMBED + k * 160
                side_mlp[:, to : to + 160] = hidden[:, at : at + 160]
                side_mlp[:, to + EMBED : to + EMBED + 160] = preact_grad[:, at : at + 160]

        @pl.when(core == c)
        def _():
            store(mine, mine_mlp)

        @pl.when(core != c)
        def _():
            store(theirs, theirs_mlp)

    edges = []
    for cycle in (0, 1, CYCLES - 2, CYCLES - 1):
        start = base(cycle)
        for k in range(BASIS):
            edges.append(
                jnp.concatenate([coef[d, pl.ds(start + k, 1), :] for d in range(SPAN)], axis=1)
            )
    to_up[0:RIM, :] = grad[CELLS - RIM :, :]
    to_up[RIM : RIM + 8, :] = jnp.concatenate(edges[8:], axis=0).astype(bf16)
    to_down[0:RIM, :] = grad[:RIM, :]
    to_down[RIM : RIM + 8, :] = jnp.concatenate(edges[:8], axis=0).astype(bf16)


def block_out_kernel(hidden, mine_mlp, weight_out, out):
    out[...] = (
        mine_mlp[:, 0:EMBED].astype(f32) + dot(hidden[...], weight_out[...], ((1,), (0,)))
    ).astype(bf16)


def mlp_grad_kernel(place, mine, other, tangent, other_tangent, order, o0, o1, o2, o3, acc):
    x = place[3]
    hidden, grad = slice(EMBED, 2 * EMBED), slice(2 * EMBED, 3 * EMBED)
    units = jnp.concatenate([mine[:, grad], other[:, grad], mine[:, hidden], other[:, hidden]])
    units = dot(order[...], units, ((1,), (1,))).astype(bf16)
    blended = jnp.concatenate([mine[:, 0:EMBED], other[:, 0:EMBED]])
    cots = jnp.concatenate([tangent[...], other_tangent[...]])
    acc[0:EMBED, :] = dot(units[:, 0 : 2 * CELLS], blended, ((1,), (0,)))
    acc[EMBED : 2 * EMBED, :] = dot(units[:, 2 * CELLS :], cots, ((1,), (0,)))
    for s, o in enumerate((o0, o1, o2, o3)):
        at = pl.multiple_of(lax.rem(x + s, 4) * 160, 160)
        o[0:160, :] = acc[pl.ds(at, 160), :].astype(o.dtype)
        o[160:320, :] = acc[pl.ds(at + EMBED, 160), :].astype(o.dtype)


def conv_grad_kernel(place, mine, other, o0, o1, o2, o3):
    y = place[4]
    grads = jnp.concatenate([mine[:, 0:EMBED], other[:, 0:EMBED]])
    for s, o in enumerate((o0, o1, o2, o3)):
        lanes = pl.ds(pl.multiple_of(lax.rem(y + s, 4) * 384 + EMBED, 128), 384)
        spread = jnp.concatenate([mine[:, lanes], other[:, lanes]])
        rows = dot(spread, grads, ((0,), (0,)))
        o[...] = rows[0:320, :].astype(o.dtype)


def mlp_sum_kernel(place, r0, r1, r2, r3, o0, o1, o2, o3, acc):
    y = place[4]
    acc[...] = r0[...] + r1[...].astype(f32) + r2[...].astype(f32) + r3[...].astype(f32)
    for s, o in enumerate((o0, o1, o2, o3)):
        at = pl.multiple_of(lax.rem(y + s, 4) * 40, 40)
        o[0:40, :] = acc[pl.ds(at, 40), :].astype(o.dtype)
        o[40:80, :] = acc[pl.ds(at + 160, 40), :].astype(o.dtype)


def conv_sum_kernel(place, r0, r1, r2, r3, o0, o1, o2, o3, acc):
    x = place[3]
    total = r0[...] + r1[...].astype(f32) + r2[...].astype(f32) + r3[...].astype(f32)
    for lon in range(4):
        for to in range(4):
            at = lon * 80 + to * 20
            acc[to * 80 + lon * 20 : to * 80 + lon * 20 + 20, :] = total[at : at + 20, :]
    for s, o in enumerate((o0, o1, o2, o3)):
        at = pl.multiple_of(lax.rem(x + s, 4) * 80, 80)
        o[...] = acc[pl.ds(at, 80), :].astype(o.dtype)


def pack_kernel(m0, m1, m2, m3, c0, c1, c2, c3, o):
    mlp = m0[...] + m1[...].astype(f32) + m2[...].astype(f32) + m3[...].astype(f32)
    conv = c0[...] + c1[...].astype(f32) + c2[...].astype(f32) + c3[...].astype(f32)
    for to in range(8):
        rows = to // 2 % 2 * 4 + to // 4 * 2 + to % 2
        o[to, 0:10, :] = conv[rows * 10 : rows * 10 + 10, :].astype(bf16)
        o[to, 10:15, :] = mlp[rows * 5 : rows * 5 + 5, :].astype(bf16)
        o[to, 15:20, :] = mlp[40 + rows * 5 : 45 + rows * 5, :].astype(bf16)


def final_kernel(parts, conv, w_in, w_out):
    total = parts[0].astype(f32)
    for i in range(1, 8):
        total = total + parts[i].astype(f32)
    total = total * (1.0 / math.sqrt(MEMBERS * NLAT * NLON))
    conv[...] = total[0:10, :]
    w_in[...] = total[10:15, :]
    w_out[...] = total[15:20, :]


def field_grad_kernel(
    place, tile, left, right, top, bottom, left_side, right_side,
    own_e, left_e, right_e, far_e, conv_hbm, field_grad, win, band, coef, mixed,
    conv_weight, sem
):
    lat = place[0]
    lon = place[1]
    load = pltpu.make_async_copy(conv_hbm, conv_weight, sem)
    load.start()
    fill_window(win, tile, left, right, top, bottom, left_side, right_side, lat)
    rows = jnp.concatenate(
        [
            left_e[2 * RIM :, :], own_e[...], right_e[2 * RIM :, :], far_e[...],
            top[RIM:, :], bottom[RIM:, :],
        ],
        axis=0,
    )
    lane = lax.broadcasted_iota(jnp.int32, (2 * NLON, 2 * NLON), 0)
    to = lax.broadcasted_iota(jnp.int32, (2 * NLON, 2 * NLON), 1)
    flip = (lax.rem(lane + to, 2 * NLON) == 0).astype(f32).astype(bf16)
    for d in range(SPAN):
        coef[d, :, :] = dot(rows[:, d * 128 : (d + 1) * 128], flip, ((1,), (0,)))

    def base(cycle):
        if cycle < 0:
            return 64 + (cycle + HALO) * BASIS
        if cycle >= CYCLES:
            return 72 + (cycle - CYCLES) * BASIS
        return lax.rem(cycle // OWNED - lon + 1 + 4, 4) * 16 + (cycle % OWNED) * BASIS

    for j in range(CYCLES):
        starts = [base(j + e - HALO) for e in range(SPAN)]
        rows = band_rows(
            win, band.at[j % 2], coef, j, lambda e, k: (starts[e] + k, SPAN - 1 - e)
        )
        for k in range(BASIS):
            mixed[j * LON : (j + 1) * LON, k * EMBED : (k + 1) * EMBED] = rows[
                k * LON : (k + 1) * LON, :
            ].astype(bf16)
    total = tile[...].astype(f32)
    load.wait()
    for k in range(BASIS):
        total = total + dot(
            mixed[:, k * EMBED : (k + 1) * EMBED],
            conv_weight[k * EMBED : (k + 1) * EMBED, :],
            ((1,), (1,)),
        )
    field_grad[...] = total.astype(bf16)


def call(kernel, outs, scratch, mib, place, *args, in_hbm=()):
    vmem, hbm = pl.BlockSpec(memory_space=pltpu.VMEM), pl.BlockSpec(memory_space=pltpu.HBM)
    in_specs = [vmem] * len(args) + [hbm] * len(in_hbm)
    args = args + tuple(pltpu.with_memory_space_constraint(a, pltpu.HBM) for a in in_hbm)
    if place is not None:
        in_specs = [pl.BlockSpec(memory_space=pltpu.SMEM)] + in_specs
        args = (place,) + args
    return pl.pallas_call(
        kernel,
        out_shape=outs,
        in_specs=in_specs,
        scratch_shapes=scratch,
        compiler_params=pltpu.CompilerParams(vmem_limit_bytes=mib * 1024 * 1024),
    )(*args)


def neighbours(tile, to_up, to_down):
    forward = [(i, i + 1) for i in range(7)]
    backward = [(i + 1, i) for i in range(7)]
    left = shift(tile, LINE, 4, 1)
    right = shift(tile, LINE, 4, 3)
    top = lax.ppermute(to_up, LAT, forward)
    bottom = lax.ppermute(to_down, LAT, backward)
    return left, right, top, bottom


def relay(place, left, right, top, bottom, *extra):
    rows = 2 * RIM + sum(e.shape[0] for e in extra)
    to_right, to_left = call(
        side_kernel, (struct((rows, EMBED), bf16),) * 2, [], 4, place,
        left, right, top, bottom, *extra,
    )
    left_side = shift(to_right, LINE, 4, 1)
    right_side = shift(to_left, LINE, 4, 3)
    return left_side, right_side


def spread_out(chunks, axis):
    parts = [chunks[0]]
    for s in (1, 2, 3):
        parts.append(shift(chunks[s], axis, 4, s))
    return tuple(parts)


def coefficients(filter_basis, lon_offsets):
    lanes = jnp.arange(2 * NLON, dtype=jnp.int32) % NLON
    values = filter_basis.astype(f32).transpose(0, 2, 1, 3)
    hit = lanes[None, None, None, :] == (lon_offsets % NLON)[:, :, :, None]
    kept = jnp.where(hit[:, None], values[..., None], 0.0)
    rows = kept.sum(axis=3).astype(bf16).reshape(OWNED * BASIS, SPAN * 2 * NLON)
    return jnp.pad(rows, ((0, 16 - OWNED * BASIS), (0, 0)))


def block(fields, filter_basis, lon_offsets, conv_weight, weight_in, weight_out, cotangent):
    y = lax.axis_index("y")
    core = lax.axis_index("core")
    lon = lax.axis_index(LINE)
    x = lax.axis_index("x")
    lat = 2 * y + core
    place = jnp.stack([lat, lon, core, x, y]).astype(jnp.int32)
    tile = fields.reshape(CELLS, EMBED)
    tangent = cotangent.reshape(CELLS, EMBED)

    left, right, top, bottom = neighbours(tile, tile[CELLS - RIM :], tile[:RIM])
    own_e = coefficients(filter_basis, lon_offsets)
    far_e = shift(own_e, LINE, 4, 2)
    left_side, right_side = relay(place, left, right, top, bottom, own_e)
    other_tangent = shift(tangent, "core", 2, 1)

    unit = jnp.arange(EMBED, dtype=jnp.int32)
    ux, uy, ul, ur = unit // 160, unit // 40 % 4, unit // 10 % 4, unit % 10
    source = uy * 160 + ul * 40 + ux * 10 + ur
    order = (source[:, None] == unit[None, :]).astype(bf16)

    hidden_grad = call(
        hidden_grad_kernel, struct((CELLS, HIDDEN), f32), [], 8, None, tangent, weight_out
    )
    far_e, other_tangent, order = lax.optimization_barrier((far_e, other_tangent, order))
    window = pltpu.VMEM(((CYCLES + 2 * HALO) * NLON, EMBED), bf16)
    band = pltpu.VMEM((2, BASIS * LON, 384), bf16)
    edge = struct((RIM + 8, EMBED), bf16)
    parts = (struct((CELLS, CONV_PART), bf16), struct((CELLS, MLP_PART), bf16))
    hidden, blend_grad, mine, mine_mlp, theirs, theirs_mlp, to_up, to_down = call(
        forward_kernel,
        (struct((CELLS, HIDDEN), bf16), struct((CELLS, EMBED), bf16))
        + parts
        + parts
        + (edge, edge),
        [
            window,
            band,
            pltpu.VMEM((SPAN, 64, 2 * NLON), f32),
            pltpu.VMEM((CELLS, WIDE), bf16),
            pltpu.VMEM((WIDE, EMBED), bf16),
            pltpu.VMEM((EMBED, HIDDEN), bf16),
            pltpu.SemaphoreType.DMA((2,)),
        ],
        24, place, tile, left, right, top, bottom, left_side, right_side, far_e, own_e,
        tangent, hidden_grad, in_hbm=(conv_weight, weight_in),
    )
    block_out = call(
        block_out_kernel, struct((CELLS, EMBED), bf16), [], 8, None,
        hidden, mine_mlp, weight_out,
    )
    other = shift(theirs, "core", 2, 1)
    other_mlp = shift(theirs_mlp, "core", 2, 1)
    g_left, g_right, g_top, g_bottom = neighbours(blend_grad, to_up, to_down)

    chunk = (struct((320, EMBED), f32),) + (struct((320, EMBED), bf16),) * 3
    c = call(conv_grad_kernel, chunk, [], 16, place, mine, other)
    c = spread_out(c, "y")
    m = call(
        mlp_grad_kernel, chunk, [pltpu.VMEM((2 * EMBED, EMBED), f32)],
        16, place, mine_mlp, other_mlp, tangent, other_tangent, order,
    )
    m = spread_out(m, "x")

    g_left_side, g_right_side = relay(place, g_left, g_right, g_top, g_bottom)
    piece = (struct((80, EMBED), f32),) + (struct((80, EMBED), bf16),) * 3
    total = pltpu.VMEM((320, EMBED), f32)
    c = call(conv_sum_kernel, piece, [total], 8, place, *c)
    c = spread_out(c, "x")
    m = call(mlp_sum_kernel, piece, [total], 8, place, *m)
    m = spread_out(m, "y")
    field_grad = call(
        field_grad_kernel,
        struct((CELLS, EMBED), bf16),
        [
            window,
            band,
            pltpu.VMEM((SPAN, 80, 2 * NLON), f32),
            pltpu.VMEM((CELLS, WIDE), bf16),
            pltpu.VMEM((WIDE, EMBED), bf16),
            pltpu.SemaphoreType.DMA,
        ],
        16, place, blend_grad, g_left, g_right, g_top, g_bottom, g_left_side, g_right_side,
        own_e, left_side, right_side, far_e, in_hbm=(conv_weight,),
    )
    packed = call(pack_kernel, struct((8, 20, EMBED), bf16), [], 4, None, *m, *c)
    parts = lax.all_to_all(packed, ("zl0", "zl1", "zhi"), split_axis=0, concat_axis=0, tiled=True)
    conv_grad, in_grad, out_grad = call(
        final_kernel,
        (struct((10, EMBED), f32), struct((5, EMBED), f32), struct((5, EMBED), f32)),
        [], 4, None, parts,
    )
    return (
        block_out.reshape(fields.shape),
        field_grad.reshape(fields.shape),
        conv_grad,
        in_grad.T,
        out_grad,
    )


def solution(mesh):
    everyone = LAT + LINE + ("x", "zhi")
    fine = Mesh(mesh.devices.reshape(4, 2, 2, 2, 4, 2), everyone)
    tile_spec = P(("x", "zhi"), LAT, LINE, None)
    return jax.shard_map(
        block,
        mesh=fine,
        in_specs=(
            tile_spec,
            P(LAT + LINE, None, None, None),
            P(LAT + LINE, None, None),
            P(),
            P(),
            P(),
            tile_spec,
        ),
        out_specs=(
            tile_spec,
            tile_spec,
            P(everyone, None),
            P(None, everyone),
            P(everyone, None),
        ),
        check_vma=False,
    )
```
